768 devices in a mesh: gx: 4 (over x), gy: 16 (over y, core), gz: 12 (over z).
Axes of the slice: x: 4, y: 8, z: 12, core: 2. Of those that a mesh axis runs over, the one named last changes fastest.
Arguments:
- drops: float32 [96, 256, 128, 128], P('gz', 'gx', 'gy'), may hold values from 0 to 1
- capture_efficiency_matrix: float32 [128, 128], replicated, may hold values from 0 to 0.015625
- transfer: float32 [128, 128], replicated, may hold values from 0 to 0.015625
- courant_u: float32 [96], P('gz'), may hold values from -0.45 to 0.45
- courant_v: float32 [96], P('gz'), may hold values from -0.45 to 0.45
- fall_class: int32 [128], replicated, may hold values from 0 to 2, as said below
- cloud_mask: int32 [256, 128], P('gx', 'gy'), may hold values from 0 to 1, as said below
Outputs:
- drops_out: float32 [96, 256, 128, 128], P('gz', 'gx', 'gy')
The draws below stay inside these ranges and needn't reach their ends.
Inputs may be any that keep to these rules, and one draw needn't show every extreme that they name: `fall_class`: nondecreasing in the bin index; the first bin has 0 and the last 2. `cloud_mask`: each aligned tile of 64 x 8 columns (one device's) holds at most 256 cloudy columns, and some tile holds exactly 256.
All inputs are finite; a program needn't handle non-finite values.
Results may differ from the reference program's by a relative error of at most 0.0001.
Values sent between devices are 32-bit elements; how exact they have to be, the bound alone decides.
No kernel may reach another device: no remote copies, remote signals or barrier semaphores. Data moves between devices by JAX's collectives and lax.ppermute only.
A program may use at most 32 MiB of HBM per device.

```python
import jax
import jax.numpy as jnp
from jax import lax

NB = 128
CX = 64
CY = 8
H_MAX = 2
STEPS = 2
CLOUD_MAX = 256
NX = 256
NY = 128
NZ = 96


def draw_fall_class(key, part):
    raw_class = jax.random.randint(jax.random.fold_in(key, 3), (NB,), 0, H_MAX + 1)
    sorted_columns = jnp.sort(raw_class)
    sorted_columns = sorted_columns.at[0].set(0).at[NB - 1].set(H_MAX)
    return sorted_columns.astype(jnp.int32)


def draw_cloud_mask(key, part):
    tiles_x = NX // CX
    tiles_y = NY // CY
    tile_count = jax.random.randint(jax.random.fold_in(key, 11), (tiles_x, tiles_y), 0, CLOUD_MAX + 1)
    full_x = jax.random.randint(jax.random.fold_in(key, 13), (), 0, tiles_x)
    full_y = jax.random.randint(jax.random.fold_in(key, 14), (), 0, tiles_y)
    filled_positions = (jnp.arange(tiles_x)[:, None] == full_x) & (jnp.arange(tiles_y)[None, :] == full_y)
    tile_count = jnp.where(filled_positions, CLOUD_MAX, tile_count)
    random_bits = jax.random.randint(jax.random.fold_in(key, 12), (tiles_x, tiles_y, CX * CY), 0, 2 ** 30)
    ordering = jnp.argsort(random_bits, axis=-1, stable=True)
    column_position = jnp.argsort(ordering, axis=-1, stable=True)
    cloudy = (column_position < tile_count[:, :, None]).astype(jnp.int32)
    cloudy = cloudy.reshape(tiles_x, tiles_y, CX, CY).transpose(0, 2, 1, 3).reshape(NX, NY)
    return cloudy.astype(jnp.int32)


def block_levels(rng, extent, cuts, least, top_value):
    factor_of, own = 1.0, jax.random.fold_in(rng, 6)
    for axis_at, blocks in cuts:
        steps = jnp.exp(jax.random.uniform(jax.random.fold_in(own, axis_at), (blocks,), jnp.float32, least / len(cuts), top_value / len(cuts)))
        factor_of = factor_of * jnp.repeat(steps, extent[axis_at] // blocks).reshape([-1 if axis == axis_at else 1 for axis in range(len(extent))])
    return factor_of


def setup_inputs(seed: int = 0) -> dict:
    key_of = jax.random.split(jax.random.key(seed), 8)
    drops = jnp.clip(1.0 * jax.random.uniform(key_of[0], (NZ, NX, NY, NB), jnp.float32) ** block_levels(key_of[0], (NZ, NX, NY, NB), ((0, 12), (1, 4), (2, 16)), -0.2, 0.2), 0.0, 1.0)
    capture_efficiency_matrix = jnp.clip(jax.random.uniform(key_of[1], (NB, NB), jnp.float32, 0.0, 0.015625), 0.0, 0.015625)
    transfer = jnp.clip(jax.random.uniform(key_of[2], (NB, NB), jnp.float32, 0.0, 0.015625), 0.0, 0.015625)
    courant_u = jnp.clip(jax.random.uniform(key_of[3], (NZ,), jnp.float32, -0.45, 0.45) * block_levels(key_of[3], (NZ,), ((0, 12),), -0.4, 0.0), -0.45, 0.45)
    courant_v = jnp.clip(jax.random.uniform(key_of[4], (NZ,), jnp.float32, -0.45, 0.45) * block_levels(key_of[4], (NZ,), ((0, 12),), -0.4, 0.0), -0.45, 0.45)
    fall_class = draw_fall_class(jax.random.fold_in(key_of[7], 71), 0)
    cloud_mask = draw_cloud_mask(jax.random.fold_in(key_of[7], 71), 0)
    return dict(drops=drops, capture_efficiency_matrix=capture_efficiency_matrix, transfer=transfer, courant_u=courant_u, courant_v=courant_v, fall_class=fall_class, cloud_mask=cloud_mask)


def collide(particle_distribution, capture_efficiency_matrix, transfer, cloudy):
    def one_level(altitude_layer):
        merger_speed = jnp.einsum("zcl,vl->zcv", altitude_layer, capture_efficiency_matrix, precision=lax.Precision.HIGHEST)
        water_removed = altitude_layer * merger_speed
        mass_gain = jnp.einsum("xyi,ik->xyk", water_removed, transfer, precision=lax.Precision.HIGHEST)
        return altitude_layer + cloudy[:, :, None] * (mass_gain - water_removed)
    return lax.map(one_level, particle_distribution)


def advect(coalesced_drops, courant_u, courant_v):
    x_plus = jnp.maximum(courant_u, 0.0)[:, None, None, None]
    x_minus = jnp.minimum(courant_u, 0.0)[:, None, None, None]
    northward_neighbor = jnp.maximum(courant_v, 0.0)[:, None, None, None]
    y_minus = jnp.minimum(courant_v, 0.0)[:, None, None, None]
    west_side = jnp.roll(coalesced_drops, 1, axis=1)
    east_side = jnp.roll(coalesced_drops, -1, axis=1)
    south_side = jnp.roll(coalesced_drops, 1, axis=2)
    north_side = jnp.roll(coalesced_drops, -1, axis=2)
    result = coalesced_drops - x_plus * (coalesced_drops - west_side) - x_minus * (east_side - coalesced_drops)
    return result - northward_neighbor * (coalesced_drops - south_side) - y_minus * (north_side - coalesced_drops)


def sediment(padded, fall_class, levels):
    result = padded[:levels]
    for fall_depth in range(1, H_MAX + 1):
        result = jnp.where((fall_class == fall_depth)[None, None, None, :], padded[fall_depth:fall_depth + levels], result)
    return result


def reference(drops, capture_efficiency_matrix, transfer, courant_u, courant_v, fall_class, cloud_mask):
    cloudy = cloud_mask.astype(jnp.float32)
    particle_distribution = drops
    for repeat in range(STEPS):
        coalesced_drops = collide(particle_distribution, capture_efficiency_matrix, transfer, cloudy)
        advected = advect(coalesced_drops, courant_u, courant_v)
        empty_upper_boundary = jnp.zeros((H_MAX,) + advected.shape[1:], jnp.float32)
        particle_distribution = sediment(jnp.concatenate([advected, empty_upper_boundary], axis=0), fall_class, NZ)
    return particle_distribution
```

```python
import functools

import jax
import jax.numpy as jnp
from jax import lax
from jax.experimental import pallas as pl
from jax.experimental.pallas import tpu as pltpu
from jax.sharding import PartitionSpec as P

H_MAX = 2
Z, X, Y, B = 8, 64, 8, 128
T = 8
XW = X + 4
XA = X + 2
HALO = 2 * X * Z
XROWS = 2 * Z * Y
F32, BF16 = jnp.float32, jnp.bfloat16

VMEM = pl.BlockSpec(memory_space=pltpu.VMEM)
SMEM = pl.BlockSpec(memory_space=pltpu.SMEM)
ANY = pl.BlockSpec(memory_space=pl.ANY)


def rows(start, n=T):
    return pl.ds(start if isinstance(start, int) else pl.multiple_of(start, T), n)


def call(body, outs, args, specs, scratch=(), cost=(0, 0), out_specs=None, aliases=None):
    shapes = [pltpu.VMEM(s, d) if m else jax.ShapeDtypeStruct(s, d) for s, d, m in outs]
    args = [
        pltpu.with_memory_space_constraint(a, pltpu.VMEM) if s is VMEM else a
        for a, s in zip(args, specs)
    ]
    return pl.pallas_call(
        body,
        out_shape=shapes,
        in_specs=list(specs),
        out_specs=out_specs or [VMEM] * len(outs),
        scratch_shapes=list(scratch),
        input_output_aliases=aliases or {},
        cost_estimate=pl.CostEstimate(flops=cost[0], bytes_accessed=cost[1], transcendentals=0),
        compiler_params=pltpu.CompilerParams(vmem_limit_bytes=40 << 20),
    )(*args)


def split(x):
    high = x.astype(BF16)
    return high, (x - high.astype(F32)).astype(BF16)


def product(x, weights):
    out = jnp.dot(jnp.concatenate(split(x), axis=1), weights, preferred_element_type=F32)
    return out[:, :B] + out[:, B:]


def collide(s, cloudy, capture, transfer):
    loss = s * product(s, capture)
    return s + cloudy * (product(loss, transfer) - loss)


def eightfold(ref, row):
    return ref[pl.ds(row, T, stride=0), :]


def repeated(ref, start, n):
    return jnp.concatenate([eightfold(ref, start + i) for i in range(n)], axis=0)


def classes(sc_ref):
    lane = lax.broadcasted_iota(jnp.int32, (T, B), 1)
    return lane < sc_ref[0], lane >= sc_ref[1]


def fall(c0, c2, a, b, c):
    return jnp.where(c0, a, jnp.where(c2, c, b))


def edges_body(drops, cloudy, k_ref, t_ref, own, xm, xp, ym, yp, kk, tt, sem):
    copy = pltpu.make_async_copy(drops, own, sem)
    copy.start()
    for ref, out, turned in ((k_ref, kk, True), (t_ref, tt, False)):
        w = ref[...].T if turned else ref[...]
        high, low = split(w)
        half = jnp.concatenate([high, low], axis=1)
        out[...] = jnp.concatenate([half, half], axis=0)
    for out, cols in ((xm, (0, 1)), (xp, (X - 1, X - 2))):
        for d, x in enumerate(cols):
            out[XROWS + d * Y : XROWS + d * Y + Y] = cloudy[x * Y : x * Y + Y]
    for out, ys in ((ym, (0, 1)), (yp, (Y - 1, Y - 2))):
        for d, y in enumerate(ys):
            out[HALO + d * X : HALO + d * X + X] = cloudy[pl.ds(y, X, stride=Y), :]
    copy.wait()
    for out, cols in ((xm, (0, 1)), (xp, (X - 1, X - 2))):
        for d, x in enumerate(cols):
            for z in range(Z):
                at = (z * X + x) * Y
                out[(d * Z + z) * Y : (d * Z + z + 1) * Y] = own[at : at + Y]
    for out, ys in ((ym, (0, 1)), (yp, (Y - 1, Y - 2))):
        for d, y in enumerate(ys):
            for x in range(X):
                at = (d * X + x) * Z
                out[at : at + Z] = own[pl.ds(x * Y + y, Z, stride=X * Y), :]


def corners_body(left, right, up, down):
    for out, y in ((up, Y - 1), (down, 0)):
        out[...] = jnp.zeros_like(out)
        for i, ref in enumerate((left, right)):
            out[i * Z : (i + 1) * Z] = ref[pl.ds(y, Z, stride=Y), :]
            out[2 * Z + i : 2 * Z + i + 1] = ref[XROWS + y : XROWS + y + 1]


def cy_at(side, d, x):
    return ((side * 2 + d) * XA + x + 1) * Z


def first_body(own, cloudy, left, right, south, north, kk, tt, c1, cy, m1, my):
    k, t = kk[...], tt[...]

    def level(z, _):
        c1[rows((z * XW + 2) * Y, X * Y)] = collide(own[rows(z * X * Y, X * Y)], cloudy[...], k, t)
        return 0

    lax.fori_loop(0, Z, level, 0)
    m1[0:Y] = left[XROWS : XROWS + Y]
    m1[Y : Y + X * Y] = cloudy[...]
    m1[Y + X * Y :] = right[XROWS : XROWS + Y]
    for ref, at in ((left, (1, 0)), (right, (XW - 2, XW - 1))):
        mask = jnp.concatenate(
            [ref[XROWS + d * Y : XROWS + d * Y + Y] for d in range(2) for _ in range(Z)], axis=0
        )
        c = collide(ref[0:XROWS], mask, k, t)
        for d in range(2):
            for z in range(Z):
                to = (z * XW + at[d]) * Y
                c1[to : to + Y] = c[(d * Z + z) * Y : (d * Z + z + 1) * Y]
    for side, ref in enumerate((south, north)):
        for d in range(2):
            mask = repeated(ref, HALO + d * X, X)
            if d == 0:
                my[side * X * Z : (side + 1) * X * Z] = mask
            at = cy_at(side, d, 0)
            cy[at : at + X * Z] = collide(ref[d * X * Z : (d + 1) * X * Z], mask, k, t)


def advect_level(z, c_ref, width, first, count, out_ref, out_width, edge, u_ref, v_ref):
    u, v = u_ref[z], v_ref[z]
    au, av = jnp.abs(u), jnp.abs(v)
    shift = jnp.where(v > 0, 1, T - 1)
    side = jnp.where(v > 0, 0, 1)
    at_edge = lax.broadcasted_iota(jnp.int32, (T, B), 0) == jnp.where(v > 0, 0, T - 1)
    base = (z * width + first) * Y
    base_x = base + jnp.where(u > 0, -Y, Y)
    base_out = z * out_width * Y
    edge_ref, edge_at, edge_stride = edge(side)
    for i in range(count):
        c = c_ref[rows(base + i * Y)]
        x = c_ref[rows(base_x + i * Y)]
        e = eightfold(edge_ref, edge_at + i * edge_stride)
        y = jnp.where(at_edge, e, pltpu.roll(c, shift, 0))
        out_ref[rows(base_out + i * Y)] = c - au * (c - x) - av * (c - y)


def second_body(
    sc, u_ref, v_ref, ub, vb, c1_in, cy_in, cs, cn, kk, tt, m1, my, a1, a1y, c2, c2y, a2, pay, cy
):
    k, t = kk[...], tt[...]
    c0, cc2 = classes(sc)
    cy[...] = cy_in[...]
    for side, ref in enumerate((cs, cn)):
        mask = repeated(ref, 2 * Z, 2)
        c = collide(ref[0 : 2 * Z], mask, k, t)
        for i, x in enumerate((-1, X)):
            at = cy_at(side, 0, x)
            cy[at : at + Z] = c[i * Z : (i + 1) * Z]

    def edge1(z):
        return lambda side: (cy, side * (2 * XA * Z) + z, Z)

    def adv1(z, _):
        advect_level(z, c1_in, XW, 1, XA, a1, XA, edge1(z), u_ref, v_ref)
        return 0

    lax.fori_loop(0, 4, adv1, 0)
    au, av = jnp.abs(ub[...]), jnp.abs(vb[...])
    upos, vpos = ub[...] > 0, vb[...] > 0
    for side in range(2):
        for x in range(X):
            at = cy_at(side, 0, x)
            far = cy_at(side, 1, x)
            c = cy[at : at + Z]
            xx = jnp.where(upos, cy[at - Z : at], cy[at + Z : at + 2 * Z])
            outer = cy[far : far + Z]
            inner = c1_in[pl.ds((x + 2) * Y + (Y - 1) * side, Z, stride=XW * Y), :]
            yy = jnp.where(vpos, *((outer, inner) if side == 0 else (inner, outer)))
            a = c - au * (c - xx) - av * (c - yy)
            to = (side * X + x) * Z
            a1y[to : to + Z] = a
            c2y[to : to + Z] = fall(c0, cc2, a, pltpu.roll(a, Z - 1, 0), pltpu.roll(a, Z - 2, 0))
    for i in range(2):
        at = rows(i * X * Z, X * Z)
        c2y[at] = collide(c2y[at], my[at], k, t)
    settle_collide(0, 2, c0, cc2, a1, m1, c2, k, t)

    def adv2(z, _):
        advect_level(z, c2, XA, 1, X, a2, X, lambda side: (c2y, side * (X * Z) + z, Z), u_ref, v_ref)
        return 0

    lax.fori_loop(0, 2, adv2, 0)
    for i in range(XA):
        l0, l1 = a1[i * T : (i + 1) * T], a1[(XA + i) * T : (XA + i + 1) * T]
        pay[i * T : (i + 1) * T] = fall(c0, cc2, l0, l0, l1)
        pay[(NT + i) * T : (NT + i + 1) * T] = l0
    for i in range(2 * X // T):
        at = i * T * Z
        l0, l1 = a1y[pl.ds(at, T, stride=Z), :], a1y[pl.ds(at + 1, T, stride=Z), :]
        j = XA + i
        pay[j * T : (j + 1) * T] = fall(c0, cc2, l0, l0, l1)
        pay[(NT + j) * T : (NT + j + 1) * T] = l0
    for i in range(X):
        l0, l1 = a2[i * T : (i + 1) * T], a2[(X + i) * T : (X + i + 1) * T]
        j = XA + 2 * X // T + i
        pay[j * T : (j + 1) * T] = fall(c0, cc2, l0, l0, l1)
        pay[(NT + j) * T : (NT + j + 1) * T] = l0


NT = XA + 2 * X // T + X


def settle_collide(lo, hi, c0, cc2, a1, m1, c2, k, t):
    def level(z, _):
        for i in range(XA):
            at = (z * XA + i) * T
            c2[rows(at)] = fall(
                c0, cc2, a1[rows(at)], a1[rows(at + XA * T)], a1[rows(at + 2 * XA * T)]
            )
        at = rows(z * XA * T, XA * T)
        c2[at] = collide(c2[at], m1[...], k, t)
        return 0

    lax.fori_loop(lo, hi, level, 0)


def third_body(sc, u_ref, v_ref, c1, cy, a1_in, c2_in, c2y, a2_in, kk, tt, m1, a1_hi, a2_hi, out, a1, c2, a2, c2b, sem):
    k, t = kk[...], tt[...]
    c0, cc2 = classes(sc)
    a1[0 : 4 * XA * T] = a1_in[...]
    c2[0 : 2 * XA * T] = c2_in[...]
    a2[0 : 2 * X * T] = a2_in[...]

    def adv1(z, _):
        advect_level(
            z, c1, XW, 1, XA, a1, XA, lambda side: (cy, side * (2 * XA * Z) + z, Z), u_ref, v_ref
        )
        return 0

    lax.fori_loop(4, 8, adv1, 0)
    settle_collide(2, 6, c0, cc2, a1, m1, c2, k, t)

    def adv2(z, _):
        advect_level(z, c2, XA, 1, X, a2, X, lambda side: (c2y, side * (X * Z) + z, Z), u_ref, v_ref)
        return 0

    lax.fori_loop(2, 6, adv2, 0)

    def done(z, _):
        for i in range(X):
            at = (z * X + i) * T
            c2b[rows(at)] = fall(
                c0, cc2, a2[rows(at)], a2[rows(at + X * T)], a2[rows(at + 2 * X * T)]
            )
        return 0

    lax.fori_loop(0, 4, done, 0)
    copy = pltpu.make_async_copy(c2b, out.at[pl.ds(0, 4 * X * T)], sem)
    copy.start()
    a1_hi[...] = a1[6 * XA * T : 8 * XA * T]
    a2_hi[...] = a2[4 * X * T : 6 * X * T]
    copy.wait()


def last_body(sc, u_ref, v_ref, a1_hi, a1y, a2_hi, south, north, kk, tt, m1, pay, out_in, out, c2, c2y, a2, res, sem):
    k, t = kk[...], tt[...]
    c0, cc2 = classes(sc)
    c0w = lax.broadcasted_iota(jnp.int32, (T, B), 1) < sc[0]
    for i in range(XA):
        p7 = pay[i * T : (i + 1) * T]
        p6 = pay[(NT + i) * T : (NT + i + 1) * T]
        x6, x7 = a1_hi[i * T : (i + 1) * T], a1_hi[(XA + i) * T : (XA + i + 1) * T]
        c2[i * T : (i + 1) * T] = fall(c0, cc2, x6, x7, p6)
        c2[(XA + i) * T : (XA + i + 1) * T] = jnp.where(c0w, x7, p7)
    for i in range(2 * X // T):
        j = XA + i
        p7 = pay[j * T : (j + 1) * T]
        p6 = pay[(NT + j) * T : (NT + j + 1) * T]
        at = i * T * Z
        x6, x7 = a1y[pl.ds(at + 6, T, stride=Z), :], a1y[pl.ds(at + 7, T, stride=Z), :]
        c2y[i * T : (i + 1) * T] = fall(c0, cc2, x6, x7, p6)
        c2y[2 * X + i * T : 2 * X + (i + 1) * T] = jnp.where(c0w, x7, p7)
    mask = jnp.concatenate([south[HALO : HALO + X], north[HALO : HALO + X]] * 2, axis=0)
    c2y[...] = collide(c2y[...], mask, k, t)
    for z in range(2):
        at = slice(z * XA * T, (z + 1) * XA * T)
        c2[at] = collide(c2[at], m1[...], k, t)
    a2[0 : 2 * X * T] = a2_hi[...]
    for z in (6, 7):
        advect_one(z, c2, a2, c2y, u_ref, v_ref)
    for i in range(X):
        j = XA + 2 * X // T + i
        p7 = pay[j * T : (j + 1) * T]
        p6 = pay[(NT + j) * T : (NT + j + 1) * T]
        x = [a2[(z * X + i) * T : (z * X + i + 1) * T] for z in range(4)]
        for z, v in enumerate(
            (
                fall(c0, cc2, x[0], x[1], x[2]),
                fall(c0, cc2, x[1], x[2], x[3]),
                fall(c0, cc2, x[2], x[3], p6),
                jnp.where(c0w, x[3], p7),
            )
        ):
            res[(z * X + i) * T : (z * X + i + 1) * T] = v
    copy = pltpu.make_async_copy(res, out.at[pl.ds(4 * X * T, 4 * X * T)], sem)
    copy.start()
    copy.wait()


def advect_one(z, c2, a2, c2y, u_ref, v_ref):
    u, v = u_ref[z], v_ref[z]
    au, av = jnp.abs(u), jnp.abs(v)
    shift = jnp.where(v > 0, 1, T - 1)
    at_edge = lax.broadcasted_iota(jnp.int32, (T, B), 0) == jnp.where(v > 0, 0, T - 1)
    base = ((z - 6) * XA + 1) * Y
    base_x = base + jnp.where(u > 0, -Y, Y)
    base_e = (z - 6) * 2 * X + jnp.where(v > 0, 0, X)
    for i in range(X):
        c = c2[rows(base + i * Y)]
        x = c2[rows(base_x + i * Y)]
        e = eightfold(c2y, base_e + i)
        y = jnp.where(at_edge, e, pltpu.roll(c, shift, 0))
        a2[((z - 4) * X + i) * T : ((z - 4) * X + i + 1) * T] = c - au * (c - x) - av * (c - y)


def ring(axis, step):
    n = lax.axis_size(axis)
    return [(i, (i + step) % n) for i in range(n)]


def on_device(drops, capture, transfer, courant_u, courant_v, fall_class, cloud_mask):
    drops = drops.reshape(Z * X * Y, B)
    cloudy = jnp.broadcast_to(cloud_mask.astype(F32)[:, :, None], (X, Y, B)).reshape(X * Y, B)
    n0 = jnp.sum((fall_class == 0).astype(jnp.int32))
    n2 = jnp.sum((fall_class == H_MAX).astype(jnp.int32))
    sc = jnp.stack([n0, B - n2])
    ub = jnp.broadcast_to(courant_u[:, None], (Z, B))
    vb = jnp.broadcast_to(courant_v[:, None], (Z, B))
    v = lambda n, d=F32: ((n, B), d, True)
    own, xm, xp, ym, yp, kk, tt = call(
        edges_body,
        [v(Z * X * Y), v(XROWS + 16), v(XROWS + 16), v(HALO + 128), v(HALO + 128)]
        + [((2 * B, 2 * B), BF16, True)] * 2,
        [drops, cloudy, capture, transfer],
        [ANY, VMEM, VMEM, VMEM],
        [pltpu.SemaphoreType.DMA],
        cost=(1000, 4 << 20),
    )
    south = lax.ppermute(yp, "gy", ring("gy", 1))
    north = lax.ppermute(ym, "gy", ring("gy", -1))
    left = lax.ppermute(xp, "gx", ring("gx", 1))
    right = lax.ppermute(xm, "gx", ring("gx", -1))
    up, down = call(corners_body, [v(3 * T), v(3 * T)], [left, right], [VMEM] * 2, cost=(1000, 1 << 18))
    cs = lax.ppermute(up, "gy", ring("gy", 1))
    cn = lax.ppermute(down, "gy", ring("gy", -1))
    c1, cy, m1, my = call(
        first_body,
        [v(Z * XW * Y), v(4 * XA * Z), v(XA * Y), v(2 * X * Z)],
        [own, cloudy, left, right, south, north, kk, tt],
        [VMEM] * 8,
        cost=(3 << 30, 8 << 20),
    )
    a1, a1y, c2, c2y, a2, pay, cy = call(
        second_body,
        [v(4 * XA * T), v(2 * X * Z), v(2 * XA * T), v(2 * X * Z), v(2 * X * T), v(2 * NT * T), v(4 * XA * Z)],
        [sc, courant_u, courant_v, ub, vb, c1, cy, cs, cn, kk, tt, m1, my],
        [SMEM] * 3 + [VMEM] * 10,
        cost=(3 << 30, 8 << 20),
    )
    n = lax.axis_size("gz")
    above = lax.ppermute(pay, "gz", [(i, i - 1) for i in range(1, n)])
    a1_hi, a2_hi, out = call(
        third_body,
        [v(2 * XA * T), v(2 * X * T), ((Z * X * Y, B), F32, False)],
        [sc, courant_u, courant_v, c1, cy, a1, c2, c2y, a2, kk, tt, m1],
        [SMEM] * 3 + [VMEM] * 9,
        [
            pltpu.VMEM((8 * XA * T, B), F32),
            pltpu.VMEM((6 * XA * T, B), F32),
            pltpu.VMEM((6 * X * T, B), F32),
            pltpu.VMEM((4 * X * T, B), F32),
            pltpu.SemaphoreType.DMA,
        ],
        cost=(3 << 30, 8 << 20),
        out_specs=[VMEM, VMEM, ANY],
    )
    (out,) = call(
        last_body,
        [((Z * X * Y, B), F32, False)],
        [sc, courant_u, courant_v, a1_hi, a1y, a2_hi, south, north, kk, tt, m1, above, out],
        [SMEM] * 3 + [VMEM] * 9 + [ANY],
        [
            pltpu.VMEM((2 * XA * T, B), F32),
            pltpu.VMEM((4 * X, B), F32),
            pltpu.VMEM((4 * X * T, B), F32),
            pltpu.VMEM((4 * X * T, B), F32),
            pltpu.SemaphoreType.DMA,
        ],
        cost=(3 << 30, 8 << 20),
        out_specs=[ANY],
        aliases={12: 0},
    )
    return out.reshape(Z, X, Y, B)


def solution(mesh):
    in_specs = (P("gz", "gx", "gy", None), P(), P(), P("gz"), P("gz"), P(), P("gx", "gy"))
    out_specs = P("gz", "gx", "gy", None)
    return jax.shard_map(
        on_device, mesh=mesh, in_specs=in_specs, out_specs=out_specs, check_vma=False
    )
```

```python
import functools

import jax
import jax.numpy as jnp
from jax import lax
from jax.experimental import pallas as pl
from jax.experimental.pallas import tpu as pltpu
from jax.sharding import PartitionSpec as P

H_MAX = 2
STEPS = 2
Z, X, Y, B = 8, 64, 8, 128
T = 8
XW = X + 4
XA = X + 2
LOW = Z // 2
HALF = 2 * LOW * X
ENDS = HALF + 2 * X
XROWS = 2 * Z * Y
EARLY = (X - 2) + 2 * X // T + (X - 4)
GROUPS = 4
SPARE = B // GROUPS
EXTRA = -(-EARLY // GROUPS)
LATE = 4 + 1 + 4
F32, BF16 = jnp.float32, jnp.bfloat16

VMEM = pl.BlockSpec(memory_space=pltpu.VMEM)
SMEM = pl.BlockSpec(memory_space=pltpu.SMEM)
HBM = pl.BlockSpec(memory_space=pltpu.HBM)


def rows(start, n=T):
    return pl.ds(start if isinstance(start, int) else pl.multiple_of(start, T), n)


def call(body, outs, args, specs, scratch=(), cost=(0, 0), out_specs=None, aliases=None):
    shapes = [pltpu.VMEM(s, d) if m else jax.ShapeDtypeStruct(s, d) for s, d, m in outs]
    args = [
        a if s is SMEM else pltpu.with_memory_space_constraint(a, s.memory_space)
        for a, s in zip(args, specs)
    ]
    return pl.pallas_call(
        body,
        out_shape=shapes,
        in_specs=list(specs),
        out_specs=out_specs or [VMEM] * len(outs),
        scratch_shapes=list(scratch),
        input_output_aliases=aliases or {},
        cost_estimate=pl.CostEstimate(flops=cost[0], bytes_accessed=cost[1], transcendentals=0),
        compiler_params=pltpu.CompilerParams(vmem_limit_bytes=8 << 20),
    )(*args)


def split(x):
    high = x.astype(BF16)
    return high, (x - high.astype(F32)).astype(BF16)


def product(x, weights):
    out = jnp.dot(jnp.concatenate(split(x), axis=1), weights, preferred_element_type=F32)
    return out[:, :B] + out[:, B:]


def collide(s, cloudy, capture, transfer):
    loss = s * product(s, capture)
    return s + cloudy * (product(loss, transfer) - loss)


def eightfold(ref, row):
    return ref[pl.ds(row, T, stride=0), :]


def repeated(ref, start, n):
    return jnp.concatenate([eightfold(ref, start + i) for i in range(n)], axis=0)


def classes(sc_ref):
    lane = lax.broadcasted_iota(jnp.int32, (T, B), 1)
    return lane < sc_ref[0], lane >= sc_ref[1]


def fall(c0, c2, a, b, c):
    return jnp.where(c0, a, jnp.where(c2, c, b))


def edges_body(drops, cloud, k_in, t_in, own, m1, ym0, ym1, yp0, yp1, kk, tt, mask, k_ref, t_ref, sem):
    copies = [
        pltpu.make_async_copy(a, b, sem.at[i])
        for i, (a, b) in enumerate(((drops, own), (cloud, mask), (k_in, k_ref), (t_in, t_ref)))
    ]
    for copy in copies[1:] + copies[:1]:
        copy.start()
    copies[1].wait()
    columns = mask[...].astype(F32)
    for x in range(X):
        m1[(x + 1) * Y : (x + 2) * Y] = jnp.broadcast_to(columns[:, x : x + 1], (Y, B))
    for i, (ref, out, turned) in enumerate(((k_ref, kk, True), (t_ref, tt, False))):
        copies[2 + i].wait()
        w = ref[...].T if turned else ref[...]
        high, low = split(w)
        half = jnp.concatenate([high, low], axis=1)
        out[...] = jnp.concatenate([half, half], axis=0)
    for out, ys in ((ym0, (0, 1)), (yp0, (Y - 1, Y - 2))):
        for d, y in enumerate(ys):
            out[HALF + d * X : HALF + (d + 1) * X] = m1[pl.ds(Y + y, X, stride=Y), :]
    copies[0].wait()
    for outs, ys in (((ym0, ym1), (0, 1)), ((yp0, yp1), (Y - 1, Y - 2))):
        for part, out in enumerate(outs):
            for d, y in enumerate(ys):
                for z in range(LOW):
                    at = (d * LOW + z) * X
                    start = (part * LOW + z) * X * Y + y
                    out[at : at + X] = own[pl.ds(start, X, stride=Y), :]
        for i, x in enumerate((0, X - 1)):
            at, start = ENDS + i * LOW, (LOW * X + x) * Y + ys[0]
            outs[0][at : at + LOW] = own[pl.ds(start, LOW, stride=X * Y), :]


def sides_body(own, m1, south, north, xm, xp):
    for out, cols in ((xm, (0, 1)), (xp, (X - 1, X - 2))):
        for d, x in enumerate(cols):
            out[XROWS + d * Y : XROWS + (d + 1) * Y] = m1[(x + 1) * Y : (x + 2) * Y]
            for z in range(Z):
                at = (z * X + x) * Y
                out[(d * Z + z) * Y : (d * Z + z + 1) * Y] = own[at : at + Y]
        x = cols[0]
        at = XROWS + 2 * Y
        out[at + 2 * Z :] = jnp.zeros((T, B), F32)
        for side, ref in enumerate((south, north)):
            row = at + side * Z
            end = ENDS + (LOW if x else 0)
            out[row : row + LOW] = ref[pl.ds(x, LOW, stride=X), :]
            out[row + LOW : row + Z] = ref[end : end + LOW]
            row = at + 2 * Z + side
            out[row : row + 1] = ref[HALF + x : HALF + x + 1]


XMESSAGE = XROWS + 2 * Y + 2 * Z + T


def own_body(own, m1, kk, tt, c1):
    k, t, mask = kk[...], tt[...], m1[Y : Y + X * Y]

    def level(z, _):
        c1[rows((z * XW + 2) * Y, X * Y)] = collide(own[rows(z * X * Y, X * Y)], mask, k, t)
        return 0

    lax.fori_loop(0, Z, level, 0)


def cy_at(side, d, x):
    return ((side * 2 + d) * XA + x + 1) * Z


def collide_rows(part, south, north, masks, cy, k, t):
    for side, (ref, mask_ref) in enumerate(zip((south, north), masks)):
        for d in range(2):
            mask = jnp.concatenate([mask_ref[HALF + d * X : HALF + (d + 1) * X]] * LOW, axis=0)
            c = collide(ref[d * LOW * X : (d + 1) * LOW * X], mask, k, t)
            for z in range(LOW):
                cy[pl.ds(cy_at(side, d, 0) + part * LOW + z, X, stride=Z), :] = c[z * X : (z + 1) * X]


def upwind(z, u_ref, v_ref):
    u, v = u_ref[z], v_ref[z]
    at_edge = lax.broadcasted_iota(jnp.int32, (T, B), 0) == jnp.where(v > 0, 0, T - 1)
    return (
        jnp.abs(u),
        jnp.abs(v),
        jnp.where(u > 0, -Y, Y),
        jnp.where(v > 0, 1, T - 1),
        jnp.where(v > 0, 0, 1),
        at_edge,
    )


def advect(z, columns, c_ref, width, first, out_ref, out_width, edge, u_ref, v_ref):
    au, av, step, shift, side, at_edge = upwind(z, u_ref, v_ref)
    base, base_out = (z * width + first) * Y, z * out_width * Y
    edge_ref, edge_at, edge_stride = edge(z, side)
    for i in columns:
        c = c_ref[rows(base + i * Y)]
        x = c_ref[rows(base + step + i * Y)]
        e = eightfold(edge_ref, edge_at + i * edge_stride)
        y = jnp.where(at_edge, e, pltpu.roll(c, shift, 0))
        out_ref[rows(base_out + i * Y)] = c - au * (c - x) - av * (c - y)


def advect_first(z, columns, c1, a1, cy, u_ref, v_ref):
    edge = lambda z, side: (cy, side * (2 * XA * Z) + z, Z)
    advect(z, columns, c1, XW, 1, a1, XA, edge, u_ref, v_ref)


def advect_second(z, columns, c2, a2, c2y, u_ref, v_ref):
    edge = lambda z, side: (c2y, (z * 2 + side) * X, 1)
    advect(z, columns, c2, XA, 1, a2, X, edge, u_ref, v_ref)


def advect_rows(columns, ub, vb, c1, cy, a1y):
    au, av = jnp.abs(ub[...]), jnp.abs(vb[...])
    upos, vpos = ub[...] > 0, vb[...] > 0
    for side in range(2):
        for x in columns:
            at, far = cy_at(side, 0, x), cy_at(side, 1, x)
            c = cy[at : at + Z]
            xx = jnp.where(upos, cy[at - Z : at], cy[at + Z : at + 2 * Z])
            outer = cy[far : far + Z]
            inner = c1[pl.ds((x + 2) * Y + (Y - 1) * side, Z, stride=XW * Y), :]
            yy = jnp.where(vpos, *((outer, inner) if side == 0 else (inner, outer)))
            to = (side * X + x) * Z
            a1y[to : to + Z] = c - au * (c - xx) - av * (c - yy)


def settle(z, columns, c0, cc2, a1, c2):
    for i in columns:
        at = (z * XA + i) * T
        step = XA * T
        c2[rows(at)] = fall(c0, cc2, a1[rows(at)], a1[rows(at + step)], a1[rows(at + 2 * step)])


def settle_level(z, c0, cc2, a1, m1, c2, k, t):
    settle(z, range(XA), c0, cc2, a1, c2)
    at = rows(z * XA * T, XA * T)
    c2[at] = collide(c2[at], m1[...], k, t)


def settle_rows(z, c0, cc2, a1y, masks, c2y, k, t):
    for i in range(2 * X // T):
        a = [a1y[pl.ds(i * T * Z + z + j, T, stride=Z), :] for j in range(H_MAX + 1)]
        to = z * 2 * X + i * T
        c2y[to : to + T] = fall(c0, cc2, *a)
    at = slice(z * 2 * X, (z + 1) * 2 * X)
    mask = jnp.concatenate([m[HALF : HALF + X] for m in masks], axis=0)
    c2y[at] = collide(c2y[at], mask, k, t)


def falling(a1, a1y, a2, tile):
    if tile < X - 2:
        at = (tile + 2) * T
        return lambda z: a1[z * XA * T + at : z * XA * T + at + T]
    tile -= X - 2
    if tile < 2 * X // T:
        return lambda z: a1y[pl.ds(tile * T * Z + z, T, stride=Z), :]
    at = (tile - 2 * X // T + 2) * T
    return lambda z: a2[z * X * T + at : z * X * T + at + T]


def early_body(
    sc, u_ref, v_ref, ub, vb, c1, south, north, kk, tt, m1, cy, a1, a1y, c2, c2y, a2, pay
):
    k, t = kk[...], tt[...]
    c0, cc2 = classes(sc)
    collide_rows(0, south, north, (south, north), cy, k, t)

    def first(z, _):
        advect_first(z, range(2, X), c1, a1, cy, u_ref, v_ref)
        return 0

    lax.fori_loop(0, 4, first, 0)
    advect_rows(range(1, X - 1), ub, vb, c1, cy, a1y)

    def second(z, _):
        settle_level(z, c0, cc2, a1, m1, c2, k, t)
        return 0

    lax.fori_loop(0, 2, second, 0)
    for z in range(2):
        settle_rows(z, c0, cc2, a1y, (south, north), c2y, k, t)

    def third(z, _):
        advect_second(z, range(2, X - 2), c2, a2, c2y, u_ref, v_ref)
        return 0

    lax.fori_loop(0, 2, third, 0)
    n0 = sc[0]
    n2 = B - sc[1]
    for tile in range(EARLY):
        level = falling(a1, a1y, a2, tile)
        l0 = level(0)
        packed = fall(c0, cc2, pltpu.roll(l0, n2, 1), l0, level(1))
        pay[tile * T : (tile + 1) * T] = packed
    group = lax.broadcasted_iota(jnp.int32, (T, B), 1) // SPARE
    for j in range(EXTRA):
        out = jnp.zeros((T, B), F32)
        for g in range(GROUPS):
            if j + g * EXTRA < EARLY:
                l0 = falling(a1, a1y, a2, j + g * EXTRA)(0)
                turn = (n2 - n0 + g * SPARE + B) & (B - 1)
                out = jnp.where(group == g, pltpu.roll(l0, turn, 1), out)
        pay[(EARLY + j) * T : (EARLY + j + 1) * T] = out


EDGE = (0, 1, XA - 2, XA - 1)


def late_body(
    sc, u_ref, v_ref, ub, vb, left, right, kk, tt, south, north,
    c1_in, cy_in, m1_in, a1_in, a1y_in, c2_in, c2y_in, a2_in,
    c1, cy, m1, a1, a1y, c2, c2y, a2, pay,
):
    k, t = kk[...], tt[...]
    c0, cc2 = classes(sc)
    m1[0:Y] = left[XROWS : XROWS + Y]
    m1[Y + X * Y :] = right[XROWS : XROWS + Y]
    at_mask = XROWS + 2 * Y
    pieces, masks = [], []
    for ref in (left, right):
        pieces += [ref[0:XROWS], ref[at_mask : at_mask + 2 * Z]]
        masks += [ref[XROWS + d * Y : XROWS + (d + 1) * Y] for d in range(2) for _ in range(Z)]
        masks += [eightfold(ref, at_mask + 2 * Z + side) for side in range(2)]
    c = collide(jnp.concatenate(pieces, axis=0), jnp.concatenate(masks, axis=0), k, t)
    size = XROWS + 2 * Z
    for i, (columns, x) in enumerate((((1, 0), -1), ((XW - 2, XW - 1), X))):
        for d in range(2):
            for z in range(Z):
                at, to = i * size + (d * Z + z) * Y, (z * XW + columns[d]) * Y
                c1[to : to + Y] = c[at : at + Y]
        for side in range(2):
            at, to = i * size + XROWS + side * Z, cy_at(side, 0, x)
            cy[to : to + Z] = c[at : at + Z]

    for z in range(4):
        advect_first(z, EDGE, c1, a1, cy, u_ref, v_ref)
    advect_rows((0, X - 1), ub, vb, c1, cy, a1y)
    for z in range(2):
        settle(z, EDGE, c0, cc2, a1, c2)
    tiles = [(z * XA + i) * T for z in range(2) for i in EDGE]
    c = collide(
        jnp.concatenate([c2[at : at + T] for at in tiles], axis=0),
        jnp.concatenate([m1[i * T : (i + 1) * T] for i in EDGE] * 2, axis=0),
        k,
        t,
    )
    for i, at in enumerate(tiles):
        c2[at : at + T] = c[i * T : (i + 1) * T]
    for z in range(2):
        settle_rows(z, c0, cc2, a1y, (south, north), c2y, k, t)
        advect_second(z, (0, 1, X - 2, X - 1), c2, a2, c2y, u_ref, v_ref)
    for i, x in enumerate(EDGE):
        l0, l1 = (a1[(z * XA + x) * T : (z * XA + x + 1) * T] for z in range(2))
        pay[i * T : (i + 1) * T] = fall(c0, cc2, l0, l0, l1)
        pay[(LATE + i) * T : (LATE + i + 1) * T] = l0
    at = 4 * T
    for i, row in enumerate((0, X - 1, X, 2 * X - 1)):
        l0, l1 = (a1y[row * Z + z : row * Z + z + 1] for z in range(2))
        pay[at + i : at + i + 1] = fall(c0[0:1], cc2[0:1], l0, l0, l1)
        pay[at + LATE * T + i : at + LATE * T + i + 1] = l0
    for first in (at + 4, at + LATE * T + 4):
        pay[first : first + 4] = jnp.zeros((4, B), F32)
    for i, x in enumerate((0, 1, X - 2, X - 1)):
        l0, l1 = (a2[(z * X + x) * T : (z * X + x + 1) * T] for z in range(2))
        to = at + (i + 1) * T
        pay[to : to + T] = fall(c0, cc2, l0, l0, l1)
        pay[to + LATE * T : to + LATE * T + T] = l0


def rest_body(
    sc, u_ref, v_ref, ub, vb, kk, tt, south0, south1, north0, north1, c1, m1,
    cy_in, a1_in, a1y_in, c2_in, c2y_in, a2_in,
    cy, a1, a1y, c2, c2y, a2, out, res, sem,
):
    k, t = kk[...], tt[...]
    c0, cc2 = classes(sc)
    collide_rows(1, south1, north1, (south0, north0), cy, k, t)

    def first(z, _):
        advect_first(z, range(XA), c1, a1, cy, u_ref, v_ref)
        return 0

    lax.fori_loop(4, 8, first, 0)
    advect_rows(range(X), ub, vb, c1, cy, a1y)

    def second(z, _):
        settle_level(z, c0, cc2, a1, m1, c2, k, t)
        return 0

    lax.fori_loop(2, 6, second, 0)
    for z in range(2, 6):
        settle_rows(z, c0, cc2, a1y, (south0, north0), c2y, k, t)

    def third(z, _):
        advect_second(z, range(X), c2, a2, c2y, u_ref, v_ref)
        return 0

    lax.fori_loop(2, 6, third, 0)

    def done(z, _):
        for i in range(X):
            at, step = (z * X + i) * T, X * T
            res[rows(at)] = fall(c0, cc2, a2[rows(at)], a2[rows(at + step)], a2[rows(at + 2 * step)])
        return 0

    lax.fori_loop(0, 4, done, 0)
    copy = pltpu.make_async_copy(res, out.at[pl.ds(0, 4 * X * T)], sem)
    copy.start()
    copy.wait()


def last_body(
    sc, u_ref, v_ref, kk, tt, south, north, m1, a1, a1y, c2_in, c2y_in, a2_in, early, late, out_in,
    out, c2, c2y, a2, row7, row6, res, sem,
):
    k, t = kk[...], tt[...]
    c0, cc2 = classes(sc)
    n0, start2 = sc[0], sc[1]
    lane = lax.broadcasted_iota(jnp.int32, (T, B), 1)
    within = lane < start2 + n0
    turns = [(n0 + start2 - g * SPARE + B) & (B - 1) for g in range(GROUPS)]

    def from_above(tile):
        m = early[tile * T : (tile + 1) * T]
        g, j = tile // EXTRA, tile % EXTRA
        spare = early[(EARLY + j) * T : (EARLY + j + 1) * T]
        return m, jnp.where(within, pltpu.roll(m, start2, 1), pltpu.roll(spare, turns[g], 1))

    def from_late(i):
        return late[i * T : (i + 1) * T], late[(LATE + i) * T : (LATE + i + 1) * T]

    for i in range(XA):
        p7, p6 = from_late(EDGE.index(i)) if i in EDGE else from_above(i - 2)
        x6, x7 = (a1[(z * XA + i) * T : (z * XA + i + 1) * T] for z in (6, 7))
        c2[(6 * XA + i) * T : (6 * XA + i + 1) * T] = fall(c0, cc2, x6, x7, p6)
        c2[(7 * XA + i) * T : (7 * XA + i + 1) * T] = jnp.where(c0, x7, p7)
    for i in range(2 * X // T):
        row7[i * T : (i + 1) * T], row6[i * T : (i + 1) * T] = from_above(X - 2 + i)
    p7, p6 = from_late(4)
    for i, row in enumerate((0, X - 1, X, 2 * X - 1)):
        row7[row : row + 1], row6[row : row + 1] = p7[i : i + 1], p6[i : i + 1]
    for i in range(2 * X // T):
        x6, x7 = (a1y[pl.ds(i * T * Z + z, T, stride=Z), :] for z in (6, 7))
        at = 6 * 2 * X + i * T
        c2y[at : at + T] = fall(c0, cc2, x6, x7, row6[i * T : (i + 1) * T])
        c2y[at + 2 * X : at + 2 * X + T] = jnp.where(c0, x7, row7[i * T : (i + 1) * T])
    mask = jnp.concatenate([south[HALF : HALF + X], north[HALF : HALF + X]] * 2, axis=0)
    at = slice(12 * X, 16 * X)
    c2y[at] = collide(c2y[at], mask, k, t)
    for z in (6, 7):
        at = slice(z * XA * T, (z + 1) * XA * T)
        c2[at] = collide(c2[at], m1[...], k, t)
        advect_second(z, range(X), c2, a2, c2y, u_ref, v_ref)
    for i in range(X):
        ends = (0, 1, X - 2, X - 1)
        tile = X - 2 + 2 * X // T + i - 2
        p7, p6 = from_late(5 + ends.index(i)) if i in ends else from_above(tile)
        x = [a2[(z * X + i) * T : (z * X + i + 1) * T] for z in range(4, 8)]
        for z, v in enumerate(
            (
                fall(c0, cc2, x[0], x[1], x[2]),
                fall(c0, cc2, x[1], x[2], x[3]),
                fall(c0, cc2, x[2], x[3], p6),
                jnp.where(c0, x[3], p7),
            )
        ):
            res[(z * X + i) * T : (z * X + i + 1) * T] = v
    copy = pltpu.make_async_copy(res, out.at[pl.ds(4 * X * T, 4 * X * T)], sem)
    copy.start()
    copy.wait()


def ring(axis, step):
    n = lax.axis_size(axis)
    return [(i, (i + step) % n) for i in range(n)]


def below(value):
    return lax.ppermute(value, "gz", [(i, i - 1) for i in range(1, lax.axis_size("gz"))])


def packed(n0, n2, drops, capture, transfer, courant_u, courant_v, fall_class, cloud_mask):
    drops = drops.reshape(Z * X * Y, B)
    sc = jnp.stack([n0, B - n2])
    ub = jnp.broadcast_to(courant_u[:, None], (Z, B))
    vb = jnp.broadcast_to(courant_v[:, None], (Z, B))
    v = lambda n, d=F32: ((n, B), d, True)
    weights = [((2 * B, 2 * B), BF16, True)] * 2
    own, m1, ym0, ym1, yp0, yp1, kk, tt = call(
        edges_body,
        [v(Z * X * Y), v(XA * Y), v(ENDS + T), v(HALF), v(ENDS + T), v(HALF)] + weights,
        [drops, cloud_mask.T, capture, transfer],
        [HBM] * 4,
        [pltpu.VMEM((Y, X), jnp.int32), pltpu.VMEM((B, B), F32), pltpu.VMEM((B, B), F32), pltpu.SemaphoreType.DMA((4,))],
        cost=(1000, 4 << 20),
    )
    south0 = lax.ppermute(yp0, "gy", ring("gy", 1))
    north0 = lax.ppermute(ym0, "gy", ring("gy", -1))
    south1 = lax.ppermute(yp1, "gy", ring("gy", 1))
    north1 = lax.ppermute(ym1, "gy", ring("gy", -1))
    (c1,) = call(own_body, [v(Z * XW * Y)], [own, m1, kk, tt], [VMEM] * 4, cost=(3 << 30, 8 << 20))
    shapes = [v(4 * XA * Z), v(Z * XA * T), v(2 * X * Z), v(Z * XA * T), v(Z * 2 * X), v(Z * X * T)]
    scalars = [sc, courant_u, courant_v]
    cy, a1, a1y, c2, c2y, a2, pay = call(
        early_body,
        shapes + [v((EARLY + EXTRA) * T)],
        scalars + [ub, vb, c1, south0, north0, kk, tt, m1],
        [SMEM] * 3 + [VMEM] * 8,
        cost=(1 << 30, 4 << 20),
    )
    early = below(pay)
    xm, xp = call(
        sides_body,
        [v(XMESSAGE)] * 2,
        [own, m1, south0, north0],
        [VMEM] * 4,
        cost=(1000, 1 << 18),
    )
    left = lax.ppermute(xp, "gx", ring("gx", 1))
    right = lax.ppermute(xm, "gx", ring("gx", -1))
    c1, cy, m1, a1, a1y, c2, c2y, a2, pay = call(
        late_body,
        [v(Z * XW * Y), shapes[0], v(XA * Y)] + shapes[1:] + [v(2 * LATE * T)],
        scalars + [ub, vb, left, right, kk, tt, south0, north0, c1, cy, m1, a1, a1y, c2, c2y, a2],
        [SMEM] * 3 + [VMEM] * 16,
        cost=(1 << 28, 1 << 20),
        aliases={11 + i: i for i in range(8)},
    )
    late = below(pay)
    *state, out = call(
        rest_body,
        shapes + [((Z * X * Y, B), F32, False)],
        scalars + [ub, vb, kk, tt, south0, south1, north0, north1, c1, m1, cy, a1, a1y, c2, c2y, a2],
        [SMEM] * 3 + [VMEM] * 16,
        [pltpu.VMEM((4 * X * T, B), F32), pltpu.SemaphoreType.DMA],
        cost=(3 << 30, 8 << 20),
        out_specs=[VMEM] * 6 + [HBM],
        aliases={13 + i: i for i in range(6)},
    )
    (cy, a1, a1y, c2, c2y, a2) = state
    out, *_ = call(
        last_body,
        [((Z * X * Y, B), F32, False), shapes[3], shapes[4], shapes[5]],
        scalars + [kk, tt, south0, north0, m1, a1, a1y, c2, c2y, a2, early, late, out],
        [SMEM] * 3 + [VMEM] * 12 + [HBM],
        [pltpu.VMEM((2 * X, B), F32), pltpu.VMEM((2 * X, B), F32), pltpu.VMEM((4 * X * T, B), F32), pltpu.SemaphoreType.DMA],
        cost=(1 << 30, 8 << 20),
        out_specs=[HBM] + [VMEM] * 3,
        aliases={15: 0, 10: 1, 11: 2, 12: 3},
    )
    return out.reshape(Z, X, Y, B)


def passed_along(block, axis, distance):
    devices = range(lax.axis_size(axis))
    route = [(i - distance, i) for i in devices if i - distance in devices]
    return lax.ppermute(block, axis, route)


def with_halo(value, sides, width):
    edges = {}
    for axis, dim in sides:
        devices, length = (lax.axis_size(axis), value.shape[dim])
        up = [(i, (i + 1) % devices) for i in range(devices)]
        last = lax.slice_in_dim(value, length - width, length, axis=dim)
        leading = lax.slice_in_dim(value, 0, width, axis=dim)
        edges[dim] = (
            lax.ppermute(last, axis, up),
            lax.ppermute(leading, axis, [(b, a) for a, b in up]),
        )
    done = []
    for _, dim in sides:
        low, high = edges[dim]
        around = [(width, width) if d in done else (0, 0) for d in range(value.ndim)]
        value = jnp.concatenate([jnp.pad(low, around), value, jnp.pad(high, around)], axis=dim)
        done.append(dim)
    return value


def collide_plain(particle_distribution, capture_efficiency_matrix, transfer, cloudy):
    merger_speed = jnp.einsum(
        "ugcr,mr->ugcm",
        particle_distribution,
        capture_efficiency_matrix,
        precision=lax.Precision.HIGHEST,
    )
    water_removed = particle_distribution * merger_speed
    mass_gain = jnp.einsum(
        "zxyi,ik->zxyk", water_removed, transfer, precision=lax.Precision.HIGHEST
    )
    return particle_distribution + cloudy[None, :, :, None] * (mass_gain - water_removed)


def advect_plain(with_edges, courant_u, courant_v):
    centre = with_edges[:, 1:-1, 1:-1]
    west_side = with_edges[:, :-2, 1:-1]
    east_side = with_edges[:, 2:, 1:-1]
    south_side = with_edges[:, 1:-1, :-2]
    north_side = with_edges[:, 1:-1, 2:]
    x_plus = jnp.maximum(courant_u, 0.0)[:, None, None, None]
    x_minus = jnp.minimum(courant_u, 0.0)[:, None, None, None]
    northward_neighbor = jnp.maximum(courant_v, 0.0)[:, None, None, None]
    y_minus = jnp.minimum(courant_v, 0.0)[:, None, None, None]
    result = centre - x_plus * (centre - west_side) - x_minus * (east_side - centre)
    return result - northward_neighbor * (centre - south_side) - y_minus * (north_side - centre)


def sediment(padded, fall_class, levels):
    result = padded[:levels]
    for fall_depth in range(1, H_MAX + 1):
        result = jnp.where(
            (fall_class == fall_depth)[None, None, None, :],
            padded[fall_depth : fall_depth + levels],
            result,
        )
    return result


def plain(
    drops, capture_efficiency_matrix, transfer, courant_u, courant_v, fall_class, cloud_mask
):
    cloudy = cloud_mask.astype(jnp.float32)
    reach = STEPS * H_MAX
    from_above, upper_u, upper_v = passed_along(
        (drops[:reach], courant_u[:reach], courant_v[:reach]), "gz", -1
    )
    particle_distribution = jnp.concatenate([drops, from_above], axis=0)
    column_u = jnp.concatenate([courant_u, upper_u], axis=0)
    column_v = jnp.concatenate([courant_v, upper_v], axis=0)
    for repeat in range(STEPS):
        current = particle_distribution.shape[0]
        coalesced_drops = collide_plain(
            particle_distribution, capture_efficiency_matrix, transfer, cloudy
        )
        with_edges = with_halo(coalesced_drops, (("gx", 1), ("gy", 2)), 1)
        advected = advect_plain(with_edges, column_u[:current], column_v[:current])
        particle_distribution = sediment(advected, fall_class, current - H_MAX)
    return particle_distribution


def on_device(*args):
    fall_class = args[5]
    n0 = jnp.sum((fall_class == 0).astype(jnp.int32))
    n2 = jnp.sum((fall_class == H_MAX).astype(jnp.int32))
    return lax.cond(
        n2 - n0 <= SPARE, lambda a: packed(*a), lambda a: plain(*a[2:]), (n0, n2, *args)
    )


def solution(mesh):
    in_specs = (P("gz", "gx", "gy", None), P(), P(), P("gz"), P("gz"), P(), P("gx", "gy"))
    out_specs = P("gz", "gx", "gy", None)
    return jax.shard_map(
        on_device, mesh=mesh, in_specs=in_specs, out_specs=out_specs, check_vma=False
    )
```

```python
import functools

import jax
import jax.numpy as jnp
from jax import lax
from jax.experimental import pallas as pl
from jax.experimental.pallas import tpu as pltpu
from jax.sharding import PartitionSpec as P

H_MAX = 2
STEPS = 2
Z, X, Y, B = 8, 64, 8, 128
T = 8
XW = X + 4
XA = X + 2
HALO = 2 * Z * X
XROWS = 2 * Z * Y
EARLY = (X - 2) + 2 * X // T + (X - 4)
GROUPS = 4
SPARE = B // GROUPS
EXTRA = -(-EARLY // GROUPS)
LATE = 4 + 1 + 4
F32, BF16 = jnp.float32, jnp.bfloat16

VMEM = pl.BlockSpec(memory_space=pltpu.VMEM)
SMEM = pl.BlockSpec(memory_space=pltpu.SMEM)
HBM = pl.BlockSpec(memory_space=pltpu.HBM)


def rows(start, n=T):
    return pl.ds(start if isinstance(start, int) else pl.multiple_of(start, T), n)


def call(body, outs, args, specs, scratch=(), cost=(0, 0), out_specs=None, aliases=None):
    shapes = [pltpu.VMEM(s, d) if m else jax.ShapeDtypeStruct(s, d) for s, d, m in outs]
    args = [
        a if s is SMEM else pltpu.with_memory_space_constraint(a, s.memory_space)
        for a, s in zip(args, specs)
    ]
    return pl.pallas_call(
        body,
        out_shape=shapes,
        in_specs=list(specs),
        out_specs=out_specs or [VMEM] * len(outs),
        scratch_shapes=list(scratch),
        input_output_aliases=aliases or {},
        cost_estimate=pl.CostEstimate(flops=cost[0], bytes_accessed=cost[1], transcendentals=0),
        compiler_params=pltpu.CompilerParams(vmem_limit_bytes=8 << 20),
    )(*args)


def split(x):
    high = x.astype(BF16)
    return high, (x - high.astype(F32)).astype(BF16)


def product(x, weights):
    out = jnp.dot(jnp.concatenate(split(x), axis=1), weights, preferred_element_type=F32)
    return out[:, :B] + out[:, B:]


def collide(s, cloudy, capture, transfer):
    loss = s * product(s, capture)
    return s + cloudy * (product(loss, transfer) - loss)


def eightfold(ref, row):
    return ref[pl.ds(row, T, stride=0), :]


def repeated(ref, start, n):
    return jnp.concatenate([eightfold(ref, start + i) for i in range(n)], axis=0)


def classes(sc_ref):
    lane = lax.broadcasted_iota(jnp.int32, (T, B), 1)
    return lane < sc_ref[0], lane >= sc_ref[1]


def fall(c0, c2, a, b, c):
    return jnp.where(c0, a, jnp.where(c2, c, b))


def edges_body(drops, cloud, k_in, t_in, own, m1, ym, yp, kk, tt, mask, k_ref, t_ref, sem):
    copies = [
        pltpu.make_async_copy(a, b, sem.at[i])
        for i, (a, b) in enumerate(((drops, own), (cloud, mask), (k_in, k_ref), (t_in, t_ref)))
    ]
    for copy in copies[1:] + copies[:1]:
        copy.start()
    copies[1].wait()
    columns = mask[...].astype(F32)
    for x in range(X):
        m1[(x + 1) * Y : (x + 2) * Y] = jnp.broadcast_to(columns[:, x : x + 1], (Y, B))
    for i, (ref, out, turned) in enumerate(((k_ref, kk, True), (t_ref, tt, False))):
        copies[2 + i].wait()
        w = ref[...].T if turned else ref[...]
        high, low = split(w)
        half = jnp.concatenate([high, low], axis=1)
        out[...] = jnp.concatenate([half, half], axis=0)
    for out, ys in ((ym, (0, 1)), (yp, (Y - 1, Y - 2))):
        for d, y in enumerate(ys):
            out[HALO + d * X : HALO + (d + 1) * X] = m1[pl.ds(Y + y, X, stride=Y), :]
    copies[0].wait()
    for out, ys in ((ym, (0, 1)), (yp, (Y - 1, Y - 2))):
        for d, y in enumerate(ys):
            for z in range(Z):
                at = (d * Z + z) * X
                out[at : at + X] = own[pl.ds(z * X * Y + y, X, stride=Y), :]


def sides_body(own, m1, south, north, xm, xp):
    for out, cols in ((xm, (0, 1)), (xp, (X - 1, X - 2))):
        for d, x in enumerate(cols):
            out[XROWS + d * Y : XROWS + (d + 1) * Y] = m1[(x + 1) * Y : (x + 2) * Y]
            for z in range(Z):
                at = (z * X + x) * Y
                out[(d * Z + z) * Y : (d * Z + z + 1) * Y] = own[at : at + Y]
        x = cols[0]
        at = XROWS + 2 * Y
        out[at + 2 * Z :] = jnp.zeros((T, B), F32)
        for side, ref in enumerate((south, north)):
            row = at + side * Z
            out[row : row + Z] = ref[pl.ds(x, Z, stride=X), :]
            row = at + 2 * Z + side
            out[row : row + 1] = ref[HALO + x : HALO + x + 1]


XMESSAGE = XROWS + 2 * Y + 2 * Z + T


def own_body(own, m1, kk, tt, c1):
    k, t, mask = kk[...], tt[...], m1[Y : Y + X * Y]

    def level(z, _):
        c1[rows((z * XW + 2) * Y, X * Y)] = collide(own[rows(z * X * Y, X * Y)], mask, k, t)
        return 0

    lax.fori_loop(0, Z, level, 0, unroll=4)


def cy_at(side, d, x):
    return ((side * 2 + d) * XA + x + 1) * Z


def collide_rows(south, north, cy, k, t):
    for side, ref in enumerate((south, north)):
        for d in range(2):
            mask = jnp.concatenate([ref[HALO + d * X : HALO + (d + 1) * X]] * Z, axis=0)
            c = collide(ref[d * Z * X : (d + 1) * Z * X], mask, k, t)
            for z in range(Z):
                cy[pl.ds(cy_at(side, d, 0) + z, X, stride=Z), :] = c[z * X : (z + 1) * X]


def upwind(z, u_ref, v_ref):
    u, v = u_ref[z], v_ref[z]
    at_edge = lax.broadcasted_iota(jnp.int32, (T, B), 0) == jnp.where(v > 0, 0, T - 1)
    return (
        jnp.abs(u),
        jnp.abs(v),
        jnp.where(u > 0, -Y, Y),
        jnp.where(v > 0, 1, T - 1),
        jnp.where(v > 0, 0, 1),
        at_edge,
    )


def advect(z, columns, c_ref, width, first, out_ref, out_width, edge, u_ref, v_ref):
    au, av, step, shift, side, at_edge = upwind(z, u_ref, v_ref)
    base, base_out = (z * width + first) * Y, z * out_width * Y
    edge_ref, edge_at, edge_stride = edge(z, side)
    for i in columns:
        c = c_ref[rows(base + i * Y)]
        x = c_ref[rows(base + step + i * Y)]
        e = eightfold(edge_ref, edge_at + i * edge_stride)
        y = jnp.where(at_edge, e, pltpu.roll(c, shift, 0))
        out_ref[rows(base_out + i * Y)] = c - au * (c - x) - av * (c - y)


def advect_first(z, columns, c1, a1, cy, u_ref, v_ref):
    edge = lambda z, side: (cy, side * (2 * XA * Z) + z, Z)
    advect(z, columns, c1, XW, 1, a1, XA, edge, u_ref, v_ref)


def advect_second(z, columns, c2, a2, c2y, u_ref, v_ref):
    edge = lambda z, side: (c2y, (z * 2 + side) * X, 1)
    advect(z, columns, c2, XA, 1, a2, X, edge, u_ref, v_ref)


def advect_rows(columns, ub, vb, c1, cy, a1y):
    au, av = jnp.abs(ub[...]), jnp.abs(vb[...])
    upos, vpos = ub[...] > 0, vb[...] > 0
    for side in range(2):
        for x in columns:
            at, far = cy_at(side, 0, x), cy_at(side, 1, x)
            c = cy[at : at + Z]
            xx = jnp.where(upos, cy[at - Z : at], cy[at + Z : at + 2 * Z])
            outer = cy[far : far + Z]
            inner = c1[pl.ds((x + 2) * Y + (Y - 1) * side, Z, stride=XW * Y), :]
            yy = jnp.where(vpos, *((outer, inner) if side == 0 else (inner, outer)))
            to = (side * X + x) * Z
            a1y[to : to + Z] = c - au * (c - xx) - av * (c - yy)


def settle(z, columns, c0, cc2, a1, c2):
    for i in columns:
        at = (z * XA + i) * T
        step = XA * T
        c2[rows(at)] = fall(c0, cc2, a1[rows(at)], a1[rows(at + step)], a1[rows(at + 2 * step)])


def settle_level(z, c0, cc2, a1, m1, c2, k, t):
    settle(z, range(XA), c0, cc2, a1, c2)
    at = rows(z * XA * T, XA * T)
    c2[at] = collide(c2[at], m1[...], k, t)


def settle_rows(z, c0, cc2, a1y, masks, c2y, k, t):
    for i in range(2 * X // T):
        a = [a1y[pl.ds(i * T * Z + z + j, T, stride=Z), :] for j in range(H_MAX + 1)]
        to = z * 2 * X + i * T
        c2y[to : to + T] = fall(c0, cc2, *a)
    at = slice(z * 2 * X, (z + 1) * 2 * X)
    mask = jnp.concatenate([m[HALO : HALO + X] for m in masks], axis=0)
    c2y[at] = collide(c2y[at], mask, k, t)


def falling(a1, a1y, a2, tile):
    if tile < X - 2:
        at = (tile + 2) * T
        return lambda z: a1[z * XA * T + at : z * XA * T + at + T]
    tile -= X - 2
    if tile < 2 * X // T:
        return lambda z: a1y[pl.ds(tile * T * Z + z, T, stride=Z), :]
    at = (tile - 2 * X // T + 2) * T
    return lambda z: a2[z * X * T + at : z * X * T + at + T]


def early_body(
    sc, u_ref, v_ref, ub, vb, c1, south, north, kk, tt, m1, cy, a1, a1y, c2, c2y, a2, pay
):
    k, t = kk[...], tt[...]
    c0, cc2 = classes(sc)
    collide_rows(south, north, cy, k, t)

    def first(z, _):
        advect_first(z, range(2, X), c1, a1, cy, u_ref, v_ref)
        return 0

    lax.fori_loop(0, 4, first, 0)
    advect_rows(range(1, X - 1), ub, vb, c1, cy, a1y)

    def second(z, _):
        settle_level(z, c0, cc2, a1, m1, c2, k, t)
        return 0

    lax.fori_loop(0, 2, second, 0, unroll=2)
    for z in range(2):
        settle_rows(z, c0, cc2, a1y, (south, north), c2y, k, t)

    def third(z, _):
        advect_second(z, range(2, X - 2), c2, a2, c2y, u_ref, v_ref)
        return 0

    lax.fori_loop(0, 2, third, 0)
    n0 = sc[0]
    n2 = B - sc[1]
    for tile in range(EARLY):
        level = falling(a1, a1y, a2, tile)
        l0 = level(0)
        packed = fall(c0, cc2, pltpu.roll(l0, n2, 1), l0, level(1))
        pay[tile * T : (tile + 1) * T] = packed
    group = lax.broadcasted_iota(jnp.int32, (T, B), 1) // SPARE
    for j in range(EXTRA):
        out = jnp.zeros((T, B), F32)
        for g in range(GROUPS):
            if j + g * EXTRA < EARLY:
                l0 = falling(a1, a1y, a2, j + g * EXTRA)(0)
                turn = (n2 - n0 + g * SPARE + B) & (B - 1)
                out = jnp.where(group == g, pltpu.roll(l0, turn, 1), out)
        pay[(EARLY + j) * T : (EARLY + j + 1) * T] = out


EDGE = (0, 1, XA - 2, XA - 1)


def late_body(
    sc, u_ref, v_ref, ub, vb, left, right, kk, tt, south, north,
    c1_in, cy_in, m1_in, a1_in, a1y_in, c2_in, c2y_in, a2_in,
    c1, cy, m1, a1, a1y, c2, c2y, a2, pay,
):
    k, t = kk[...], tt[...]
    c0, cc2 = classes(sc)
    m1[0:Y] = left[XROWS : XROWS + Y]
    m1[Y + X * Y :] = right[XROWS : XROWS + Y]
    at_mask = XROWS + 2 * Y
    pieces, masks = [], []
    for ref in (left, right):
        pieces += [ref[0:XROWS], ref[at_mask : at_mask + 2 * Z]]
        masks += [ref[XROWS + d * Y : XROWS + (d + 1) * Y] for d in range(2) for _ in range(Z)]
        masks += [eightfold(ref, at_mask + 2 * Z + side) for side in range(2)]
    c = collide(jnp.concatenate(pieces, axis=0), jnp.concatenate(masks, axis=0), k, t)
    size = XROWS + 2 * Z
    for i, (columns, x) in enumerate((((1, 0), -1), ((XW - 2, XW - 1), X))):
        for d in range(2):
            for z in range(Z):
                at, to = i * size + (d * Z + z) * Y, (z * XW + columns[d]) * Y
                c1[to : to + Y] = c[at : at + Y]
        for side in range(2):
            at, to = i * size + XROWS + side * Z, cy_at(side, 0, x)
            cy[to : to + Z] = c[at : at + Z]

    for z in range(4):
        advect_first(z, EDGE, c1, a1, cy, u_ref, v_ref)
    advect_rows((0, X - 1), ub, vb, c1, cy, a1y)
    for z in range(2):
        settle(z, EDGE, c0, cc2, a1, c2)
    tiles = [(z * XA + i) * T for z in range(2) for i in EDGE]
    c = collide(
        jnp.concatenate([c2[at : at + T] for at in tiles], axis=0),
        jnp.concatenate([m1[i * T : (i + 1) * T] for i in EDGE] * 2, axis=0),
        k,
        t,
    )
    for i, at in enumerate(tiles):
        c2[at : at + T] = c[i * T : (i + 1) * T]
    for z in range(2):
        settle_rows(z, c0, cc2, a1y, (south, north), c2y, k, t)
        advect_second(z, (0, 1, X - 2, X - 1), c2, a2, c2y, u_ref, v_ref)
    for i, x in enumerate(EDGE):
        l0, l1 = (a1[(z * XA + x) * T : (z * XA + x + 1) * T] for z in range(2))
        pay[i * T : (i + 1) * T] = fall(c0, cc2, l0, l0, l1)
        pay[(LATE + i) * T : (LATE + i + 1) * T] = l0
    at = 4 * T
    for i, row in enumerate((0, X - 1, X, 2 * X - 1)):
        l0, l1 = (a1y[row * Z + z : row * Z + z + 1] for z in range(2))
        pay[at + i : at + i + 1] = fall(c0[0:1], cc2[0:1], l0, l0, l1)
        pay[at + LATE * T + i : at + LATE * T + i + 1] = l0
    for first in (at + 4, at + LATE * T + 4):
        pay[first : first + 4] = jnp.zeros((4, B), F32)
    for i, x in enumerate((0, 1, X - 2, X - 1)):
        l0, l1 = (a2[(z * X + x) * T : (z * X + x + 1) * T] for z in range(2))
        to = at + (i + 1) * T
        pay[to : to + T] = fall(c0, cc2, l0, l0, l1)
        pay[to + LATE * T : to + LATE * T + T] = l0


def rest_body(
    sc, u_ref, v_ref, ub, vb, kk, tt, south, north, c1, m1, cy,
    a1_in, a1y_in, c2_in, c2y_in, a2_in,
    a1, a1y, c2, c2y, a2, out, res, sem,
):
    k, t = kk[...], tt[...]
    c0, cc2 = classes(sc)

    def first(z, _):
        advect_first(z, range(XA), c1, a1, cy, u_ref, v_ref)
        return 0

    lax.fori_loop(4, 8, first, 0)
    advect_rows(range(X), ub, vb, c1, cy, a1y)

    def second(z, _):
        settle_level(z, c0, cc2, a1, m1, c2, k, t)
        return 0

    lax.fori_loop(2, 6, second, 0, unroll=4)
    for z in range(2, 6):
        settle_rows(z, c0, cc2, a1y, (south, north), c2y, k, t)

    def third(z, _):
        advect_second(z, range(X), c2, a2, c2y, u_ref, v_ref)
        return 0

    lax.fori_loop(2, 6, third, 0)

    def done(z, _):
        for i in range(X):
            at, step = (z * X + i) * T, X * T
            res[rows(at)] = fall(c0, cc2, a2[rows(at)], a2[rows(at + step)], a2[rows(at + 2 * step)])
        return 0

    lax.fori_loop(0, 4, done, 0)
    copy = pltpu.make_async_copy(res, out.at[pl.ds(0, 4 * X * T)], sem)
    copy.start()
    copy.wait()


def last_body(
    sc, u_ref, v_ref, kk, tt, south, north, m1, a1, a1y, c2_in, c2y_in, a2_in, early, late, out_in,
    out, c2, c2y, a2, row7, row6, res, sem,
):
    k, t = kk[...], tt[...]
    c0, cc2 = classes(sc)
    n0, start2 = sc[0], sc[1]
    lane = lax.broadcasted_iota(jnp.int32, (T, B), 1)
    within = lane < start2 + n0
    turns = [(n0 + start2 - g * SPARE + B) & (B - 1) for g in range(GROUPS)]

    def from_above(tile):
        m = early[tile * T : (tile + 1) * T]
        g, j = tile // EXTRA, tile % EXTRA
        spare = early[(EARLY + j) * T : (EARLY + j + 1) * T]
        return m, jnp.where(within, pltpu.roll(m, start2, 1), pltpu.roll(spare, turns[g], 1))

    def from_late(i):
        return late[i * T : (i + 1) * T], late[(LATE + i) * T : (LATE + i + 1) * T]

    for i in range(XA):
        p7, p6 = from_late(EDGE.index(i)) if i in EDGE else from_above(i - 2)
        x6, x7 = (a1[(z * XA + i) * T : (z * XA + i + 1) * T] for z in (6, 7))
        c2[(6 * XA + i) * T : (6 * XA + i + 1) * T] = fall(c0, cc2, x6, x7, p6)
        c2[(7 * XA + i) * T : (7 * XA + i + 1) * T] = jnp.where(c0, x7, p7)
    for i in range(2 * X // T):
        row7[i * T : (i + 1) * T], row6[i * T : (i + 1) * T] = from_above(X - 2 + i)
    p7, p6 = from_late(4)
    for i, row in enumerate((0, X - 1, X, 2 * X - 1)):
        row7[row : row + 1], row6[row : row + 1] = p7[i : i + 1], p6[i : i + 1]
    for i in range(2 * X // T):
        x6, x7 = (a1y[pl.ds(i * T * Z + z, T, stride=Z), :] for z in (6, 7))
        at = 6 * 2 * X + i * T
        c2y[at : at + T] = fall(c0, cc2, x6, x7, row6[i * T : (i + 1) * T])
        c2y[at + 2 * X : at + 2 * X + T] = jnp.where(c0, x7, row7[i * T : (i + 1) * T])
    mask = jnp.concatenate([south[HALO : HALO + X], north[HALO : HALO + X]] * 2, axis=0)
    at = slice(12 * X, 16 * X)
    c2y[at] = collide(c2y[at], mask, k, t)
    for z in (6, 7):
        at = slice(z * XA * T, (z + 1) * XA * T)
        c2[at] = collide(c2[at], m1[...], k, t)
        advect_second(z, range(X), c2, a2, c2y, u_ref, v_ref)
    for i in range(X):
        ends = (0, 1, X - 2, X - 1)
        tile = X - 2 + 2 * X // T + i - 2
        p7, p6 = from_late(5 + ends.index(i)) if i in ends else from_above(tile)
        x = [a2[(z * X + i) * T : (z * X + i + 1) * T] for z in range(4, 8)]
        for z, v in enumerate(
            (
                fall(c0, cc2, x[0], x[1], x[2]),
                fall(c0, cc2, x[1], x[2], x[3]),
                fall(c0, cc2, x[2], x[3], p6),
                jnp.where(c0, x[3], p7),
            )
        ):
            res[(z * X + i) * T : (z * X + i + 1) * T] = v
    copy = pltpu.make_async_copy(res, out.at[pl.ds(4 * X * T, 4 * X * T)], sem)
    copy.start()
    copy.wait()


def ring(axis, step):
    n = lax.axis_size(axis)
    return [(i, (i + step) % n) for i in range(n)]


def below(value):
    return lax.ppermute(value, "gz", [(i, i - 1) for i in range(1, lax.axis_size("gz"))])


def packed(n0, n2, drops, capture, transfer, courant_u, courant_v, fall_class, cloud_mask):
    drops = drops.reshape(Z * X * Y, B)
    sc = jnp.stack([n0, B - n2])
    ub = jnp.broadcast_to(courant_u[:, None], (Z, B))
    vb = jnp.broadcast_to(courant_v[:, None], (Z, B))
    v = lambda n, d=F32: ((n, B), d, True)
    weights = [((2 * B, 2 * B), BF16, True)] * 2
    own, m1, ym, yp, kk, tt = call(
        edges_body,
        [v(Z * X * Y), v(XA * Y), v(HALO + 2 * X), v(HALO + 2 * X)] + weights,
        [drops, cloud_mask.T, capture, transfer],
        [HBM] * 4,
        [pltpu.VMEM((Y, X), jnp.int32), pltpu.VMEM((B, B), F32), pltpu.VMEM((B, B), F32), pltpu.SemaphoreType.DMA((4,))],
        cost=(1000, 4 << 20),
    )
    south = lax.ppermute(yp, "gy", ring("gy", 1))
    north = lax.ppermute(ym, "gy", ring("gy", -1))
    (c1,) = call(own_body, [v(Z * XW * Y)], [own, m1, kk, tt], [VMEM] * 4, cost=(3 << 30, 8 << 20))
    shapes = [v(4 * XA * Z), v(Z * XA * T), v(2 * X * Z), v(Z * XA * T), v(Z * 2 * X), v(Z * X * T)]
    scalars = [sc, courant_u, courant_v]
    cy, a1, a1y, c2, c2y, a2, pay = call(
        early_body,
        shapes + [v((EARLY + EXTRA) * T)],
        scalars + [ub, vb, c1, south, north, kk, tt, m1],
        [SMEM] * 3 + [VMEM] * 8,
        cost=(1 << 30, 4 << 20),
    )
    early = below(pay)
    xm, xp = call(
        sides_body,
        [v(XMESSAGE)] * 2,
        [own, m1, south, north],
        [VMEM] * 4,
        cost=(1000, 1 << 18),
    )
    left = lax.ppermute(xp, "gx", ring("gx", 1))
    right = lax.ppermute(xm, "gx", ring("gx", -1))
    c1, cy, m1, a1, a1y, c2, c2y, a2, pay = call(
        late_body,
        [v(Z * XW * Y), shapes[0], v(XA * Y)] + shapes[1:] + [v(2 * LATE * T)],
        scalars + [ub, vb, left, right, kk, tt, south, north, c1, cy, m1, a1, a1y, c2, c2y, a2],
        [SMEM] * 3 + [VMEM] * 16,
        cost=(1 << 28, 1 << 20),
        aliases={11 + i: i for i in range(8)},
    )
    late = below(pay)
    *state, out = call(
        rest_body,
        shapes[1:] + [((Z * X * Y, B), F32, False)],
        scalars + [ub, vb, kk, tt, south, north, c1, m1, cy, a1, a1y, c2, c2y, a2],
        [SMEM] * 3 + [VMEM] * 14,
        [pltpu.VMEM((4 * X * T, B), F32), pltpu.SemaphoreType.DMA],
        cost=(3 << 30, 8 << 20),
        out_specs=[VMEM] * 5 + [HBM],
        aliases={12 + i: i for i in range(5)},
    )
    a1, a1y, c2, c2y, a2 = state
    out, *_ = call(
        last_body,
        [((Z * X * Y, B), F32, False), shapes[3], shapes[4], shapes[5]],
        scalars + [kk, tt, south, north, m1, a1, a1y, c2, c2y, a2, early, late, out],
        [SMEM] * 3 + [VMEM] * 12 + [HBM],
        [pltpu.VMEM((2 * X, B), F32), pltpu.VMEM((2 * X, B), F32), pltpu.VMEM((4 * X * T, B), F32), pltpu.SemaphoreType.DMA],
        cost=(1 << 30, 8 << 20),
        out_specs=[HBM] + [VMEM] * 3,
        aliases={15: 0, 10: 1, 11: 2, 12: 3},
    )
    return out.reshape(Z, X, Y, B)


def passed_along(block, axis, distance):
    devices = range(lax.axis_size(axis))
    route = [(i - distance, i) for i in devices if i - distance in devices]
    return lax.ppermute(block, axis, route)


def with_halo(value, sides, width):
    edges = {}
    for axis, dim in sides:
        devices, length = (lax.axis_size(axis), value.shape[dim])
        up = [(i, (i + 1) % devices) for i in range(devices)]
        last = lax.slice_in_dim(value, length - width, length, axis=dim)
        leading = lax.slice_in_dim(value, 0, width, axis=dim)
        edges[dim] = (
            lax.ppermute(last, axis, up),
            lax.ppermute(leading, axis, [(b, a) for a, b in up]),
        )
    done = []
    for _, dim in sides:
        low, high = edges[dim]
        around = [(width, width) if d in done else (0, 0) for d in range(value.ndim)]
        value = jnp.concatenate([jnp.pad(low, around), value, jnp.pad(high, around)], axis=dim)
        done.append(dim)
    return value


def collide_plain(particle_distribution, capture_efficiency_matrix, transfer, cloudy):
    merger_speed = jnp.einsum(
        "ugcr,mr->ugcm",
        particle_distribution,
        capture_efficiency_matrix,
        precision=lax.Precision.HIGHEST,
    )
    water_removed = particle_distribution * merger_speed
    mass_gain = jnp.einsum(
        "zxyi,ik->zxyk", water_removed, transfer, precision=lax.Precision.HIGHEST
    )
    return particle_distribution + cloudy[None, :, :, None] * (mass_gain - water_removed)


def advect_plain(with_edges, courant_u, courant_v):
    centre = with_edges[:, 1:-1, 1:-1]
    west_side = with_edges[:, :-2, 1:-1]
    east_side = with_edges[:, 2:, 1:-1]
    south_side = with_edges[:, 1:-1, :-2]
    north_side = with_edges[:, 1:-1, 2:]
    x_plus = jnp.maximum(courant_u, 0.0)[:, None, None, None]
    x_minus = jnp.minimum(courant_u, 0.0)[:, None, None, None]
    northward_neighbor = jnp.maximum(courant_v, 0.0)[:, None, None, None]
    y_minus = jnp.minimum(courant_v, 0.0)[:, None, None, None]
    result = centre - x_plus * (centre - west_side) - x_minus * (east_side - centre)
    return result - northward_neighbor * (centre - south_side) - y_minus * (north_side - centre)


def sediment(padded, fall_class, levels):
    result = padded[:levels]
    for fall_depth in range(1, H_MAX + 1):
        result = jnp.where(
            (fall_class == fall_depth)[None, None, None, :],
            padded[fall_depth : fall_depth + levels],
            result,
        )
    return result


def plain(
    drops, capture_efficiency_matrix, transfer, courant_u, courant_v, fall_class, cloud_mask
):
    cloudy = cloud_mask.astype(jnp.float32)
    reach = STEPS * H_MAX
    from_above, upper_u, upper_v = passed_along(
        (drops[:reach], courant_u[:reach], courant_v[:reach]), "gz", -1
    )
    particle_distribution = jnp.concatenate([drops, from_above], axis=0)
    column_u = jnp.concatenate([courant_u, upper_u], axis=0)
    column_v = jnp.concatenate([courant_v, upper_v], axis=0)
    for repeat in range(STEPS):
        current = particle_distribution.shape[0]
        coalesced_drops = collide_plain(
            particle_distribution, capture_efficiency_matrix, transfer, cloudy
        )
        with_edges = with_halo(coalesced_drops, (("gx", 1), ("gy", 2)), 1)
        advected = advect_plain(with_edges, column_u[:current], column_v[:current])
        particle_distribution = sediment(advected, fall_class, current - H_MAX)
    return particle_distribution


def on_device(*args):
    fall_class = args[5]
    n0 = jnp.sum((fall_class == 0).astype(jnp.int32))
    n2 = jnp.sum((fall_class == H_MAX).astype(jnp.int32))
    return lax.cond(
        n2 - n0 <= SPARE, lambda a: packed(*a), lambda a: plain(*a[2:]), (n0, n2, *args)
    )


def solution(mesh):
    in_specs = (P("gz", "gx", "gy", None), P(), P(), P("gz"), P("gz"), P(), P("gx", "gy"))
    out_specs = P("gz", "gx", "gy", None)
    return jax.shard_map(
        on_device, mesh=mesh, in_specs=in_specs, out_specs=out_specs, check_vma=False
    )
```

```python
import functools

import jax
import jax.numpy as jnp
from jax import lax
from jax.experimental import pallas as pl
from jax.experimental.pallas import tpu as pltpu
from jax.sharding import PartitionSpec as P

H_MAX = 2
STEPS = 2
Z, X, Y, B = 8, 64, 8, 128
T = 8
XW = X + 4
XA = X + 2
LOW = Z // 2
HALF = 2 * LOW * X
ENDS = HALF + 2 * X
XROWS = 2 * Z * Y
EARLY = (X - 2) + 2 * X // T + (X - 4)
GROUPS = 4
SPARE = B // GROUPS
EXTRA = -(-EARLY // GROUPS)
LATE = 4 + 1 + 4
F32, BF16 = jnp.float32, jnp.bfloat16

VMEM = pl.BlockSpec(memory_space=pltpu.VMEM)
SMEM = pl.BlockSpec(memory_space=pltpu.SMEM)
HBM = pl.BlockSpec(memory_space=pltpu.HBM)


def rows(start, n=T):
    return pl.ds(start if isinstance(start, int) else pl.multiple_of(start, T), n)


def call(body, outs, args, specs, scratch=(), cost=(0, 0), out_specs=None, aliases=None, keep=()):
    shapes = [
        pltpu.VMEM(s, d) if m is True else m(s, d) if m else jax.ShapeDtypeStruct(s, d)
        for s, d, m in outs
    ]
    shapes += [pltpu.VMEM(args[i].shape, args[i].dtype) for i in keep]
    n_in, n_out = len(args), len(outs)
    aliases = {**(aliases or {}), **{i: n_out + k for k, i in enumerate(keep)}}

    def kernel(*refs):
        body(*refs[: n_in + n_out], *refs[n_in + n_out + len(keep) :])

    args = [
        pltpu.with_memory_space_constraint(a, s.memory_space)
        for a, s in zip(args, specs)
    ]
    return pl.pallas_call(
        kernel,
        out_shape=shapes,
        in_specs=list(specs),
        out_specs=(out_specs or [VMEM] * len(outs)) + [VMEM] * len(keep),
        scratch_shapes=list(scratch),
        input_output_aliases=aliases,
        cost_estimate=pl.CostEstimate(flops=cost[0], bytes_accessed=cost[1], transcendentals=0),
        compiler_params=pltpu.CompilerParams(vmem_limit_bytes=8 << 20),
    )(*args)


def split(x):
    high = x.astype(BF16)
    return high, (x - high.astype(F32)).astype(BF16)


def product(x, weights):
    out = jnp.dot(jnp.concatenate(split(x), axis=1), weights, preferred_element_type=F32)
    return out[:, :B] + out[:, B:]


def collide(s, cloudy, capture, transfer):
    loss = s * product(s, capture)
    return s + cloudy * (product(loss, transfer) - loss)


def eightfold(ref, row):
    return ref[pl.ds(row, T, stride=0), :]


def repeated(ref, start, n):
    return jnp.concatenate([eightfold(ref, start + i) for i in range(n)], axis=0)


def classes(sc_ref):
    lane = lax.broadcasted_iota(jnp.int32, (T, B), 1)
    return lane < sc_ref[0], lane >= sc_ref[1]


def fall(c0, c2, a, b, c):
    return jnp.where(c0, a, jnp.where(c2, c, b))


def count_body(falls, u_in, v_in, out, u, v, ref, sem):
    copies = [
        pltpu.make_async_copy(a, b, sem.at[i])
        for i, (a, b) in enumerate(((falls, ref), (u_in, u), (v_in, v)))
    ]
    for copy in copies:
        copy.start()
    for copy in copies:
        copy.wait()
    n0 = jnp.sum((ref[...] == 0).astype(jnp.int32))
    n2 = jnp.sum((ref[...] == H_MAX).astype(jnp.int32))
    out[0] = n0
    out[1] = B - n2
    out[2] = (n2 - n0 <= SPARE).astype(jnp.int32)


def edges_body(drops, cloud, k_in, t_in, own, m1, ym0, ym1, yp0, yp1, kk, tt, mask, k_ref, t_ref, sem):
    level = lambda z: pl.ds(z * X * Y, X * Y)
    copies = [
        pltpu.make_async_copy(a, b, sem.at[i])
        for i, (a, b) in enumerate(
            [(drops.at[level(z)], own.at[level(z)]) for z in range(Z)]
            + [(cloud, mask), (k_in, k_ref), (t_in, t_ref)]
        )
    ]
    for copy in copies[Z:] + copies[:Z]:
        copy.start()
    copies[Z].wait()
    columns = mask[...].astype(F32)
    for x in range(X):
        m1[(x + 1) * Y : (x + 2) * Y] = jnp.broadcast_to(columns[:, x : x + 1], (Y, B))
    for i, (ref, out, turned) in enumerate(((k_ref, kk, True), (t_ref, tt, False))):
        copies[Z + 1 + i].wait()
        w = ref[...].T if turned else ref[...]
        high, low = split(w)
        half = jnp.concatenate([high, low], axis=1)
        out[...] = jnp.concatenate([half, half], axis=0)
    for out, ys in ((ym0, (0, 1)), (yp0, (Y - 1, Y - 2))):
        for d, y in enumerate(ys):
            out[HALF + d * X : HALF + (d + 1) * X] = m1[pl.ds(Y + y, X, stride=Y), :]
    for z in range(Z):
        copies[z].wait()
        for outs, ys in (((ym0, ym1), (0, 1)), ((yp0, yp1), (Y - 1, Y - 2))):
            for d, y in enumerate(ys):
                at = (d * LOW + z % LOW) * X
                outs[z // LOW][at : at + X] = own[pl.ds(z * X * Y + y, X, stride=Y), :]
    for out, y in ((ym0, 0), (yp0, Y - 1)):
        for i, x in enumerate((0, X - 1)):
            at, start = ENDS + i * LOW, (LOW * X + x) * Y + y
            out[at : at + LOW] = own[pl.ds(start, LOW, stride=X * Y), :]


def sides_body(own, m1, south, north, xm, xp):
    for out, cols in ((xm, (0, 1)), (xp, (X - 1, X - 2))):
        for d, x in enumerate(cols):
            out[XROWS + d * Y : XROWS + (d + 1) * Y] = m1[(x + 1) * Y : (x + 2) * Y]
            for z in range(Z):
                at = (z * X + x) * Y
                out[(d * Z + z) * Y : (d * Z + z + 1) * Y] = own[at : at + Y]
        x = cols[0]
        at = XROWS + 2 * Y
        out[at + 2 * Z :] = jnp.zeros((T, B), F32)
        for side, ref in enumerate((south, north)):
            row = at + side * Z
            end = ENDS + (LOW if x else 0)
            out[row : row + LOW] = ref[pl.ds(x, LOW, stride=X), :]
            out[row + LOW : row + Z] = ref[end : end + LOW]
            row = at + 2 * Z + side
            out[row : row + 1] = ref[HALF + x : HALF + x + 1]


XMESSAGE = XROWS + 2 * Y + 2 * Z + T


def own_body(own, m1, kk, tt, c1):
    k, t, mask = kk[...], tt[...], m1[Y : Y + X * Y]

    def level(z, _):
        c1[rows((z * XW + 2) * Y, X * Y)] = collide(own[rows(z * X * Y, X * Y)], mask, k, t)
        return 0

    lax.fori_loop(0, Z, level, 0, unroll=4)


def cy_at(side, d, x):
    return ((side * 2 + d) * XA + x + 1) * Z


def collide_rows(part, south, north, masks, cy, k, t):
    for side, (ref, mask_ref) in enumerate(zip((south, north), masks)):
        for d in range(2):
            mask = jnp.concatenate([mask_ref[HALF + d * X : HALF + (d + 1) * X]] * LOW, axis=0)
            c = collide(ref[d * LOW * X : (d + 1) * LOW * X], mask, k, t)
            for z in range(LOW):
                cy[pl.ds(cy_at(side, d, 0) + part * LOW + z, X, stride=Z), :] = c[z * X : (z + 1) * X]


def upwind(z, u_ref, v_ref):
    u, v = u_ref[z], v_ref[z]
    at_edge = lax.broadcasted_iota(jnp.int32, (T, B), 0) == jnp.where(v > 0, 0, T - 1)
    return (
        jnp.abs(u),
        jnp.abs(v),
        jnp.where(u > 0, -Y, Y),
        jnp.where(v > 0, 1, T - 1),
        jnp.where(v > 0, 0, 1),
        at_edge,
    )


def advect(z, columns, c_ref, width, first, out_ref, out_width, edge, u_ref, v_ref):
    au, av, step, shift, side, at_edge = upwind(z, u_ref, v_ref)
    base, base_out = (z * width + first) * Y, z * out_width * Y
    edge_ref, edge_at, edge_stride = edge(z, side)
    for i in columns:
        c = c_ref[rows(base + i * Y)]
        x = c_ref[rows(base + step + i * Y)]
        e = eightfold(edge_ref, edge_at + i * edge_stride)
        y = jnp.where(at_edge, e, pltpu.roll(c, shift, 0))
        out_ref[rows(base_out + i * Y)] = c - au * (c - x) - av * (c - y)


def advect_first(z, columns, c1, a1, cy, u_ref, v_ref):
    edge = lambda z, side: (cy, side * (2 * XA * Z) + z, Z)
    advect(z, columns, c1, XW, 1, a1, XA, edge, u_ref, v_ref)


def advect_second(z, columns, c2, a2, c2y, u_ref, v_ref):
    edge = lambda z, side: (c2y, (z * 2 + side) * X, 1)
    advect(z, columns, c2, XA, 1, a2, X, edge, u_ref, v_ref)


def advect_rows(columns, ub, vb, c1, cy, a1y):
    au, av = jnp.abs(ub[...]), jnp.abs(vb[...])
    upos, vpos = ub[...] > 0, vb[...] > 0
    for side in range(2):
        for x in columns:
            at, far = cy_at(side, 0, x), cy_at(side, 1, x)
            c = cy[at : at + Z]
            xx = jnp.where(upos, cy[at - Z : at], cy[at + Z : at + 2 * Z])
            outer = cy[far : far + Z]
            inner = c1[pl.ds((x + 2) * Y + (Y - 1) * side, Z, stride=XW * Y), :]
            yy = jnp.where(vpos, *((outer, inner) if side == 0 else (inner, outer)))
            to = (side * X + x) * Z
            a1y[to : to + Z] = c - au * (c - xx) - av * (c - yy)


def settle(z, columns, c0, cc2, a1, c2):
    for i in columns:
        at = (z * XA + i) * T
        step = XA * T
        c2[rows(at)] = fall(c0, cc2, a1[rows(at)], a1[rows(at + step)], a1[rows(at + 2 * step)])


def settle_level(z, c0, cc2, a1, m1, c2, k, t):
    settle(z, range(XA), c0, cc2, a1, c2)
    at = rows(z * XA * T, XA * T)
    c2[at] = collide(c2[at], m1[...], k, t)


def settle_rows(z, c0, cc2, a1y, masks, c2y, k, t):
    for i in range(2 * X // T):
        a = [a1y[pl.ds(i * T * Z + z + j, T, stride=Z), :] for j in range(H_MAX + 1)]
        to = z * 2 * X + i * T
        c2y[to : to + T] = fall(c0, cc2, *a)
    at = slice(z * 2 * X, (z + 1) * 2 * X)
    mask = jnp.concatenate([m[HALF : HALF + X] for m in masks], axis=0)
    c2y[at] = collide(c2y[at], mask, k, t)


def falling(a1, a1y, a2, tile):
    if tile < X - 2:
        at = (tile + 2) * T
        return lambda z: a1[z * XA * T + at : z * XA * T + at + T]
    tile -= X - 2
    if tile < 2 * X // T:
        return lambda z: a1y[pl.ds(tile * T * Z + z, T, stride=Z), :]
    at = (tile - 2 * X // T + 2) * T
    return lambda z: a2[z * X * T + at : z * X * T + at + T]


def early_body(
    sc, u_ref, v_ref, ub, vb, c1, south, north, kk, tt, m1, cy, a1, a1y, c2, c2y, a2, pay
):
    k, t = kk[...], tt[...]
    c0, cc2 = classes(sc)
    collide_rows(0, south, north, (south, north), cy, k, t)

    def first(z, _):
        advect_first(z, range(2, X), c1, a1, cy, u_ref, v_ref)
        return 0

    lax.fori_loop(0, 4, first, 0)
    advect_rows(range(1, X - 1), ub, vb, c1, cy, a1y)

    def second(z, _):
        settle_level(z, c0, cc2, a1, m1, c2, k, t)
        return 0

    lax.fori_loop(0, 2, second, 0, unroll=2)
    for z in range(2):
        settle_rows(z, c0, cc2, a1y, (south, north), c2y, k, t)

    def third(z, _):
        advect_second(z, range(2, X - 2), c2, a2, c2y, u_ref, v_ref)
        return 0

    lax.fori_loop(0, 2, third, 0)
    n0 = sc[0]
    n2 = B - sc[1]
    for tile in range(EARLY):
        level = falling(a1, a1y, a2, tile)
        l0 = level(0)
        packed = fall(c0, cc2, pltpu.roll(l0, n2, 1), l0, level(1))
        pay[tile * T : (tile + 1) * T] = packed
    group = lax.broadcasted_iota(jnp.int32, (T, B), 1) // SPARE
    for j in range(EXTRA):
        out = jnp.zeros((T, B), F32)
        for g in range(GROUPS):
            if j + g * EXTRA < EARLY:
                l0 = falling(a1, a1y, a2, j + g * EXTRA)(0)
                turn = (n2 - n0 + g * SPARE + B) & (B - 1)
                out = jnp.where(group == g, pltpu.roll(l0, turn, 1), out)
        pay[(EARLY + j) * T : (EARLY + j + 1) * T] = out


EDGE = (0, 1, XA - 2, XA - 1)


def late_body(
    sc, u_ref, v_ref, ub, vb, left, right, kk, tt, south, north,
    c1_in, cy_in, m1_in, a1_in, a1y_in, c2_in, c2y_in, a2_in,
    c1, cy, m1, a1, a1y, c2, c2y, a2, pay,
):
    k, t = kk[...], tt[...]
    c0, cc2 = classes(sc)
    m1[0:Y] = left[XROWS : XROWS + Y]
    m1[Y + X * Y :] = right[XROWS : XROWS + Y]
    at_mask = XROWS + 2 * Y
    pieces, masks = [], []
    for ref in (left, right):
        pieces += [ref[0:XROWS], ref[at_mask : at_mask + 2 * Z]]
        masks += [ref[XROWS + d * Y : XROWS + (d + 1) * Y] for d in range(2) for _ in range(Z)]
        masks += [eightfold(ref, at_mask + 2 * Z + side) for side in range(2)]
    c = collide(jnp.concatenate(pieces, axis=0), jnp.concatenate(masks, axis=0), k, t)
    size = XROWS + 2 * Z
    for i, (columns, x) in enumerate((((1, 0), -1), ((XW - 2, XW - 1), X))):
        for d in range(2):
            for z in range(Z):
                at, to = i * size + (d * Z + z) * Y, (z * XW + columns[d]) * Y
                c1[to : to + Y] = c[at : at + Y]
        for side in range(2):
            at, to = i * size + XROWS + side * Z, cy_at(side, 0, x)
            cy[to : to + Z] = c[at : at + Z]

    for z in range(4):
        advect_first(z, EDGE, c1, a1, cy, u_ref, v_ref)
    advect_rows((0, X - 1), ub, vb, c1, cy, a1y)
    for z in range(2):
        settle(z, EDGE, c0, cc2, a1, c2)
    tiles = [(z * XA + i) * T for z in range(2) for i in EDGE]
    c = collide(
        jnp.concatenate([c2[at : at + T] for at in tiles], axis=0),
        jnp.concatenate([m1[i * T : (i + 1) * T] for i in EDGE] * 2, axis=0),
        k,
        t,
    )
    for i, at in enumerate(tiles):
        c2[at : at + T] = c[i * T : (i + 1) * T]
    for z in range(2):
        settle_rows(z, c0, cc2, a1y, (south, north), c2y, k, t)
        advect_second(z, (0, 1, X - 2, X - 1), c2, a2, c2y, u_ref, v_ref)
    for i, x in enumerate(EDGE):
        l0, l1 = (a1[(z * XA + x) * T : (z * XA + x + 1) * T] for z in range(2))
        pay[i * T : (i + 1) * T] = fall(c0, cc2, l0, l0, l1)
        pay[(LATE + i) * T : (LATE + i + 1) * T] = l0
    at = 4 * T
    for i, row in enumerate((0, X - 1, X, 2 * X - 1)):
        l0, l1 = (a1y[row * Z + z : row * Z + z + 1] for z in range(2))
        pay[at + i : at + i + 1] = fall(c0[0:1], cc2[0:1], l0, l0, l1)
        pay[at + LATE * T + i : at + LATE * T + i + 1] = l0
    for first in (at + 4, at + LATE * T + 4):
        pay[first : first + 4] = jnp.zeros((4, B), F32)
    for i, x in enumerate((0, 1, X - 2, X - 1)):
        l0, l1 = (a2[(z * X + x) * T : (z * X + x + 1) * T] for z in range(2))
        to = at + (i + 1) * T
        pay[to : to + T] = fall(c0, cc2, l0, l0, l1)
        pay[to + LATE * T : to + LATE * T + T] = l0


def rest_body(
    sc, u_ref, v_ref, ub, vb, kk, tt, south0, south1, north0, north1, c1, m1,
    cy_in, a1_in, a1y_in, c2_in, c2y_in, a2_in,
    cy, a1, a1y, c2, c2y, a2, out, res, sem,
):
    k, t = kk[...], tt[...]
    c0, cc2 = classes(sc)
    collide_rows(1, south1, north1, (south0, north0), cy, k, t)

    def first(z, _):
        advect_first(z, range(XA), c1, a1, cy, u_ref, v_ref)
        return 0

    lax.fori_loop(4, 8, first, 0)
    advect_rows(range(X), ub, vb, c1, cy, a1y)

    def second(z, _):
        settle_level(z, c0, cc2, a1, m1, c2, k, t)
        return 0

    lax.fori_loop(2, 6, second, 0, unroll=4)
    for z in range(2, 6):
        settle_rows(z, c0, cc2, a1y, (south0, north0), c2y, k, t)

    def third(z, _):
        advect_second(z, range(X), c2, a2, c2y, u_ref, v_ref)
        return 0

    lax.fori_loop(2, 6, third, 0)

    copies = []
    for z in range(4):
        for i in range(X):
            at, step = (z * X + i) * T, X * T
            res[at : at + T] = fall(
                c0, cc2, *(a2[at + k * step : at + k * step + T] for k in range(H_MAX + 1))
            )
        level = pl.ds(z * X * T, X * T)
        copies.append(pltpu.make_async_copy(res.at[level], out.at[level], sem.at[z]))
        copies[-1].start()
    for copy in copies:
        copy.wait()


def last_body(
    sc, u_ref, v_ref, kk, tt, south, north, m1, a1, a1y, c2_in, c2y_in, a2_in, early, late, out_in,
    out, c2, c2y, a2, row7, row6, res, sem,
):
    k, t = kk[...], tt[...]
    c0, cc2 = classes(sc)
    n0, start2 = sc[0], sc[1]
    lane = lax.broadcasted_iota(jnp.int32, (T, B), 1)
    within = lane < start2 + n0
    turns = [(n0 + start2 - g * SPARE + B) & (B - 1) for g in range(GROUPS)]

    def from_above(tile):
        m = early[tile * T : (tile + 1) * T]
        g, j = tile // EXTRA, tile % EXTRA
        spare = early[(EARLY + j) * T : (EARLY + j + 1) * T]
        return m, jnp.where(within, pltpu.roll(m, start2, 1), pltpu.roll(spare, turns[g], 1))

    def from_late(i):
        return late[i * T : (i + 1) * T], late[(LATE + i) * T : (LATE + i + 1) * T]

    for i in range(XA):
        p7, p6 = from_late(EDGE.index(i)) if i in EDGE else from_above(i - 2)
        x6, x7 = (a1[(z * XA + i) * T : (z * XA + i + 1) * T] for z in (6, 7))
        c2[(6 * XA + i) * T : (6 * XA + i + 1) * T] = fall(c0, cc2, x6, x7, p6)
        c2[(7 * XA + i) * T : (7 * XA + i + 1) * T] = jnp.where(c0, x7, p7)
    for i in range(2 * X // T):
        row7[i * T : (i + 1) * T], row6[i * T : (i + 1) * T] = from_above(X - 2 + i)
    p7, p6 = from_late(4)
    for i, row in enumerate((0, X - 1, X, 2 * X - 1)):
        row7[row : row + 1], row6[row : row + 1] = p7[i : i + 1], p6[i : i + 1]
    for i in range(2 * X // T):
        x6, x7 = (a1y[pl.ds(i * T * Z + z, T, stride=Z), :] for z in (6, 7))
        at = 6 * 2 * X + i * T
        c2y[at : at + T] = fall(c0, cc2, x6, x7, row6[i * T : (i + 1) * T])
        c2y[at + 2 * X : at + 2 * X + T] = jnp.where(c0, x7, row7[i * T : (i + 1) * T])
    mask = jnp.concatenate([south[HALF : HALF + X], north[HALF : HALF + X]] * 2, axis=0)
    at = slice(12 * X, 16 * X)
    c2y[at] = collide(c2y[at], mask, k, t)
    for z in (6, 7):
        at = slice(z * XA * T, (z + 1) * XA * T)
        c2[at] = collide(c2[at], m1[...], k, t)
        advect_second(z, range(X), c2, a2, c2y, u_ref, v_ref)
    ends = (0, 1, X - 2, X - 1)
    copies = []
    for z in range(4, 8):
        for i in range(X):
            x = [a2[(k * X + i) * T : (k * X + i + 1) * T] for k in range(z, min(z + 3, Z))]
            if z > 5:
                tile = X - 2 + 2 * X // T + i - 2
                p7, p6 = from_late(5 + ends.index(i)) if i in ends else from_above(tile)
                x = x + [p6] if z == 6 else x + [p7, p7]
            res[((z - 4) * X + i) * T : ((z - 4) * X + i + 1) * T] = fall(c0, cc2, *x)
        to = pl.ds(z * X * T, X * T)
        copies.append(
            pltpu.make_async_copy(res.at[pl.ds((z - 4) * X * T, X * T)], out.at[to], sem.at[z - 4])
        )
        copies[-1].start()
    for copy in copies:
        copy.wait()


def ring(axis, step):
    n = lax.axis_size(axis)
    return [(i, (i + step) % n) for i in range(n)]


def below(value):
    return lax.ppermute(value, "gz", [(i, i - 1) for i in range(1, lax.axis_size("gz"))])


def packed(scalars, drops, capture, transfer, courant_u, courant_v, fall_class, cloud_mask):
    drops = drops.reshape(Z * X * Y, B)
    ub = jnp.broadcast_to(courant_u[:, None], (Z, B))
    vb = jnp.broadcast_to(courant_v[:, None], (Z, B))
    v = lambda n, d=F32: ((n, B), d, True)
    weights = [((2 * B, 2 * B), BF16, True)] * 2
    own, m1, ym0, ym1, yp0, yp1, kk, tt = call(
        edges_body,
        [v(Z * X * Y), v(XA * Y), v(ENDS + T), v(HALF), v(ENDS + T), v(HALF)] + weights,
        [drops, cloud_mask.T, capture, transfer],
        [HBM] * 4,
        [pltpu.VMEM((Y, X), jnp.int32), pltpu.VMEM((B, B), F32), pltpu.VMEM((B, B), F32), pltpu.SemaphoreType.DMA((Z + 3,))],
        cost=(1000, 4 << 20),
    )
    south0 = lax.ppermute(yp0, "gy", ring("gy", 1))
    north0 = lax.ppermute(ym0, "gy", ring("gy", -1))
    south1 = lax.ppermute(yp1, "gy", ring("gy", 1))
    north1 = lax.ppermute(ym1, "gy", ring("gy", -1))
    c1, kk, tt = call(
        own_body, [v(Z * XW * Y)], [own, m1, kk, tt], [VMEM] * 4, cost=(3 << 30, 8 << 20), keep=(2, 3)
    )
    shapes = [v(4 * XA * Z), v(Z * XA * T), v(2 * X * Z), v(Z * XA * T), v(Z * 2 * X), v(Z * X * T)]
    cy, a1, a1y, c2, c2y, a2, pay, kk, tt = call(
        early_body,
        shapes + [v((EARLY + EXTRA) * T)],
        [*scalars, ub, vb, c1, south0, north0, kk, tt, m1],
        [SMEM] * 3 + [VMEM] * 8,
        cost=(3 << 30, 8 << 20),
        keep=(8, 9),
    )
    pay, south1, north1 = lax.optimization_barrier((pay, south1, north1))
    early = below(pay)
    xm, xp = call(
        sides_body,
        [v(XMESSAGE)] * 2,
        [own, m1, south0, north0],
        [VMEM] * 4,
        cost=(1000, 1 << 18),
    )
    left = lax.ppermute(xp, "gx", ring("gx", 1))
    right = lax.ppermute(xm, "gx", ring("gx", -1))
    c1, cy, m1, a1, a1y, c2, c2y, a2, pay, kk, tt = call(
        late_body,
        [v(Z * XW * Y), shapes[0], v(XA * Y)] + shapes[1:] + [v(2 * LATE * T)],
        [*scalars, ub, vb, left, right, kk, tt, south0, north0, c1, cy, m1, a1, a1y, c2, c2y, a2],
        [SMEM] * 3 + [VMEM] * 16,
        cost=(1 << 28, 1 << 20),
        aliases={11 + i: i for i in range(8)},
        keep=(7, 8),
    )
    late = below(pay)
    *state, out, kk, tt = call(
        rest_body,
        shapes + [((Z * X * Y, B), F32, False)],
        [*scalars, ub, vb, kk, tt, south0, south1, north0, north1, c1, m1, cy, a1, a1y, c2, c2y, a2],
        [SMEM] * 3 + [VMEM] * 16,
        [pltpu.VMEM((4 * X * T, B), F32), pltpu.SemaphoreType.DMA((4,))],
        cost=(3 << 30, 8 << 20),
        out_specs=[VMEM] * 6 + [HBM],
        aliases={13 + i: i for i in range(6)},
        keep=(5, 6),
    )
    (cy, a1, a1y, c2, c2y, a2) = state
    out, *_ = call(
        last_body,
        [((Z * X * Y, B), F32, False), shapes[3], shapes[4], shapes[5]],
        [*scalars, kk, tt, south0, north0, m1, a1, a1y, c2, c2y, a2, early, late, out],
        [SMEM] * 3 + [VMEM] * 12 + [HBM],
        [pltpu.VMEM((2 * X, B), F32), pltpu.VMEM((2 * X, B), F32), pltpu.VMEM((4 * X * T, B), F32), pltpu.SemaphoreType.DMA((4,))],
        cost=(1 << 30, 8 << 20),
        out_specs=[HBM] + [VMEM] * 3,
        aliases={15: 0, 10: 1, 11: 2, 12: 3},
    )
    return out.reshape(Z, X, Y, B)


def passed_along(block, axis, distance):
    devices = range(lax.axis_size(axis))
    route = [(i - distance, i) for i in devices if i - distance in devices]
    return lax.ppermute(block, axis, route)


def with_halo(value, sides, width):
    edges = {}
    for axis, dim in sides:
        devices, length = (lax.axis_size(axis), value.shape[dim])
        up = [(i, (i + 1) % devices) for i in range(devices)]
        last = lax.slice_in_dim(value, length - width, length, axis=dim)
        leading = lax.slice_in_dim(value, 0, width, axis=dim)
        edges[dim] = (
            lax.ppermute(last, axis, up),
            lax.ppermute(leading, axis, [(b, a) for a, b in up]),
        )
    done = []
    for _, dim in sides:
        low, high = edges[dim]
        around = [(width, width) if d in done else (0, 0) for d in range(value.ndim)]
        value = jnp.concatenate([jnp.pad(low, around), value, jnp.pad(high, around)], axis=dim)
        done.append(dim)
    return value


def collide_plain(particle_distribution, capture_efficiency_matrix, transfer, cloudy):
    merger_speed = jnp.einsum(
        "ugcr,mr->ugcm",
        particle_distribution,
        capture_efficiency_matrix,
        precision=lax.Precision.HIGHEST,
    )
    water_removed = particle_distribution * merger_speed
    mass_gain = jnp.einsum(
        "zxyi,ik->zxyk", water_removed, transfer, precision=lax.Precision.HIGHEST
    )
    return particle_distribution + cloudy[None, :, :, None] * (mass_gain - water_removed)


def advect_plain(with_edges, courant_u, courant_v):
    centre = with_edges[:, 1:-1, 1:-1]
    west_side = with_edges[:, :-2, 1:-1]
    east_side = with_edges[:, 2:, 1:-1]
    south_side = with_edges[:, 1:-1, :-2]
    north_side = with_edges[:, 1:-1, 2:]
    x_plus = jnp.maximum(courant_u, 0.0)[:, None, None, None]
    x_minus = jnp.minimum(courant_u, 0.0)[:, None, None, None]
    northward_neighbor = jnp.maximum(courant_v, 0.0)[:, None, None, None]
    y_minus = jnp.minimum(courant_v, 0.0)[:, None, None, None]
    result = centre - x_plus * (centre - west_side) - x_minus * (east_side - centre)
    return result - northward_neighbor * (centre - south_side) - y_minus * (north_side - centre)


def sediment(padded, fall_class, levels):
    result = padded[:levels]
    for fall_depth in range(1, H_MAX + 1):
        result = jnp.where(
            (fall_class == fall_depth)[None, None, None, :],
            padded[fall_depth : fall_depth + levels],
            result,
        )
    return result


def plain(
    drops, capture_efficiency_matrix, transfer, courant_u, courant_v, fall_class, cloud_mask
):
    cloudy = cloud_mask.astype(jnp.float32)
    reach = STEPS * H_MAX
    from_above, upper_u, upper_v = passed_along(
        (drops[:reach], courant_u[:reach], courant_v[:reach]), "gz", -1
    )
    particle_distribution = jnp.concatenate([drops, from_above], axis=0)
    column_u = jnp.concatenate([courant_u, upper_u], axis=0)
    column_v = jnp.concatenate([courant_v, upper_v], axis=0)
    for repeat in range(STEPS):
        current = particle_distribution.shape[0]
        coalesced_drops = collide_plain(
            particle_distribution, capture_efficiency_matrix, transfer, cloudy
        )
        with_edges = with_halo(coalesced_drops, (("gx", 1), ("gy", 2)), 1)
        advected = advect_plain(with_edges, column_u[:current], column_v[:current])
        particle_distribution = sediment(advected, fall_class, current - H_MAX)
    return particle_distribution


def on_device(*args):
    scalars = call(
        count_body,
        [((3,), jnp.int32, pltpu.SMEM)] + [((Z,), F32, pltpu.SMEM)] * 2,
        [args[5].reshape(1, B), args[3], args[4]],
        [HBM] * 3,
        [pltpu.VMEM((1, B), jnp.int32), pltpu.SemaphoreType.DMA((3,))],
        out_specs=[SMEM] * 3,
    )
    return lax.cond(
        scalars[0][2] > 0, lambda a: packed(*a), lambda a: plain(*a[1:]), (scalars, *args)
    )


def solution(mesh):
    in_specs = (P("gz", "gx", "gy", None), P(), P(), P("gz"), P("gz"), P(), P("gx", "gy"))
    out_specs = P("gz", "gx", "gy", None)
    return jax.shard_map(
        on_device, mesh=mesh, in_specs=in_specs, out_specs=out_specs, check_vma=False
    )
```

```python
import functools

import jax
import jax.numpy as jnp
from jax import lax
from jax.experimental import pallas as pl
from jax.experimental.pallas import tpu as pltpu
from jax.sharding import PartitionSpec as P

H_MAX = 2
STEPS = 2
Z, X, Y, B = 8, 64, 8, 128
T = 8
XW = X + 4
XA = X + 2
LOW = Z // 2
HALF = 2 * LOW * X
ENDS = HALF + 2 * X
XROWS = 2 * Z * Y
EARLY = (X - 2) + 2 * X // T + (X - 4)
GROUPS = 4
SPARE = B // GROUPS
EXTRA = -(-EARLY // GROUPS)
LATE = 4 + 1 + 4
EDGE = (0, 1, XA - 2, XA - 1)
ENDING = (0, 1, X - 2, X - 1)
ROW_TILES = range(2 * X // T)
ROW_EDGES = (0, X // T - 1, X // T, 2 * X // T - 1)
F32, BF16 = jnp.float32, jnp.bfloat16

VMEM = pl.BlockSpec(memory_space=pltpu.VMEM)
SMEM = pl.BlockSpec(memory_space=pltpu.SMEM)
HBM = pl.BlockSpec(memory_space=pltpu.HBM)


def rows(start, n=T):
    return pl.ds(start if isinstance(start, int) else pl.multiple_of(start, T), n)


def call(body, outs, args, specs, scratch=(), cost=(0, 0), out_specs=None, aliases=None, keep=()):
    shapes = [
        pltpu.VMEM(s, d) if m is True else m(s, d) if m else jax.ShapeDtypeStruct(s, d)
        for s, d, m in outs
    ]
    shapes += [pltpu.VMEM(args[i].shape, args[i].dtype) for i in keep]
    n_in, n_out = len(args), len(outs)
    aliases = {**(aliases or {}), **{i: n_out + k for k, i in enumerate(keep)}}

    def kernel(*refs):
        body(*refs[: n_in + n_out], *refs[n_in + n_out + len(keep) :])

    args = [
        pltpu.with_memory_space_constraint(a, s.memory_space)
        for a, s in zip(args, specs)
    ]
    return pl.pallas_call(
        kernel,
        out_shape=shapes,
        in_specs=list(specs),
        out_specs=(out_specs or [VMEM] * len(outs)) + [VMEM] * len(keep),
        scratch_shapes=list(scratch),
        input_output_aliases=aliases,
        cost_estimate=pl.CostEstimate(flops=cost[0], bytes_accessed=cost[1], transcendentals=0),
        compiler_params=pltpu.CompilerParams(vmem_limit_bytes=8 << 20),
    )(*args)


def split(x):
    high = x.astype(BF16)
    return high, (x - high.astype(F32)).astype(BF16)


def product(x, weights):
    out = jnp.dot(jnp.concatenate(split(x), axis=1), weights, preferred_element_type=F32)
    return out[:, :B] + out[:, B:]


def collide(s, cloudy, capture, transfer):
    loss = s * product(s, capture)
    return s + cloudy * (product(loss, transfer) - loss)


def eightfold(ref, row):
    return ref[pl.ds(row, T, stride=0), :]


def repeated(ref, start, n):
    return jnp.concatenate([eightfold(ref, start + i) for i in range(n)], axis=0)


def classes(sc_ref):
    lane = lax.broadcasted_iota(jnp.int32, (T, B), 1)
    return lane < sc_ref[0], lane >= sc_ref[1]


def fall(c0, c2, a, b, c):
    return jnp.where(c0, a, jnp.where(c2, c, b))


def count_body(falls, u_in, v_in, way, out, u, v, ref, sem):
    copies = [
        pltpu.make_async_copy(a, b, sem.at[i])
        for i, (a, b) in enumerate(((falls, ref), (u_in, u), (v_in, v)))
    ]
    for copy in copies:
        copy.start()
    for copy in copies:
        copy.wait()
    n0 = jnp.sum((ref[...] == 0).astype(jnp.int32))
    n2 = jnp.sum((ref[...] == H_MAX).astype(jnp.int32))
    out[0] = n0
    out[1] = B - n2
    way[0] = (n2 - n0 <= SPARE).astype(jnp.int32) + (n2 <= n0).astype(jnp.int32)


def edges_body(drops, cloud, k_in, t_in, own, m1, ym0, ym1, yp0, yp1, kk, tt, mask, k_ref, t_ref, sem):
    level = lambda z: pl.ds(z * X * Y, X * Y)
    copies = [
        pltpu.make_async_copy(a, b, sem.at[i])
        for i, (a, b) in enumerate(
            [(drops.at[level(z)], own.at[level(z)]) for z in range(Z)]
            + [(cloud, mask), (k_in, k_ref), (t_in, t_ref)]
        )
    ]
    for copy in copies[Z:] + copies[:Z]:
        copy.start()
    copies[Z].wait()
    columns = mask[...].astype(F32)
    for x in range(X):
        m1[(x + 1) * Y : (x + 2) * Y] = jnp.broadcast_to(columns[:, x : x + 1], (Y, B))
    for i, (ref, out, turned) in enumerate(((k_ref, kk, True), (t_ref, tt, False))):
        copies[Z + 1 + i].wait()
        w = ref[...].T if turned else ref[...]
        high, low = split(w)
        half = jnp.concatenate([high, low], axis=1)
        out[...] = jnp.concatenate([half, half], axis=0)
    for out, ys in ((ym0, (0, 1)), (yp0, (Y - 1, Y - 2))):
        for d, y in enumerate(ys):
            out[HALF + d * X : HALF + (d + 1) * X] = m1[pl.ds(Y + y, X, stride=Y), :]
    for z in range(Z):
        copies[z].wait()
        for outs, ys in (((ym0, ym1), (0, 1)), ((yp0, yp1), (Y - 1, Y - 2))):
            for d, y in enumerate(ys):
                at = (d * LOW + z % LOW) * X
                outs[z // LOW][at : at + X] = own[pl.ds(z * X * Y + y, X, stride=Y), :]
    for out, y in ((ym0, 0), (yp0, Y - 1)):
        for i, x in enumerate((0, X - 1)):
            at, start = ENDS + i * LOW, (LOW * X + x) * Y + y
            out[at : at + LOW] = own[pl.ds(start, LOW, stride=X * Y), :]


def sides_body(own, m1, south, north, xm, xp):
    for out, cols in ((xm, (0, 1)), (xp, (X - 1, X - 2))):
        for d, x in enumerate(cols):
            out[XROWS + d * Y : XROWS + (d + 1) * Y] = m1[(x + 1) * Y : (x + 2) * Y]
            for z in range(Z):
                at = (z * X + x) * Y
                out[(d * Z + z) * Y : (d * Z + z + 1) * Y] = own[at : at + Y]
        x = cols[0]
        at = XROWS + 2 * Y
        out[at + 2 * Z :] = jnp.zeros((T, B), F32)
        for side, ref in enumerate((south, north)):
            row = at + side * Z
            end = ENDS + (LOW if x else 0)
            out[row : row + LOW] = ref[pl.ds(x, LOW, stride=X), :]
            out[row + LOW : row + Z] = ref[end : end + LOW]
            row = at + 2 * Z + side
            out[row : row + 1] = ref[HALF + x : HALF + x + 1]


XMESSAGE = XROWS + 2 * Y + 2 * Z + T


def own_body(own, m1, kk, tt, c1):
    k, t, mask = kk[...], tt[...], m1[Y : Y + X * Y]

    def level(z, _):
        c1[rows((z * XW + 2) * Y, X * Y)] = collide(own[rows(z * X * Y, X * Y)], mask, k, t)
        return 0

    lax.fori_loop(0, Z, level, 0, unroll=4)


def cy_at(side, d, x):
    return ((side * 2 + d) * XA + x + 1) * Z


def collide_rows(part, south, north, masks, cy, k, t):
    for side, (ref, mask_ref) in enumerate(zip((south, north), masks)):
        for d in range(2):
            mask = jnp.concatenate([mask_ref[HALF + d * X : HALF + (d + 1) * X]] * LOW, axis=0)
            c = collide(ref[d * LOW * X : (d + 1) * LOW * X], mask, k, t)
            for z in range(LOW):
                cy[pl.ds(cy_at(side, d, 0) + part * LOW + z, X, stride=Z), :] = c[z * X : (z + 1) * X]


def upwind(z, u_ref, v_ref):
    u, v = u_ref[z], v_ref[z]
    at_edge = lax.broadcasted_iota(jnp.int32, (T, B), 0) == jnp.where(v > 0, 0, T - 1)
    return (
        jnp.abs(u),
        jnp.abs(v),
        jnp.where(u > 0, -Y, Y),
        jnp.where(v > 0, 1, T - 1),
        jnp.where(v > 0, 0, 1),
        at_edge,
    )


def advect(z, columns, c_ref, width, first, out_ref, out_width, edge, u_ref, v_ref):
    au, av, step, shift, side, at_edge = upwind(z, u_ref, v_ref)
    base, base_out = (z * width + first) * Y, z * out_width * Y
    edge_ref, edge_at, edge_stride = edge(z, side)
    for i in columns:
        c = c_ref[rows(base + i * Y)]
        x = c_ref[rows(base + step + i * Y)]
        e = eightfold(edge_ref, edge_at + i * edge_stride)
        y = jnp.where(at_edge, e, pltpu.roll(c, shift, 0))
        out_ref[rows(base_out + i * Y)] = c - au * (c - x) - av * (c - y)


def advect_first(z, columns, c1, a1, cy, u_ref, v_ref):
    edge = lambda z, side: (cy, side * (2 * XA * Z) + z, Z)
    advect(z, columns, c1, XW, 1, a1, XA, edge, u_ref, v_ref)


def advect_second(z, columns, c2, a2, c2y, u_ref, v_ref):
    edge = lambda z, side: (c2y, (z * 2 + side) * X, 1)
    advect(z, columns, c2, XA, 1, a2, X, edge, u_ref, v_ref)


def advect_rows(columns, ub, vb, c1, cy, a1y):
    au, av = jnp.abs(ub[...]), jnp.abs(vb[...])
    upos, vpos = ub[...] > 0, vb[...] > 0
    for side in range(2):
        for x in columns:
            at, far = cy_at(side, 0, x), cy_at(side, 1, x)
            c = cy[at : at + Z]
            xx = jnp.where(upos, cy[at - Z : at], cy[at + Z : at + 2 * Z])
            outer = cy[far : far + Z]
            inner = c1[pl.ds((x + 2) * Y + (Y - 1) * side, Z, stride=XW * Y), :]
            yy = jnp.where(vpos, *((outer, inner) if side == 0 else (inner, outer)))
            to = (side * X + x) * Z
            a1y[to : to + Z] = c - au * (c - xx) - av * (c - yy)


def settle(z, columns, c0, cc2, a1, c2):
    for i in columns:
        at = (z * XA + i) * T
        step = XA * T
        c2[rows(at)] = fall(c0, cc2, a1[rows(at)], a1[rows(at + step)], a1[rows(at + 2 * step)])


def settle_level(z, c0, cc2, a1, m1, c2, k, t):
    settle(z, range(XA), c0, cc2, a1, c2)
    at = rows(z * XA * T, XA * T)
    c2[at] = collide(c2[at], m1[...], k, t)


def settle_rows(levels, tiles, c0, cc2, a1y, masks, c2y, k, t):
    pieces, cloudy, where = [], [], []
    for z in levels:
        for i in tiles:
            a = [a1y[pl.ds(i * T * Z + z + j, T, stride=Z), :] for j in range(H_MAX + 1)]
            pieces.append(fall(c0, cc2, *a))
            side, first = divmod(i * T, X)
            cloudy.append(masks[side][HALF + first : HALF + first + T])
            where.append(z * 2 * X + i * T)
    c = collide(jnp.concatenate(pieces, axis=0), jnp.concatenate(cloudy, axis=0), k, t)
    for i, to in enumerate(where):
        c2y[to : to + T] = c[i * T : (i + 1) * T]


def settle_edges(levels, c0, cc2, a1, m1, c2, k, t):
    for z in levels:
        settle(z, EDGE, c0, cc2, a1, c2)
    tiles = [(z * XA + i) * T for z in levels for i in EDGE]
    c = collide(
        jnp.concatenate([c2[at : at + T] for at in tiles], axis=0),
        jnp.concatenate([m1[i * T : (i + 1) * T] for i in EDGE] * len(levels), axis=0),
        k,
        t,
    )
    for i, at in enumerate(tiles):
        c2[at : at + T] = c[i * T : (i + 1) * T]


def falling(a1, a1y, a2, tile):
    if tile < X - 2:
        at = (tile + 2) * T
        return lambda z: a1[z * XA * T + at : z * XA * T + at + T]
    tile -= X - 2
    if tile < 2 * X // T:
        return lambda z: a1y[pl.ds(tile * T * Z + z, T, stride=Z), :]
    at = (tile - 2 * X // T + 2) * T
    return lambda z: a2[z * X * T + at : z * X * T + at + T]


def early_body(
    extra, sc, u_ref, v_ref, ub, vb, c1, south, north, kk, tt, m1, cy, a1, a1y, c2, c2y, a2, pay
):
    k, t = kk[...], tt[...]
    c0, cc2 = classes(sc)
    collide_rows(0, south, north, (south, north), cy, k, t)

    def first(z, _):
        advect_first(z, range(2, X), c1, a1, cy, u_ref, v_ref)
        return 0

    lax.fori_loop(0, 4, first, 0)
    advect_rows(range(1, X - 1), ub, vb, c1, cy, a1y)

    def second(z, _):
        settle_level(z, c0, cc2, a1, m1, c2, k, t)
        return 0

    lax.fori_loop(0, 2, second, 0, unroll=2)
    settle_rows(range(2), ROW_TILES, c0, cc2, a1y, (south, north), c2y, k, t)

    def third(z, _):
        advect_second(z, range(2, X - 2), c2, a2, c2y, u_ref, v_ref)
        return 0

    lax.fori_loop(0, 2, third, 0)
    n0 = sc[0]
    n2 = B - sc[1]
    for tile in range(EARLY):
        level = falling(a1, a1y, a2, tile)
        l0 = level(0)
        packed = fall(c0, cc2, pltpu.roll(l0, n2, 1), l0, level(1))
        pay[tile * T : (tile + 1) * T] = packed
    group = lax.broadcasted_iota(jnp.int32, (T, B), 1) // SPARE
    for j in range(extra):
        out = jnp.zeros((T, B), F32)
        for g in range(GROUPS):
            if j + g * EXTRA < EARLY:
                l0 = falling(a1, a1y, a2, j + g * EXTRA)(0)
                turn = (n2 - n0 + g * SPARE + B) & (B - 1)
                out = jnp.where(group == g, pltpu.roll(l0, turn, 1), out)
        pay[(EARLY + j) * T : (EARLY + j + 1) * T] = out


def late_body(
    sc, u_ref, v_ref, ub, vb, left, right, kk, tt, south, north,
    c1_in, cy_in, m1_in, a1_in, a1y_in, c2_in, c2y_in, a2_in,
    c1, cy, m1, a1, a1y, c2, c2y, a2, pay,
):
    k, t = kk[...], tt[...]
    c0, cc2 = classes(sc)
    m1[0:Y] = left[XROWS : XROWS + Y]
    m1[Y + X * Y :] = right[XROWS : XROWS + Y]
    at_mask = XROWS + 2 * Y
    pieces, masks = [], []
    for ref in (left, right):
        pieces += [ref[0:XROWS], ref[at_mask : at_mask + 2 * Z]]
        masks += [ref[XROWS + d * Y : XROWS + (d + 1) * Y] for d in range(2) for _ in range(Z)]
        masks += [eightfold(ref, at_mask + 2 * Z + side) for side in range(2)]
    c = collide(jnp.concatenate(pieces, axis=0), jnp.concatenate(masks, axis=0), k, t)
    size = XROWS + 2 * Z
    for i, (columns, x) in enumerate((((1, 0), -1), ((XW - 2, XW - 1), X))):
        for d in range(2):
            for z in range(Z):
                at, to = i * size + (d * Z + z) * Y, (z * XW + columns[d]) * Y
                c1[to : to + Y] = c[at : at + Y]
        for side in range(2):
            at, to = i * size + XROWS + side * Z, cy_at(side, 0, x)
            cy[to : to + Z] = c[at : at + Z]

    for z in range(4):
        advect_first(z, EDGE, c1, a1, cy, u_ref, v_ref)
    advect_rows((0, X - 1), ub, vb, c1, cy, a1y)
    settle_edges(range(2), c0, cc2, a1, m1, c2, k, t)
    settle_rows(range(2), ROW_EDGES, c0, cc2, a1y, (south, north), c2y, k, t)
    for z in range(2):
        advect_second(z, ENDING, c2, a2, c2y, u_ref, v_ref)
    for i, x in enumerate(EDGE):
        l0, l1 = (a1[(z * XA + x) * T : (z * XA + x + 1) * T] for z in range(2))
        pay[i * T : (i + 1) * T] = fall(c0, cc2, l0, l0, l1)
        pay[(LATE + i) * T : (LATE + i + 1) * T] = l0
    at = 4 * T
    for i, row in enumerate((0, X - 1, X, 2 * X - 1)):
        l0, l1 = (a1y[row * Z + z : row * Z + z + 1] for z in range(2))
        pay[at + i : at + i + 1] = fall(c0[0:1], cc2[0:1], l0, l0, l1)
        pay[at + LATE * T + i : at + LATE * T + i + 1] = l0
    for first in (at + 4, at + LATE * T + 4):
        pay[first : first + 4] = jnp.zeros((4, B), F32)
    for i, x in enumerate(ENDING):
        l0, l1 = (a2[(z * X + x) * T : (z * X + x + 1) * T] for z in range(2))
        to = at + (i + 1) * T
        pay[to : to + T] = fall(c0, cc2, l0, l0, l1)
        pay[to + LATE * T : to + LATE * T + T] = l0


def fall_out(z, columns, c0, cc2, a2, res):
    for i in columns:
        at, step = (z * X + i) * T, X * T
        res[at : at + T] = fall(
            c0, cc2, *(a2[at + k * step : at + k * step + T] for k in range(H_MAX + 1))
        )


def between_body(
    sc, u_ref, v_ref, ub, vb, kk, tt, south, north, south1, north1, c1, m1,
    cy_in, a1_in, a1y_in, c2_in, c2y_in, a2_in,
    cy, a1, a1y, c2, c2y, a2, res,
):
    k, t = kk[...], tt[...]
    c0, cc2 = classes(sc)
    collide_rows(1, south1, north1, (south, north), cy, k, t)

    def first(z, _):
        advect_first(z, range(2, X), c1, a1, cy, u_ref, v_ref)
        return 0

    lax.fori_loop(4, 8, first, 0)
    advect_rows(range(1, X - 1), ub, vb, c1, cy, a1y)

    def second(z, _):
        settle_level(z, c0, cc2, a1, m1, c2, k, t)
        return 0

    lax.fori_loop(2, 6, second, 0, unroll=4)
    settle_rows(range(2, 6), ROW_TILES, c0, cc2, a1y, (south, north), c2y, k, t)

    def third(z, _):
        advect_second(z, range(2, X - 2), c2, a2, c2y, u_ref, v_ref)
        return 0

    lax.fori_loop(2, 6, third, 0)
    for z in range(4):
        fall_out(z, range(2, X - 2), c0, cc2, a2, res)


def rest_body(
    sc, u_ref, v_ref, kk, tt, south, north, c1, m1, cy, a1y,
    a1_in, c2_in, c2y_in, a2_in, res_in,
    a1, c2, c2y, a2, res, out, sem,
):
    k, t = kk[...], tt[...]
    c0, cc2 = classes(sc)
    for z in range(4, 8):
        advect_first(z, EDGE, c1, a1, cy, u_ref, v_ref)
    settle_edges(range(2, 6), c0, cc2, a1, m1, c2, k, t)
    settle_rows(range(2, 6), ROW_EDGES, c0, cc2, a1y, (south, north), c2y, k, t)
    for z in range(2, 6):
        advect_second(z, ENDING, c2, a2, c2y, u_ref, v_ref)
    for z in range(4):
        fall_out(z, ENDING, c0, cc2, a2, res)
    copy = pltpu.make_async_copy(res, out.at[pl.ds(0, 4 * X * T)], sem)
    copy.start()
    copy.wait()


def last_body(
    extra, sc, u_ref, v_ref, kk, tt, south, north, m1, a1, a1y, c2_in, c2y_in, a2_in, early, late, out_in,
    out, c2, c2y, a2, row7, row6, res, sem,
):
    k, t = kk[...], tt[...]
    c0, cc2 = classes(sc)
    n0, start2 = sc[0], sc[1]
    lane = lax.broadcasted_iota(jnp.int32, (T, B), 1)
    within = lane < start2 + n0
    turns = [(n0 + start2 - g * SPARE + B) & (B - 1) for g in range(GROUPS)]

    def from_above(tile):
        m = early[tile * T : (tile + 1) * T]
        if not extra:
            return m, pltpu.roll(m, start2, 1)
        g, j = tile // EXTRA, tile % EXTRA
        spare = early[(EARLY + j) * T : (EARLY + j + 1) * T]
        return m, jnp.where(within, pltpu.roll(m, start2, 1), pltpu.roll(spare, turns[g], 1))

    def from_late(i):
        return late[i * T : (i + 1) * T], late[(LATE + i) * T : (LATE + i + 1) * T]

    for i in range(XA):
        p7, p6 = from_late(EDGE.index(i)) if i in EDGE else from_above(i - 2)
        x6, x7 = (a1[(z * XA + i) * T : (z * XA + i + 1) * T] for z in (6, 7))
        c2[(6 * XA + i) * T : (6 * XA + i + 1) * T] = fall(c0, cc2, x6, x7, p6)
        c2[(7 * XA + i) * T : (7 * XA + i + 1) * T] = jnp.where(c0, x7, p7)
    for i in range(2 * X // T):
        row7[i * T : (i + 1) * T], row6[i * T : (i + 1) * T] = from_above(X - 2 + i)
    p7, p6 = from_late(4)
    for i, row in enumerate((0, X - 1, X, 2 * X - 1)):
        row7[row : row + 1], row6[row : row + 1] = p7[i : i + 1], p6[i : i + 1]
    for i in range(2 * X // T):
        x6, x7 = (a1y[pl.ds(i * T * Z + z, T, stride=Z), :] for z in (6, 7))
        at = 6 * 2 * X + i * T
        c2y[at : at + T] = fall(c0, cc2, x6, x7, row6[i * T : (i + 1) * T])
        c2y[at + 2 * X : at + 2 * X + T] = jnp.where(c0, x7, row7[i * T : (i + 1) * T])
    mask = jnp.concatenate([south[HALF : HALF + X], north[HALF : HALF + X]] * 2, axis=0)
    at = slice(12 * X, 16 * X)
    c2y[at] = collide(c2y[at], mask, k, t)
    for z in (6, 7):
        at = slice(z * XA * T, (z + 1) * XA * T)
        c2[at] = collide(c2[at], m1[...], k, t)
        advect_second(z, range(X), c2, a2, c2y, u_ref, v_ref)
    copies = []
    for z in range(4, 8):
        for i in range(X):
            x = [a2[(k * X + i) * T : (k * X + i + 1) * T] for k in range(z, min(z + 3, Z))]
            if z > 5:
                tile = X - 2 + 2 * X // T + i - 2
                p7, p6 = from_late(5 + ENDING.index(i)) if i in ENDING else from_above(tile)
                x = x + [p6] if z == 6 else x + [p7, p7]
            res[((z - 4) * X + i) * T : ((z - 4) * X + i + 1) * T] = fall(c0, cc2, *x)
        to = pl.ds(z * X * T, X * T)
        copies.append(
            pltpu.make_async_copy(res.at[pl.ds((z - 4) * X * T, X * T)], out.at[to], sem.at[z - 4])
        )
        copies[-1].start()
    for copy in copies:
        copy.wait()


def ring(axis, step):
    n = lax.axis_size(axis)
    return [(i, (i + step) % n) for i in range(n)]


def below(value):
    return lax.ppermute(value, "gz", [(i, i - 1) for i in range(1, lax.axis_size("gz"))])


def packed(extra, scalars, drops, capture, transfer, courant_u, courant_v, fall_class, cloud_mask):
    drops = drops.reshape(Z * X * Y, B)
    ub = jnp.broadcast_to(courant_u[:, None], (Z, B))
    vb = jnp.broadcast_to(courant_v[:, None], (Z, B))
    v = lambda n, d=F32: ((n, B), d, True)
    weights = [((2 * B, 2 * B), BF16, True)] * 2
    own, m1, ym0, ym1, yp0, yp1, kk, tt = call(
        edges_body,
        [v(Z * X * Y), v(XA * Y), v(ENDS + T), v(HALF), v(ENDS + T), v(HALF)] + weights,
        [drops, cloud_mask.T, capture, transfer],
        [HBM] * 4,
        [pltpu.VMEM((Y, X), jnp.int32), pltpu.VMEM((B, B), F32), pltpu.VMEM((B, B), F32), pltpu.SemaphoreType.DMA((Z + 3,))],
        cost=(1000, 4 << 20),
    )
    south0 = lax.ppermute(yp0, "gy", ring("gy", 1))
    north0 = lax.ppermute(ym0, "gy", ring("gy", -1))
    south1 = lax.ppermute(yp1, "gy", ring("gy", 1))
    north1 = lax.ppermute(ym1, "gy", ring("gy", -1))
    c1, kk, tt = call(
        own_body, [v(Z * XW * Y)], [own, m1, kk, tt], [VMEM] * 4, cost=(3 << 30, 8 << 20), keep=(2, 3)
    )
    shapes = [v(4 * XA * Z), v(Z * XA * T), v(2 * X * Z), v(Z * XA * T), v(Z * 2 * X), v(Z * X * T)]
    cy, a1, a1y, c2, c2y, a2, pay, kk, tt = call(
        functools.partial(early_body, extra),
        shapes + [v((EARLY + extra) * T)],
        [*scalars, ub, vb, c1, south0, north0, kk, tt, m1],
        [SMEM] * 3 + [VMEM] * 8,
        cost=(3 << 30, 8 << 20),
        keep=(8, 9),
    )
    pay, south1, north1 = lax.optimization_barrier((pay, south1, north1))
    early = below(pay)
    xm, xp = call(
        sides_body,
        [v(XMESSAGE)] * 2,
        [own, m1, south0, north0],
        [VMEM] * 4,
        cost=(1000, 1 << 18),
    )
    left = lax.ppermute(xp, "gx", ring("gx", 1))
    right = lax.ppermute(xm, "gx", ring("gx", -1))
    cy, a1, a1y, c2, c2y, a2, res, kk, tt = call(
        between_body,
        shapes + [v(4 * X * T)],
        [*scalars, ub, vb, kk, tt, south0, north0, south1, north1, c1, m1, cy, a1, a1y, c2, c2y, a2],
        [SMEM] * 3 + [VMEM] * 16,
        cost=(3 << 30, 8 << 20),
        aliases={13 + i: i for i in range(6)},
        keep=(5, 6),
    )
    c1, cy, m1, a1, a1y, c2, c2y, a2, pay, kk, tt = call(
        late_body,
        [v(Z * XW * Y), shapes[0], v(XA * Y)] + shapes[1:] + [v(2 * LATE * T)],
        [*scalars, ub, vb, left, right, kk, tt, south0, north0, c1, cy, m1, a1, a1y, c2, c2y, a2],
        [SMEM] * 3 + [VMEM] * 16,
        cost=(1 << 28, 1 << 20),
        aliases={11 + i: i for i in range(8)},
        keep=(7, 8),
    )
    late = below(pay)
    a1, c2, c2y, a2, _, out, kk, tt = call(
        rest_body,
        [shapes[1], *shapes[3:], v(4 * X * T), ((Z * X * Y, B), F32, False)],
        [*scalars, kk, tt, south0, north0, c1, m1, cy, a1y, a1, c2, c2y, a2, res],
        [SMEM] * 3 + [VMEM] * 13,
        [pltpu.SemaphoreType.DMA],
        cost=(1 << 28, 1 << 20),
        out_specs=[VMEM] * 5 + [HBM],
        aliases={11 + i: i for i in range(5)},
        keep=(3, 4),
    )
    out, *_ = call(
        functools.partial(last_body, extra),
        [((Z * X * Y, B), F32, False), shapes[3], shapes[4], shapes[5]],
        [*scalars, kk, tt, south0, north0, m1, a1, a1y, c2, c2y, a2, early, late, out],
        [SMEM] * 3 + [VMEM] * 12 + [HBM],
        [pltpu.VMEM((2 * X, B), F32), pltpu.VMEM((2 * X, B), F32), pltpu.VMEM((4 * X * T, B), F32), pltpu.SemaphoreType.DMA((4,))],
        cost=(1 << 30, 8 << 20),
        out_specs=[HBM] + [VMEM] * 3,
        aliases={15: 0, 10: 1, 11: 2, 12: 3},
    )
    return out.reshape(Z, X, Y, B)


def passed_along(block, axis, distance):
    devices = range(lax.axis_size(axis))
    route = [(i - distance, i) for i in devices if i - distance in devices]
    return lax.ppermute(block, axis, route)


def with_halo(value, sides, width):
    edges = {}
    for axis, dim in sides:
        devices, length = (lax.axis_size(axis), value.shape[dim])
        up = [(i, (i + 1) % devices) for i in range(devices)]
        last = lax.slice_in_dim(value, length - width, length, axis=dim)
        leading = lax.slice_in_dim(value, 0, width, axis=dim)
        edges[dim] = (
            lax.ppermute(last, axis, up),
            lax.ppermute(leading, axis, [(b, a) for a, b in up]),
        )
    done = []
    for _, dim in sides:
        low, high = edges[dim]
        around = [(width, width) if d in done else (0, 0) for d in range(value.ndim)]
        value = jnp.concatenate([jnp.pad(low, around), value, jnp.pad(high, around)], axis=dim)
        done.append(dim)
    return value


def collide_plain(particle_distribution, capture_efficiency_matrix, transfer, cloudy):
    merger_speed = jnp.einsum(
        "ugcr,mr->ugcm",
        particle_distribution,
        capture_efficiency_matrix,
        precision=lax.Precision.HIGHEST,
    )
    water_removed = particle_distribution * merger_speed
    mass_gain = jnp.einsum(
        "zxyi,ik->zxyk", water_removed, transfer, precision=lax.Precision.HIGHEST
    )
    return particle_distribution + cloudy[None, :, :, None] * (mass_gain - water_removed)


def advect_plain(with_edges, courant_u, courant_v):
    centre = with_edges[:, 1:-1, 1:-1]
    west_side = with_edges[:, :-2, 1:-1]
    east_side = with_edges[:, 2:, 1:-1]
    south_side = with_edges[:, 1:-1, :-2]
    north_side = with_edges[:, 1:-1, 2:]
    x_plus = jnp.maximum(courant_u, 0.0)[:, None, None, None]
    x_minus = jnp.minimum(courant_u, 0.0)[:, None, None, None]
    northward_neighbor = jnp.maximum(courant_v, 0.0)[:, None, None, None]
    y_minus = jnp.minimum(courant_v, 0.0)[:, None, None, None]
    result = centre - x_plus * (centre - west_side) - x_minus * (east_side - centre)
    return result - northward_neighbor * (centre - south_side) - y_minus * (north_side - centre)


def sediment(padded, fall_class, levels):
    result = padded[:levels]
    for fall_depth in range(1, H_MAX + 1):
        result = jnp.where(
            (fall_class == fall_depth)[None, None, None, :],
            padded[fall_depth : fall_depth + levels],
            result,
        )
    return result


def plain(
    drops, capture_efficiency_matrix, transfer, courant_u, courant_v, fall_class, cloud_mask
):
    cloudy = cloud_mask.astype(jnp.float32)
    reach = STEPS * H_MAX
    from_above, upper_u, upper_v = passed_along(
        (drops[:reach], courant_u[:reach], courant_v[:reach]), "gz", -1
    )
    particle_distribution = jnp.concatenate([drops, from_above], axis=0)
    column_u = jnp.concatenate([courant_u, upper_u], axis=0)
    column_v = jnp.concatenate([courant_v, upper_v], axis=0)
    for repeat in range(STEPS):
        current = particle_distribution.shape[0]
        coalesced_drops = collide_plain(
            particle_distribution, capture_efficiency_matrix, transfer, cloudy
        )
        with_edges = with_halo(coalesced_drops, (("gx", 1), ("gy", 2)), 1)
        advected = advect_plain(with_edges, column_u[:current], column_v[:current])
        particle_distribution = sediment(advected, fall_class, current - H_MAX)
    return particle_distribution


def on_device(*args):
    way, *scalars = call(
        count_body,
        [((1,), jnp.int32, pltpu.SMEM), ((2,), jnp.int32, pltpu.SMEM)] + [((Z,), F32, pltpu.SMEM)] * 2,
        [args[5].reshape(1, B), args[3], args[4]],
        [HBM] * 3,
        [pltpu.VMEM((1, B), jnp.int32), pltpu.SemaphoreType.DMA((3,))],
        out_specs=[SMEM] * 4,
    )
    ways = (
        lambda s, *a: plain(*a),
        lambda s, *a: packed(EXTRA, s, *a),
        lambda s, *a: packed(0, s, *a),
    )
    return lax.switch(way.reshape(()), ways, scalars, *args)


def solution(mesh):
    in_specs = (P("gz", "gx", "gy", None), P(), P(), P("gz"), P("gz"), P(), P("gx", "gy"))
    out_specs = P("gz", "gx", "gy", None)
    return jax.shard_map(
        on_device, mesh=mesh, in_specs=in_specs, out_specs=out_specs, check_vma=False
    )
```

```python
import functools

import jax
import jax.numpy as jnp
from jax import lax
from jax.experimental import pallas as pl
from jax.experimental.pallas import tpu as pltpu
from jax.sharding import PartitionSpec as P

H_MAX = 2
STEPS = 2
Z, X, Y, B = 8, 64, 8, 128
T = 8
XW = X + 4
XA = X + 2
LOW = Z // 2
HALF = 2 * LOW * X
ENDS = HALF + 2 * X
XROWS = 2 * Z * Y
EARLY = (X - 2) + 2 * X // T + (X - 4)
GROUPS = 4
SPARE = B // GROUPS
EXTRA = -(-EARLY // GROUPS)
LATE = 4 + 1 + 4
EDGE = (0, 1, XA - 2, XA - 1)
ENDING = (0, 1, X - 2, X - 1)
ROW_TILES = range(2 * X // T)
ROW_EDGES = (0, X // T - 1, X // T, 2 * X // T - 1)
F32, BF16 = jnp.float32, jnp.bfloat16

VMEM = pl.BlockSpec(memory_space=pltpu.VMEM)
SMEM = pl.BlockSpec(memory_space=pltpu.SMEM)
HBM = pl.BlockSpec(memory_space=pltpu.HBM)


def rows(start, n=T):
    return pl.ds(start if isinstance(start, int) else pl.multiple_of(start, T), n)


def call(body, outs, args, specs, scratch=(), cost=(0, 0), out_specs=None, aliases=None, keep=()):
    shapes = [
        pltpu.VMEM(s, d) if m is True else m(s, d) if m else jax.ShapeDtypeStruct(s, d)
        for s, d, m in outs
    ]
    shapes += [pltpu.VMEM(args[i].shape, args[i].dtype) for i in keep]
    n_in, n_out = len(args), len(outs)
    aliases = {**(aliases or {}), **{i: n_out + k for k, i in enumerate(keep)}}

    def kernel(*refs):
        body(*refs[: n_in + n_out], *refs[n_in + n_out + len(keep) :])

    args = [
        pltpu.with_memory_space_constraint(a, s.memory_space)
        for a, s in zip(args, specs)
    ]
    return pl.pallas_call(
        kernel,
        out_shape=shapes,
        in_specs=list(specs),
        out_specs=(out_specs or [VMEM] * len(outs)) + [VMEM] * len(keep),
        scratch_shapes=list(scratch),
        input_output_aliases=aliases,
        cost_estimate=pl.CostEstimate(flops=cost[0], bytes_accessed=cost[1], transcendentals=0),
        compiler_params=pltpu.CompilerParams(vmem_limit_bytes=8 << 20),
    )(*args)


def split(x):
    high = x.astype(BF16)
    return high, (x - high.astype(F32)).astype(BF16)


def product(x, weights):
    out = jnp.dot(jnp.concatenate(split(x), axis=1), weights, preferred_element_type=F32)
    return out[:, :B] + out[:, B:]


def collide(s, cloudy, capture, transfer):
    loss = s * product(s, capture)
    return s + cloudy * (product(loss, transfer) - loss)


def eightfold(ref, row):
    return ref[pl.ds(row, T, stride=0), :]


def repeated(ref, start, n):
    return jnp.concatenate([eightfold(ref, start + i) for i in range(n)], axis=0)


def classes(sc_ref):
    lane = lax.broadcasted_iota(jnp.int32, (T, B), 1)
    return lane < sc_ref[0], lane >= sc_ref[1]


def fall(c0, c2, a, b, c):
    return jnp.where(c0, a, jnp.where(c2, c, b))


def count_body(falls, u_in, v_in, way, out, u, v, ref, sem):
    copies = [
        pltpu.make_async_copy(a, b, sem.at[i])
        for i, (a, b) in enumerate(((falls, ref), (u_in, u), (v_in, v)))
    ]
    for copy in copies:
        copy.start()
    for copy in copies:
        copy.wait()
    n0 = jnp.sum((ref[...] == 0).astype(jnp.int32))
    n2 = jnp.sum((ref[...] == H_MAX).astype(jnp.int32))
    out[0] = n0
    out[1] = B - n2
    way[0] = (n2 - n0 <= SPARE).astype(jnp.int32) + (n2 <= n0).astype(jnp.int32)


def edges_body(drops, cloud, k_in, t_in, own, m1, ym0, ym1, yp0, yp1, kk, tt, mask, k_ref, t_ref, sem):
    level = lambda z: pl.ds(z * X * Y, X * Y)
    copies = [
        pltpu.make_async_copy(a, b, sem.at[i])
        for i, (a, b) in enumerate(
            [(drops.at[level(z)], own.at[level(z)]) for z in range(Z)]
            + [(cloud, mask), (k_in, k_ref), (t_in, t_ref)]
        )
    ]
    for copy in copies[Z:] + copies[:Z]:
        copy.start()
    copies[Z].wait()
    columns = mask[...].astype(F32)
    for x in range(X):
        m1[(x + 1) * Y : (x + 2) * Y] = jnp.broadcast_to(columns[:, x : x + 1], (Y, B))
    for i, (ref, out, turned) in enumerate(((k_ref, kk, True), (t_ref, tt, False))):
        copies[Z + 1 + i].wait()
        w = ref[...].T if turned else ref[...]
        high, low = split(w)
        half = jnp.concatenate([high, low], axis=1)
        out[...] = jnp.concatenate([half, half], axis=0)
    for out, ys in ((ym0, (0, 1)), (yp0, (Y - 1, Y - 2))):
        for d, y in enumerate(ys):
            out[HALF + d * X : HALF + (d + 1) * X] = m1[pl.ds(Y + y, X, stride=Y), :]
    for z in range(Z):
        copies[z].wait()
        for outs, ys in (((ym0, ym1), (0, 1)), ((yp0, yp1), (Y - 1, Y - 2))):
            for d, y in enumerate(ys):
                at = (d * LOW + z % LOW) * X
                outs[z // LOW][at : at + X] = own[pl.ds(z * X * Y + y, X, stride=Y), :]
    for out, y in ((ym0, 0), (yp0, Y - 1)):
        for i, x in enumerate((0, X - 1)):
            at, start = ENDS + i * LOW, (LOW * X + x) * Y + y
            out[at : at + LOW] = own[pl.ds(start, LOW, stride=X * Y), :]


def sides_body(own, m1, south, north, xm, xp):
    for out, cols in ((xm, (0, 1)), (xp, (X - 1, X - 2))):
        for d, x in enumerate(cols):
            out[XROWS + d * Y : XROWS + (d + 1) * Y] = m1[(x + 1) * Y : (x + 2) * Y]
            for z in range(Z):
                at = (z * X + x) * Y
                out[(d * Z + z) * Y : (d * Z + z + 1) * Y] = own[at : at + Y]
        x = cols[0]
        at = XROWS + 2 * Y
        out[at + 2 * Z :] = jnp.zeros((T, B), F32)
        for side, ref in enumerate((south, north)):
            row = at + side * Z
            end = ENDS + (LOW if x else 0)
            out[row : row + LOW] = ref[pl.ds(x, LOW, stride=X), :]
            out[row + LOW : row + Z] = ref[end : end + LOW]
            row = at + 2 * Z + side
            out[row : row + 1] = ref[HALF + x : HALF + x + 1]


XMESSAGE = XROWS + 2 * Y + 2 * Z + T


def own_body(own, m1, kk, tt, c1):
    k, t, mask = kk[...], tt[...], m1[Y : Y + X * Y]

    def level(z, _):
        c1[rows((z * XW + 2) * Y, X * Y)] = collide(own[rows(z * X * Y, X * Y)], mask, k, t)
        return 0

    lax.fori_loop(0, Z, level, 0, unroll=4)


def cy_at(side, d, x):
    return ((side * 2 + d) * XA + x + 1) * Z


def collide_rows(part, south, north, masks, cy, k, t):
    for side, (ref, mask_ref) in enumerate(zip((south, north), masks)):
        for d in range(2):
            mask = jnp.concatenate([mask_ref[HALF + d * X : HALF + (d + 1) * X]] * LOW, axis=0)
            c = collide(ref[d * LOW * X : (d + 1) * LOW * X], mask, k, t)
            for z in range(LOW):
                cy[pl.ds(cy_at(side, d, 0) + part * LOW + z, X, stride=Z), :] = c[z * X : (z + 1) * X]


def upwind(z, u_ref, v_ref):
    u, v = u_ref[z], v_ref[z]
    at_edge = lax.broadcasted_iota(jnp.int32, (T, B), 0) == jnp.where(v > 0, 0, T - 1)
    return (
        jnp.abs(u),
        jnp.abs(v),
        jnp.where(u > 0, -Y, Y),
        jnp.where(v > 0, 1, T - 1),
        jnp.where(v > 0, 0, 1),
        at_edge,
    )


def advect(z, columns, c_ref, width, first, out_ref, out_width, edge, u_ref, v_ref):
    au, av, step, shift, side, at_edge = upwind(z, u_ref, v_ref)
    base, base_out = (z * width + first) * Y, z * out_width * Y
    edge_ref, edge_at, edge_stride = edge(z, side)
    for i in columns:
        c = c_ref[rows(base + i * Y)]
        x = c_ref[rows(base + step + i * Y)]
        e = eightfold(edge_ref, edge_at + i * edge_stride)
        y = jnp.where(at_edge, e, pltpu.roll(c, shift, 0))
        out_ref[rows(base_out + i * Y)] = c - au * (c - x) - av * (c - y)


def advect_first(z, columns, c1, a1, cy, u_ref, v_ref):
    edge = lambda z, side: (cy, side * (2 * XA * Z) + z, Z)
    advect(z, columns, c1, XW, 1, a1, XA, edge, u_ref, v_ref)


def advect_second(z, columns, c2, a2, c2y, u_ref, v_ref):
    edge = lambda z, side: (c2y, (z * 2 + side) * X, 1)
    advect(z, columns, c2, XA, 1, a2, X, edge, u_ref, v_ref)


def advect_rows(columns, ub, vb, c1, cy, a1y):
    au, av = jnp.abs(ub[...]), jnp.abs(vb[...])
    upos, vpos = ub[...] > 0, vb[...] > 0
    for side in range(2):
        for x in columns:
            at, far = cy_at(side, 0, x), cy_at(side, 1, x)
            c = cy[at : at + Z]
            xx = jnp.where(upos, cy[at - Z : at], cy[at + Z : at + 2 * Z])
            outer = cy[far : far + Z]
            inner = c1[pl.ds((x + 2) * Y + (Y - 1) * side, Z, stride=XW * Y), :]
            yy = jnp.where(vpos, *((outer, inner) if side == 0 else (inner, outer)))
            to = (side * X + x) * Z
            a1y[to : to + Z] = c - au * (c - xx) - av * (c - yy)


def settle(z, columns, c0, cc2, a1, c2):
    for i in columns:
        at = (z * XA + i) * T
        step = XA * T
        c2[rows(at)] = fall(c0, cc2, a1[rows(at)], a1[rows(at + step)], a1[rows(at + 2 * step)])


def settle_level(z, c0, cc2, a1, m1, c2, k, t):
    settle(z, range(XA), c0, cc2, a1, c2)
    at = rows(z * XA * T, XA * T)
    c2[at] = collide(c2[at], m1[...], k, t)


def settle_rows(levels, tiles, c0, cc2, a1y, masks, c2y, k, t):
    pieces, cloudy, where = [], [], []
    for z in levels:
        for i in tiles:
            a = [a1y[pl.ds(i * T * Z + z + j, T, stride=Z), :] for j in range(H_MAX + 1)]
            pieces.append(fall(c0, cc2, *a))
            side, first = divmod(i * T, X)
            cloudy.append(masks[side][HALF + first : HALF + first + T])
            where.append(z * 2 * X + i * T)
    c = collide(jnp.concatenate(pieces, axis=0), jnp.concatenate(cloudy, axis=0), k, t)
    for i, to in enumerate(where):
        c2y[to : to + T] = c[i * T : (i + 1) * T]


def settle_edges(levels, c0, cc2, a1, m1, c2, k, t):
    for z in levels:
        settle(z, EDGE, c0, cc2, a1, c2)
    tiles = [(z * XA + i) * T for z in levels for i in EDGE]
    c = collide(
        jnp.concatenate([c2[at : at + T] for at in tiles], axis=0),
        jnp.concatenate([m1[i * T : (i + 1) * T] for i in EDGE] * len(levels), axis=0),
        k,
        t,
    )
    for i, at in enumerate(tiles):
        c2[at : at + T] = c[i * T : (i + 1) * T]


def falling(a1, a1y, a2, tile):
    if tile < X - 2:
        at = (tile + 2) * T
        return lambda z: a1[z * XA * T + at : z * XA * T + at + T]
    tile -= X - 2
    if tile < 2 * X // T:
        return lambda z: a1y[pl.ds(tile * T * Z + z, T, stride=Z), :]
    at = (tile - 2 * X // T + 2) * T
    return lambda z: a2[z * X * T + at : z * X * T + at + T]


def early_body(
    extra, sc, u_ref, v_ref, ub, vb, c1, south, north, kk, tt, m1, cy, a1, a1y, c2, c2y, a2, pay
):
    k, t = kk[...], tt[...]
    c0, cc2 = classes(sc)
    collide_rows(0, south, north, (south, north), cy, k, t)

    def first(z, _):
        advect_first(z, range(2, X), c1, a1, cy, u_ref, v_ref)
        return 0

    lax.fori_loop(0, 4, first, 0)
    advect_rows(range(1, X - 1), ub, vb, c1, cy, a1y)

    def second(z, _):
        settle_level(z, c0, cc2, a1, m1, c2, k, t)
        return 0

    lax.fori_loop(0, 2, second, 0, unroll=2)
    settle_rows(range(2), ROW_TILES, c0, cc2, a1y, (south, north), c2y, k, t)

    def third(z, _):
        advect_second(z, range(2, X - 2), c2, a2, c2y, u_ref, v_ref)
        return 0

    lax.fori_loop(0, 2, third, 0)
    n0 = sc[0]
    n2 = B - sc[1]
    for tile in range(EARLY):
        level = falling(a1, a1y, a2, tile)
        l0 = level(0)
        packed = fall(c0, cc2, pltpu.roll(l0, n2, 1), l0, level(1))
        pay[tile * T : (tile + 1) * T] = packed
    group = lax.broadcasted_iota(jnp.int32, (T, B), 1) // SPARE
    for j in range(extra):
        out = jnp.zeros((T, B), F32)
        for g in range(GROUPS):
            if j + g * EXTRA < EARLY:
                l0 = falling(a1, a1y, a2, j + g * EXTRA)(0)
                turn = (n2 - n0 + g * SPARE + B) & (B - 1)
                out = jnp.where(group == g, pltpu.roll(l0, turn, 1), out)
        pay[(EARLY + j) * T : (EARLY + j + 1) * T] = out


def late_body(
    extra, sc, u_ref, v_ref, ub, vb, left, right, kk, tt, south, north,
    c1_in, cy_in, m1_in, a1_in, a1y_in, c2_in, c2y_in, a2_in,
    c1, cy, m1, a1, a1y, c2, c2y, a2, pay,
):
    k, t = kk[...], tt[...]
    c0, cc2 = classes(sc)
    m1[0:Y] = left[XROWS : XROWS + Y]
    m1[Y + X * Y :] = right[XROWS : XROWS + Y]
    at_mask = XROWS + 2 * Y
    pieces, masks = [], []
    for ref in (left, right):
        pieces += [ref[0:XROWS], ref[at_mask : at_mask + 2 * Z]]
        masks += [ref[XROWS + d * Y : XROWS + (d + 1) * Y] for d in range(2) for _ in range(Z)]
        masks += [eightfold(ref, at_mask + 2 * Z + side) for side in range(2)]
    c = collide(jnp.concatenate(pieces, axis=0), jnp.concatenate(masks, axis=0), k, t)
    size = XROWS + 2 * Z
    for i, (columns, x) in enumerate((((1, 0), -1), ((XW - 2, XW - 1), X))):
        for d in range(2):
            for z in range(Z):
                at, to = i * size + (d * Z + z) * Y, (z * XW + columns[d]) * Y
                c1[to : to + Y] = c[at : at + Y]
        for side in range(2):
            at, to = i * size + XROWS + side * Z, cy_at(side, 0, x)
            cy[to : to + Z] = c[at : at + Z]

    for z in range(4):
        advect_first(z, EDGE, c1, a1, cy, u_ref, v_ref)
    advect_rows((0, X - 1), ub, vb, c1, cy, a1y)
    settle_edges(range(2), c0, cc2, a1, m1, c2, k, t)
    settle_rows(range(2), ROW_EDGES, c0, cc2, a1y, (south, north), c2y, k, t)
    for z in range(2):
        advect_second(z, ENDING, c2, a2, c2y, u_ref, v_ref)
    tiles = [[a1[(z * XA + x) * T : (z * XA + x + 1) * T] for z in range(2)] for x in EDGE]
    ends = (0, X - 1, X, 2 * X - 1)
    tiles.append(
        [
            jnp.concatenate(
                [a1y[row * Z + z : row * Z + z + 1] for row in ends] + [jnp.zeros((T - 4, B), F32)],
                axis=0,
            )
            for z in range(2)
        ]
    )
    tiles += [[a2[(z * X + x) * T : (z * X + x + 1) * T] for z in range(2)] for x in ENDING]
    for i, (l0, l1) in enumerate(tiles):
        own = l0 if extra else pltpu.roll(l0, B - sc[1], 1)
        pay[i * T : (i + 1) * T] = fall(c0, cc2, own, l0, l1)
        if extra:
            pay[(LATE + i) * T : (LATE + i + 1) * T] = l0


def fall_out(z, columns, c0, cc2, a2, res):
    for i in columns:
        at, step = (z * X + i) * T, X * T
        res[at : at + T] = fall(
            c0, cc2, *(a2[at + k * step : at + k * step + T] for k in range(H_MAX + 1))
        )


def between_body(
    sc, u_ref, v_ref, ub, vb, kk, tt, south, north, south1, north1, c1, m1,
    cy_in, a1_in, a1y_in, c2_in, c2y_in, a2_in,
    cy, a1, a1y, c2, c2y, a2, res,
):
    k, t = kk[...], tt[...]
    c0, cc2 = classes(sc)
    collide_rows(1, south1, north1, (south, north), cy, k, t)

    def first(z, _):
        advect_first(z, range(2, X), c1, a1, cy, u_ref, v_ref)
        return 0

    lax.fori_loop(4, 8, first, 0)
    advect_rows(range(1, X - 1), ub, vb, c1, cy, a1y)

    def second(z, _):
        settle_level(z, c0, cc2, a1, m1, c2, k, t)
        return 0

    lax.fori_loop(2, 6, second, 0, unroll=4)
    settle_rows(range(2, 6), ROW_TILES, c0, cc2, a1y, (south, north), c2y, k, t)

    def third(z, _):
        advect_second(z, range(2, X - 2), c2, a2, c2y, u_ref, v_ref)
        return 0

    lax.fori_loop(2, 6, third, 0)
    for z in range(4):
        fall_out(z, range(2, X - 2), c0, cc2, a2, res)


def rest_body(
    sc, u_ref, v_ref, kk, tt, south, north, c1, m1, cy, a1y,
    a1_in, c2_in, c2y_in, a2_in, res_in,
    a1, c2, c2y, a2, res,
):
    k, t = kk[...], tt[...]
    c0, cc2 = classes(sc)
    for z in range(4, 8):
        advect_first(z, EDGE, c1, a1, cy, u_ref, v_ref)
    settle_edges(range(2, 6), c0, cc2, a1, m1, c2, k, t)
    settle_rows(range(2, 6), ROW_EDGES, c0, cc2, a1y, (south, north), c2y, k, t)
    for z in range(2, 6):
        advect_second(z, ENDING, c2, a2, c2y, u_ref, v_ref)
    for z in range(4):
        fall_out(z, ENDING, c0, cc2, a2, res)


def unpacking(extra, sc):
    n0, start2 = sc[0], sc[1]
    within = lax.broadcasted_iota(jnp.int32, (T, B), 1) < start2 + n0

    def early(ref, tile):
        m = ref[tile * T : (tile + 1) * T]
        p6 = pltpu.roll(m, start2, 1)
        if extra:
            g, j = divmod(tile, EXTRA)
            spare = ref[(EARLY + j) * T : (EARLY + j + 1) * T]
            turn = (n0 + start2 - g * SPARE + B) & (B - 1)
            p6 = jnp.where(within, p6, pltpu.roll(spare, turn, 1))
        return m, p6

    def late(ref, i):
        m = ref[i * T : (i + 1) * T]
        return m, ref[(LATE + i) * T : (LATE + i + 1) * T] if extra else pltpu.roll(m, start2, 1)

    return early, late


def settle_top(columns, above, c0, cc2, a1, c2):
    for i in columns:
        p7, p6 = above(i)
        x6, x7 = (a1[(z * XA + i) * T : (z * XA + i + 1) * T] for z in (6, 7))
        c2[(6 * XA + i) * T : (6 * XA + i + 1) * T] = fall(c0, cc2, x6, x7, p6)
        c2[(7 * XA + i) * T : (7 * XA + i + 1) * T] = jnp.where(c0, x7, p7)


def settle_top_rows(tiles, row7, row6, c0, cc2, a1y, c2y):
    for i in tiles:
        x6, x7 = (a1y[pl.ds(i * T * Z + z, T, stride=Z), :] for z in (6, 7))
        at = 6 * 2 * X + i * T
        c2y[at : at + T] = fall(c0, cc2, x6, x7, row6[i * T : (i + 1) * T])
        c2y[at + 2 * X : at + 2 * X + T] = jnp.where(c0, x7, row7[i * T : (i + 1) * T])


def fall_top(z, i, above, c0, cc2, a2):
    x = [a2[(k * X + i) * T : (k * X + i + 1) * T] for k in range(z, min(z + 3, Z))]
    if z > 5:
        p7, p6 = above(i)
        x = x + [p6] if z == 6 else x + [p7, p7]
    return fall(c0, cc2, *x)


def upper_body(
    extra, sc, u_ref, v_ref, kk, tt, south, north, m1, a1, a1y, early, low, c2_in, c2y_in, a2_in,
    out, c2, c2y, a2, row7, row6, res, sem,
):
    k, t = kk[...], tt[...]
    c0, cc2 = classes(sc)
    copies = [pltpu.make_async_copy(low, out.at[pl.ds(0, 4 * X * T)], sem.at[4])]
    copies[0].start()
    unpack, _ = unpacking(extra, sc)
    settle_top(range(2, X), lambda i: unpack(early, i - 2), c0, cc2, a1, c2)
    for i in ROW_TILES:
        row7[i * T : (i + 1) * T], row6[i * T : (i + 1) * T] = unpack(early, X - 2 + i)
    settle_top_rows(ROW_TILES, row7, row6, c0, cc2, a1y, c2y)
    mask = jnp.concatenate([south[HALF : HALF + X], north[HALF : HALF + X]] * 2, axis=0)
    at = slice(12 * X, 16 * X)
    c2y[at] = collide(c2y[at], mask, k, t)
    for z in (6, 7):
        at = slice((z * XA + 2) * T, (z * XA + X) * T)
        c2[at] = collide(c2[at], m1[2 * T : X * T], k, t)
    columns = range(2, X - 2)
    for z in (6, 7):
        advect_second(z, columns, c2, a2, c2y, u_ref, v_ref)
    above = lambda i: unpack(early, X - 2 + 2 * X // T + i - 2)
    for z in range(4, 8):
        for i in columns:
            at = ((z - 4) * X + i) * T
            res[at : at + T] = fall_top(z, i, above, c0, cc2, a2)
        n = len(columns) * T
        copies.append(
            pltpu.make_async_copy(
                res.at[pl.ds(((z - 4) * X + 2) * T, n)],
                out.at[pl.ds((z * X + 2) * T, n)],
                sem.at[z - 4],
            )
        )
        copies[-1].start()
    for copy in copies:
        copy.wait()


def last_body(
    extra, sc, u_ref, v_ref, kk, tt, south, north, m1, a1, a1y, row7_in, row6_in, late, out_in,
    c2_in, c2y_in, a2_in, out, c2, c2y, a2, res, sem,
):
    k, t = kk[...], tt[...]
    c0, cc2 = classes(sc)
    _, unpack = unpacking(extra, sc)
    settle_top(EDGE, lambda i: unpack(late, EDGE.index(i)), c0, cc2, a1, c2)
    p7, p6 = unpack(late, 4)
    lane_row = lax.broadcasted_iota(jnp.int32, (T, B), 0)
    fixed = {}
    for i, tile in enumerate(ROW_EDGES):
        row = lane_row == (T - 1 if i % 2 else 0)
        fixed[tile] = [
            jnp.where(row, p[i : i + 1], ref[tile * T : (tile + 1) * T])
            for p, ref in ((p7, row7_in), (p6, row6_in))
        ]
    where, pieces, cloudy = [], [], []
    for z in (6, 7):
        for i in EDGE:
            where.append((c2, (z * XA + i) * T))
            pieces.append(c2[where[-1][1] : where[-1][1] + T])
            cloudy.append(m1[i * T : (i + 1) * T])
    for tile in ROW_EDGES:
        x6, x7 = (a1y[pl.ds(tile * T * Z + z, T, stride=Z), :] for z in (6, 7))
        side, first = divmod(tile * T, X)
        mask = (south, north)[side][HALF + first : HALF + first + T]
        for z, value in ((6, fall(c0, cc2, x6, x7, fixed[tile][1])), (7, jnp.where(c0, x7, fixed[tile][0]))):
            where.append((c2y, z * 2 * X + tile * T))
            pieces.append(value)
            cloudy.append(mask)
    c = collide(jnp.concatenate(pieces, axis=0), jnp.concatenate(cloudy, axis=0), k, t)
    for i, (ref, to) in enumerate(where):
        ref[to : to + T] = c[i * T : (i + 1) * T]
    for z in (6, 7):
        advect_second(z, ENDING, c2, a2, c2y, u_ref, v_ref)
    above = lambda i: unpack(late, 5 + ENDING.index(i))
    copies = []
    for z in range(4, 8):
        for half in range(2):
            at = ((z - 4) * 2 + half) * 2 * T
            for j in range(2):
                i = ENDING[half * 2 + j]
                res[at + j * T : at + (j + 1) * T] = fall_top(z, i, above, c0, cc2, a2)
            to = out.at[pl.ds((z * X + ENDING[half * 2]) * T, 2 * T)]
            copies.append(
                pltpu.make_async_copy(res.at[pl.ds(at, 2 * T)], to, sem.at[(z - 4) * 2 + half])
            )
            copies[-1].start()
    for copy in copies:
        copy.wait()


def ring(axis, step):
    n = lax.axis_size(axis)
    return [(i, (i + step) % n) for i in range(n)]


def below(value):
    return lax.ppermute(value, "gz", [(i, i - 1) for i in range(1, lax.axis_size("gz"))])


def packed(extra, scalars, drops, capture, transfer, courant_u, courant_v, fall_class, cloud_mask):
    drops = drops.reshape(Z * X * Y, B)
    ub = jnp.broadcast_to(courant_u[:, None], (Z, B))
    vb = jnp.broadcast_to(courant_v[:, None], (Z, B))
    v = lambda n, d=F32: ((n, B), d, True)
    weights = [((2 * B, 2 * B), BF16, True)] * 2
    own, m1, ym0, ym1, yp0, yp1, kk, tt = call(
        edges_body,
        [v(Z * X * Y), v(XA * Y), v(ENDS + T), v(HALF), v(ENDS + T), v(HALF)] + weights,
        [drops, cloud_mask.T, capture, transfer],
        [HBM] * 4,
        [pltpu.VMEM((Y, X), jnp.int32), pltpu.VMEM((B, B), F32), pltpu.VMEM((B, B), F32), pltpu.SemaphoreType.DMA((Z + 3,))],
        cost=(1000, 4 << 20),
    )
    south0 = lax.ppermute(yp0, "gy", ring("gy", 1))
    north0 = lax.ppermute(ym0, "gy", ring("gy", -1))
    south1 = lax.ppermute(yp1, "gy", ring("gy", 1))
    north1 = lax.ppermute(ym1, "gy", ring("gy", -1))
    c1, kk, tt = call(
        own_body, [v(Z * XW * Y)], [own, m1, kk, tt], [VMEM] * 4, cost=(3 << 30, 8 << 20), keep=(2, 3)
    )
    shapes = [v(4 * XA * Z), v(Z * XA * T), v(2 * X * Z), v(Z * XA * T), v(Z * 2 * X), v(Z * X * T)]
    cy, a1, a1y, c2, c2y, a2, pay, kk, tt = call(
        functools.partial(early_body, extra),
        shapes + [v((EARLY + extra) * T)],
        [*scalars, ub, vb, c1, south0, north0, kk, tt, m1],
        [SMEM] * 3 + [VMEM] * 8,
        cost=(3 << 30, 8 << 20),
        keep=(8, 9),
    )
    pay, south1, north1 = lax.optimization_barrier((pay, south1, north1))
    early = below(pay)
    xm, xp = call(
        sides_body,
        [v(XMESSAGE)] * 2,
        [own, m1, south0, north0],
        [VMEM] * 4,
        cost=(1000, 1 << 18),
    )
    left = lax.ppermute(xp, "gx", ring("gx", 1))
    right = lax.ppermute(xm, "gx", ring("gx", -1))
    cy, a1, a1y, c2, c2y, a2, res, kk, tt = call(
        between_body,
        shapes + [v(4 * X * T)],
        [*scalars, ub, vb, kk, tt, south0, north0, south1, north1, c1, m1, cy, a1, a1y, c2, c2y, a2],
        [SMEM] * 3 + [VMEM] * 16,
        cost=(3 << 30, 8 << 20),
        aliases={13 + i: i for i in range(6)},
        keep=(5, 6),
    )
    c1, cy, m1, a1, a1y, c2, c2y, a2, pay, kk, tt = call(
        functools.partial(late_body, extra),
        [v(Z * XW * Y), shapes[0], v(XA * Y)] + shapes[1:] + [v((2 if extra else 1) * LATE * T)],
        [*scalars, ub, vb, left, right, kk, tt, south0, north0, c1, cy, m1, a1, a1y, c2, c2y, a2],
        [SMEM] * 3 + [VMEM] * 16,
        cost=(1 << 28, 1 << 20),
        aliases={11 + i: i for i in range(8)},
        keep=(7, 8),
    )
    late = below(pay)
    a1, c2, c2y, a2, res, kk, tt = call(
        rest_body,
        [shapes[1], *shapes[3:], v(4 * X * T)],
        [*scalars, kk, tt, south0, north0, c1, m1, cy, a1y, a1, c2, c2y, a2, res],
        [SMEM] * 3 + [VMEM] * 13,
        cost=(1 << 29, 1 << 20),
        aliases={11 + i: i for i in range(5)},
        keep=(3, 4),
    )
    out, c2, c2y, a2, row7, row6, kk, tt = call(
        functools.partial(upper_body, extra),
        [((Z * X * Y, B), F32, False), *shapes[3:], v(2 * X), v(2 * X)],
        [*scalars, kk, tt, south0, north0, m1, a1, a1y, early, res, c2, c2y, a2],
        [SMEM] * 3 + [VMEM] * 12,
        [pltpu.VMEM((4 * X * T, B), F32), pltpu.SemaphoreType.DMA((5,))],
        cost=(3 << 30, 8 << 20),
        out_specs=[HBM] + [VMEM] * 5,
        aliases={12: 1, 13: 2, 14: 3},
        keep=(3, 4),
    )
    out, *_ = call(
        functools.partial(last_body, extra),
        [((Z * X * Y, B), F32, False), *shapes[3:]],
        [*scalars, kk, tt, south0, north0, m1, a1, a1y, row7, row6, late, out, c2, c2y, a2],
        [SMEM] * 3 + [VMEM] * 10 + [HBM] + [VMEM] * 3,
        [pltpu.VMEM((4 * len(ENDING) * T, B), F32), pltpu.SemaphoreType.DMA((8,))],
        cost=(1 << 28, 1 << 20),
        out_specs=[HBM] + [VMEM] * 3,
        aliases={13: 0, 14: 1, 15: 2, 16: 3},
    )
    return out.reshape(Z, X, Y, B)


def passed_along(block, axis, distance):
    devices = range(lax.axis_size(axis))
    route = [(i - distance, i) for i in devices if i - distance in devices]
    return lax.ppermute(block, axis, route)


def with_halo(value, sides, width):
    edges = {}
    for axis, dim in sides:
        devices, length = (lax.axis_size(axis), value.shape[dim])
        up = [(i, (i + 1) % devices) for i in range(devices)]
        last = lax.slice_in_dim(value, length - width, length, axis=dim)
        leading = lax.slice_in_dim(value, 0, width, axis=dim)
        edges[dim] = (
            lax.ppermute(last, axis, up),
            lax.ppermute(leading, axis, [(b, a) for a, b in up]),
        )
    done = []
    for _, dim in sides:
        low, high = edges[dim]
        around = [(width, width) if d in done else (0, 0) for d in range(value.ndim)]
        value = jnp.concatenate([jnp.pad(low, around), value, jnp.pad(high, around)], axis=dim)
        done.append(dim)
    return value


def collide_plain(particle_distribution, capture_efficiency_matrix, transfer, cloudy):
    merger_speed = jnp.einsum(
        "ugcr,mr->ugcm",
        particle_distribution,
        capture_efficiency_matrix,
        precision=lax.Precision.HIGHEST,
    )
    water_removed = particle_distribution * merger_speed
    mass_gain = jnp.einsum(
        "zxyi,ik->zxyk", water_removed, transfer, precision=lax.Precision.HIGHEST
    )
    return particle_distribution + cloudy[None, :, :, None] * (mass_gain - water_removed)


def advect_plain(with_edges, courant_u, courant_v):
    centre = with_edges[:, 1:-1, 1:-1]
    west_side = with_edges[:, :-2, 1:-1]
    east_side = with_edges[:, 2:, 1:-1]
    south_side = with_edges[:, 1:-1, :-2]
    north_side = with_edges[:, 1:-1, 2:]
    x_plus = jnp.maximum(courant_u, 0.0)[:, None, None, None]
    x_minus = jnp.minimum(courant_u, 0.0)[:, None, None, None]
    northward_neighbor = jnp.maximum(courant_v, 0.0)[:, None, None, None]
    y_minus = jnp.minimum(courant_v, 0.0)[:, None, None, None]
    result = centre - x_plus * (centre - west_side) - x_minus * (east_side - centre)
    return result - northward_neighbor * (centre - south_side) - y_minus * (north_side - centre)


def sediment(padded, fall_class, levels):
    result = padded[:levels]
    for fall_depth in range(1, H_MAX + 1):
        result = jnp.where(
            (fall_class == fall_depth)[None, None, None, :],
            padded[fall_depth : fall_depth + levels],
            result,
        )
    return result


def plain(
    drops, capture_efficiency_matrix, transfer, courant_u, courant_v, fall_class, cloud_mask
):
    cloudy = cloud_mask.astype(jnp.float32)
    reach = STEPS * H_MAX
    from_above, upper_u, upper_v = passed_along(
        (drops[:reach], courant_u[:reach], courant_v[:reach]), "gz", -1
    )
    particle_distribution = jnp.concatenate([drops, from_above], axis=0)
    column_u = jnp.concatenate([courant_u, upper_u], axis=0)
    column_v = jnp.concatenate([courant_v, upper_v], axis=0)
    for repeat in range(STEPS):
        current = particle_distribution.shape[0]
        coalesced_drops = collide_plain(
            particle_distribution, capture_efficiency_matrix, transfer, cloudy
        )
        with_edges = with_halo(coalesced_drops, (("gx", 1), ("gy", 2)), 1)
        advected = advect_plain(with_edges, column_u[:current], column_v[:current])
        particle_distribution = sediment(advected, fall_class, current - H_MAX)
    return particle_distribution


def on_device(*args):
    way, *scalars = call(
        count_body,
        [((1,), jnp.int32, pltpu.SMEM), ((2,), jnp.int32, pltpu.SMEM)] + [((Z,), F32, pltpu.SMEM)] * 2,
        [args[5].reshape(1, B), args[3], args[4]],
        [HBM] * 3,
        [pltpu.VMEM((1, B), jnp.int32), pltpu.SemaphoreType.DMA((3,))],
        out_specs=[SMEM] * 4,
    )
    ways = (
        lambda s, *a: plain(*a),
        lambda s, *a: packed(EXTRA, s, *a),
        lambda s, *a: packed(0, s, *a),
    )
    return lax.switch(way.reshape(()), ways, scalars, *args)


def solution(mesh):
    in_specs = (P("gz", "gx", "gy", None), P(), P(), P("gz"), P("gz"), P(), P("gx", "gy"))
    out_specs = P("gz", "gx", "gy", None)
    return jax.shard_map(
        on_device, mesh=mesh, in_specs=in_specs, out_specs=out_specs, check_vma=False
    )
```

```python
import functools

import jax
import jax.numpy as jnp
from jax import lax
from jax.experimental import pallas as pl
from jax.experimental.pallas import tpu as pltpu
from jax.sharding import PartitionSpec as P

H_MAX = 2
Z, X, Y, B = 8, 64, 8, 128
T = 8
XW = X + 4
XA = X + 2
LOW = Z // 2
HALF = 2 * LOW * X
ENDS = HALF + 2 * X
XROWS = 2 * Z * Y
EARLY = (X - 2) + 2 * X // T + (X - 4)
SPARES = (0, 8, 24, B)
LATE = 4 + 1 + 4
EDGE = (0, 1, XA - 2, XA - 1)
ENDING = (0, 1, X - 2, X - 1)
ROW_TILES = range(2 * X // T)
ROW_EDGES = (0, X // T - 1, X // T, 2 * X // T - 1)
F32, BF16 = jnp.float32, jnp.bfloat16

VMEM = pl.BlockSpec(memory_space=pltpu.VMEM)
SMEM = pl.BlockSpec(memory_space=pltpu.SMEM)
HBM = pl.BlockSpec(memory_space=pltpu.HBM)


def rows(start, n=T):
    return pl.ds(start if isinstance(start, int) else pl.multiple_of(start, T), n)


def call(body, outs, args, specs, scratch=(), cost=(0, 0), out_specs=None, aliases=None, keep=()):
    shapes = [
        pltpu.VMEM(s, d) if m is True else m(s, d) if m else jax.ShapeDtypeStruct(s, d)
        for s, d, m in outs
    ]
    shapes += [pltpu.VMEM(args[i].shape, args[i].dtype) for i in keep]
    n_in, n_out = len(args), len(outs)
    aliases = {**(aliases or {}), **{i: n_out + k for k, i in enumerate(keep)}}

    def kernel(*refs):
        body(*refs[: n_in + n_out], *refs[n_in + n_out + len(keep) :])

    args = [
        pltpu.with_memory_space_constraint(a, s.memory_space)
        for a, s in zip(args, specs)
    ]
    return pl.pallas_call(
        kernel,
        out_shape=shapes,
        in_specs=list(specs),
        out_specs=(out_specs or [VMEM] * len(outs)) + [VMEM] * len(keep),
        scratch_shapes=list(scratch),
        input_output_aliases=aliases,
        cost_estimate=pl.CostEstimate(flops=cost[0], bytes_accessed=cost[1], transcendentals=0),
        compiler_params=pltpu.CompilerParams(vmem_limit_bytes=8 << 20),
    )(*args)


def split(x):
    high = x.astype(BF16)
    return high, (x - high.astype(F32)).astype(BF16)


def product(x, weights):
    out = jnp.dot(jnp.concatenate(split(x), axis=1), weights, preferred_element_type=F32)
    return out[:, :B] + out[:, B:]


def collide(s, cloudy, capture, transfer):
    loss = s * product(s, capture)
    return s + cloudy * (product(loss, transfer) - loss)


def eightfold(ref, row):
    return ref[pl.ds(row, T, stride=0), :]


def repeated(ref, start, n):
    return jnp.concatenate([eightfold(ref, start + i) for i in range(n)], axis=0)


def classes(sc_ref):
    lane = lax.broadcasted_iota(jnp.int32, (T, B), 1)
    return lane < sc_ref[0], lane >= sc_ref[1]


def fall(c0, c2, a, b, c):
    return jnp.where(c0, a, jnp.where(c2, c, b))


def count_body(falls, u_in, v_in, way, out, u, v, ref, sem):
    copies = [
        pltpu.make_async_copy(a, b, sem.at[i])
        for i, (a, b) in enumerate(((falls, ref), (u_in, u), (v_in, v)))
    ]
    for copy in copies:
        copy.start()
    for copy in copies:
        copy.wait()
    n0 = jnp.sum((ref[...] == 0).astype(jnp.int32))
    n2 = jnp.sum((ref[...] == H_MAX).astype(jnp.int32))
    out[0] = n0
    out[1] = B - n2
    way[0] = sum((n2 - n0 > spare).astype(jnp.int32) for spare in SPARES[:-1])


def edges_body(drops, cloud, k_in, t_in, own, m1, ym0, ym1, yp0, yp1, kk, tt, mask, k_ref, t_ref, sem):
    level = lambda z: pl.ds(z * X * Y, X * Y)
    copies = [
        pltpu.make_async_copy(a, b, sem.at[i])
        for i, (a, b) in enumerate(
            [(drops.at[level(z)], own.at[level(z)]) for z in range(Z)]
            + [(cloud, mask), (k_in, k_ref), (t_in, t_ref)]
        )
    ]
    for copy in copies[Z:] + copies[:Z]:
        copy.start()
    copies[Z].wait()
    columns = mask[...].astype(F32)
    for x in range(X):
        m1[(x + 1) * Y : (x + 2) * Y] = jnp.broadcast_to(columns[:, x : x + 1], (Y, B))
    for i, (ref, out, turned) in enumerate(((k_ref, kk, True), (t_ref, tt, False))):
        copies[Z + 1 + i].wait()
        w = ref[...].T if turned else ref[...]
        high, low = split(w)
        half = jnp.concatenate([high, low], axis=1)
        out[...] = jnp.concatenate([half, half], axis=0)
    for out, ys in ((ym0, (0, 1)), (yp0, (Y - 1, Y - 2))):
        for d, y in enumerate(ys):
            out[HALF + d * X : HALF + (d + 1) * X] = m1[pl.ds(Y + y, X, stride=Y), :]
    for z in range(Z):
        copies[z].wait()
        for outs, ys in (((ym0, ym1), (0, 1)), ((yp0, yp1), (Y - 1, Y - 2))):
            for d, y in enumerate(ys):
                at = (d * LOW + z % LOW) * X
                outs[z // LOW][at : at + X] = own[pl.ds(z * X * Y + y, X, stride=Y), :]
    for out, y in ((ym0, 0), (yp0, Y - 1)):
        for i, x in enumerate((0, X - 1)):
            at, start = ENDS + i * LOW, (LOW * X + x) * Y + y
            out[at : at + LOW] = own[pl.ds(start, LOW, stride=X * Y), :]


def sides_body(own, m1, south, north, first, second):
    even = lax.axis_index("gx") % 2 == 0
    for out, to_right in ((first, even), (second, jnp.logical_not(even))):
        edge = jnp.where(to_right, X - 1, 0)
        inward = jnp.where(to_right, -1, 1)
        for d in range(2):
            x = edge + d * inward
            out[XROWS + d * Y : XROWS + (d + 1) * Y] = m1[rows((x + 1) * Y)]
            for z in range(Z):
                out[(d * Z + z) * Y : (d * Z + z + 1) * Y] = own[rows((z * X + x) * Y)]
        at = XROWS + 2 * Y
        out[at + 2 * Z :] = jnp.zeros((T, B), F32)
        for side, ref in enumerate((south, north)):
            row = at + side * Z
            end = ENDS + jnp.where(to_right, LOW, 0)
            out[row : row + LOW] = ref[pl.ds(edge, LOW, stride=X), :]
            out[row + LOW : row + Z] = ref[pl.ds(end, LOW), :]
            row = at + 2 * Z + side
            out[row : row + 1] = ref[pl.ds(HALF + edge, 1), :]


XMESSAGE = XROWS + 2 * Y + 2 * Z + T


def own_body(own, m1, kk, tt, c1):
    k, t, mask = kk[...], tt[...], m1[Y : Y + X * Y]

    def level(z, _):
        c1[rows((z * XW + 2) * Y, X * Y)] = collide(own[rows(z * X * Y, X * Y)], mask, k, t)
        return 0

    lax.fori_loop(0, Z, level, 0, unroll=4)


def cy_at(side, d, x):
    return ((side * 2 + d) * XA + x + 1) * Z


def collide_rows(part, south, north, masks, cy, k, t):
    for side, (ref, mask_ref) in enumerate(zip((south, north), masks)):
        for d in range(2):
            mask = jnp.concatenate([mask_ref[HALF + d * X : HALF + (d + 1) * X]] * LOW, axis=0)
            c = collide(ref[d * LOW * X : (d + 1) * LOW * X], mask, k, t)
            for z in range(LOW):
                cy[pl.ds(cy_at(side, d, 0) + part * LOW + z, X, stride=Z), :] = c[z * X : (z + 1) * X]


def upwind(z, u_ref, v_ref):
    u, v = u_ref[z], v_ref[z]
    at_edge = lax.broadcasted_iota(jnp.int32, (T, B), 0) == jnp.where(v > 0, 0, T - 1)
    return (
        jnp.abs(u),
        jnp.abs(v),
        jnp.where(u > 0, -Y, Y),
        jnp.where(v > 0, 1, T - 1),
        jnp.where(v > 0, 0, 1),
        at_edge,
    )


def advect(z, columns, c_ref, width, first, out_ref, out_width, edge, u_ref, v_ref):
    au, av, step, shift, side, at_edge = upwind(z, u_ref, v_ref)
    base, base_out = (z * width + first) * Y, z * out_width * Y
    edge_ref, edge_at, edge_stride = edge(z, side)
    for i in columns:
        c = c_ref[rows(base + i * Y)]
        x = c_ref[rows(base + step + i * Y)]
        e = eightfold(edge_ref, edge_at + i * edge_stride)
        y = jnp.where(at_edge, e, pltpu.roll(c, shift, 0))
        out_ref[rows(base_out + i * Y)] = c - au * (c - x) - av * (c - y)


def advect_first(z, columns, c1, a1, cy, u_ref, v_ref):
    edge = lambda z, side: (cy, side * (2 * XA * Z) + z, Z)
    advect(z, columns, c1, XW, 1, a1, XA, edge, u_ref, v_ref)


def advect_second(z, columns, c2, a2, c2y, u_ref, v_ref):
    edge = lambda z, side: (c2y, (z * 2 + side) * X, 1)
    advect(z, columns, c2, XA, 1, a2, X, edge, u_ref, v_ref)


def advect_rows(columns, ub, vb, c1, cy, a1y):
    au, av = jnp.abs(ub[...]), jnp.abs(vb[...])
    upos, vpos = ub[...] > 0, vb[...] > 0
    for side in range(2):
        for x in columns:
            at, far = cy_at(side, 0, x), cy_at(side, 1, x)
            c = cy[at : at + Z]
            xx = jnp.where(upos, cy[at - Z : at], cy[at + Z : at + 2 * Z])
            outer = cy[far : far + Z]
            inner = c1[pl.ds((x + 2) * Y + (Y - 1) * side, Z, stride=XW * Y), :]
            yy = jnp.where(vpos, *((outer, inner) if side == 0 else (inner, outer)))
            to = (side * X + x) * Z
            a1y[to : to + Z] = c - au * (c - xx) - av * (c - yy)


def settle(z, columns, c0, cc2, a1, c2):
    for i in columns:
        at = (z * XA + i) * T
        step = XA * T
        c2[rows(at)] = fall(c0, cc2, a1[rows(at)], a1[rows(at + step)], a1[rows(at + 2 * step)])


def settle_level(z, c0, cc2, a1, m1, c2, k, t):
    settle(z, range(XA), c0, cc2, a1, c2)
    at = rows(z * XA * T, XA * T)
    c2[at] = collide(c2[at], m1[...], k, t)


def settle_rows(levels, tiles, c0, cc2, a1y, masks, c2y, k, t):
    pieces, cloudy, where = [], [], []
    for z in levels:
        for i in tiles:
            a = [a1y[pl.ds(i * T * Z + z + j, T, stride=Z), :] for j in range(H_MAX + 1)]
            pieces.append(fall(c0, cc2, *a))
            side, first = divmod(i * T, X)
            cloudy.append(masks[side][HALF + first : HALF + first + T])
            where.append(z * 2 * X + i * T)
    c = collide(jnp.concatenate(pieces, axis=0), jnp.concatenate(cloudy, axis=0), k, t)
    for i, to in enumerate(where):
        c2y[to : to + T] = c[i * T : (i + 1) * T]


def settle_edges(levels, c0, cc2, a1, m1, c2, k, t):
    for z in levels:
        settle(z, EDGE, c0, cc2, a1, c2)
    tiles = [(z * XA + i) * T for z in levels for i in EDGE]
    c = collide(
        jnp.concatenate([c2[at : at + T] for at in tiles], axis=0),
        jnp.concatenate([m1[i * T : (i + 1) * T] for i in EDGE] * len(levels), axis=0),
        k,
        t,
    )
    for i, at in enumerate(tiles):
        c2[at : at + T] = c[i * T : (i + 1) * T]


def falling(a1, a1y, a2, tile):
    if tile < X - 2:
        at = (tile + 2) * T
        return lambda z: a1[z * XA * T + at : z * XA * T + at + T]
    tile -= X - 2
    if tile < 2 * X // T:
        return lambda z: a1y[pl.ds(tile * T * Z + z, T, stride=Z), :]
    at = (tile - 2 * X // T + 2) * T
    return lambda z: a2[z * X * T + at : z * X * T + at + T]


def early_body(
    spare, sc, u_ref, v_ref, ub, vb, c1, south, north, kk, tt, m1, cy, a1, a1y, c2, c2y, a2, pay
):
    k, t = kk[...], tt[...]
    c0, cc2 = classes(sc)
    collide_rows(0, south, north, (south, north), cy, k, t)

    def first(z, _):
        advect_first(z, range(2, X), c1, a1, cy, u_ref, v_ref)
        return 0

    lax.fori_loop(0, 4, first, 0)
    advect_rows(range(1, X - 1), ub, vb, c1, cy, a1y)

    def second(z, _):
        settle_level(z, c0, cc2, a1, m1, c2, k, t)
        return 0

    lax.fori_loop(0, 2, second, 0, unroll=2)
    settle_rows(range(2), ROW_TILES, c0, cc2, a1y, (south, north), c2y, k, t)

    def third(z, _):
        advect_second(z, range(2, X - 2), c2, a2, c2y, u_ref, v_ref)
        return 0

    lax.fori_loop(0, 2, third, 0)
    n0 = sc[0]
    n2 = B - sc[1]
    for tile in range(EARLY):
        level = falling(a1, a1y, a2, tile)
        l0 = level(0)
        packed = fall(c0, cc2, pltpu.roll(l0, n2, 1), l0, level(1))
        pay[tile * T : (tile + 1) * T] = packed
    tiles = spare_tiles(spare)
    lane = lax.broadcasted_iota(jnp.int32, (T, B), 1)
    for j in range(tiles):
        out = jnp.zeros((T, B), F32)
        for g in range(B // spare):
            if j + g * tiles < EARLY:
                l0 = falling(a1, a1y, a2, j + g * tiles)(0)
                turn = (n2 - n0 + g * spare + B) & (B - 1)
                here = (lane >= g * spare) & (lane < (g + 1) * spare)
                out = jnp.where(here, pltpu.roll(l0, turn, 1), out)
        pay[(EARLY + j) * T : (EARLY + j + 1) * T] = out


def late_body(
    spare, sc, u_ref, v_ref, ub, vb, first, second, kk, tt, south, north,
    c1_in, cy_in, m1_in, a1_in, a1y_in, c2_in, c2y_in, a2_in,
    c1, cy, m1, a1, a1y, c2, c2y, a2, pay, sides,
):
    k, t = kk[...], tt[...]
    c0, cc2 = classes(sc)
    even = lax.axis_index("gx") % 2 == 0
    for to, a, b in ((sides.at[0], second, first), (sides.at[1], first, second)):
        to[...] = jnp.where(even, a[...], b[...])
    left, right = sides.at[0], sides.at[1]
    m1[0:Y] = left[XROWS : XROWS + Y]
    m1[Y + X * Y :] = right[XROWS : XROWS + Y]
    at_mask = XROWS + 2 * Y
    pieces, masks = [], []
    for ref in (left, right):
        pieces += [ref[0:XROWS], ref[at_mask : at_mask + 2 * Z]]
        masks += [ref[XROWS + d * Y : XROWS + (d + 1) * Y] for d in range(2) for _ in range(Z)]
        masks += [eightfold(ref, at_mask + 2 * Z + side) for side in range(2)]
    c = collide(jnp.concatenate(pieces, axis=0), jnp.concatenate(masks, axis=0), k, t)
    size = XROWS + 2 * Z
    for i, (columns, x) in enumerate((((1, 0), -1), ((XW - 2, XW - 1), X))):
        for d in range(2):
            for z in range(Z):
                at, to = i * size + (d * Z + z) * Y, (z * XW + columns[d]) * Y
                c1[to : to + Y] = c[at : at + Y]
        for side in range(2):
            at, to = i * size + XROWS + side * Z, cy_at(side, 0, x)
            cy[to : to + Z] = c[at : at + Z]

    for z in range(4):
        advect_first(z, EDGE, c1, a1, cy, u_ref, v_ref)
    advect_rows((0, X - 1), ub, vb, c1, cy, a1y)
    settle_edges(range(2), c0, cc2, a1, m1, c2, k, t)
    settle_rows(range(2), ROW_EDGES, c0, cc2, a1y, (south, north), c2y, k, t)
    for z in range(2):
        advect_second(z, ENDING, c2, a2, c2y, u_ref, v_ref)
    tiles = [[a1[(z * XA + x) * T : (z * XA + x + 1) * T] for z in range(2)] for x in EDGE]
    ends = (0, X - 1, X, 2 * X - 1)
    tiles.append(
        [
            jnp.concatenate(
                [a1y[row * Z + z : row * Z + z + 1] for row in ends] + [jnp.zeros((T - 4, B), F32)],
                axis=0,
            )
            for z in range(2)
        ]
    )
    tiles += [[a2[(z * X + x) * T : (z * X + x + 1) * T] for z in range(2)] for x in ENDING]
    for i, (l0, l1) in enumerate(tiles):
        own = l0 if spare else pltpu.roll(l0, B - sc[1], 1)
        pay[i * T : (i + 1) * T] = fall(c0, cc2, own, l0, l1)
        if spare:
            pay[(LATE + i) * T : (LATE + i + 1) * T] = l0


def fall_out(z, columns, c0, cc2, a2, res):
    for i in columns:
        at, step = (z * X + i) * T, X * T
        res[at : at + T] = fall(
            c0, cc2, *(a2[at + k * step : at + k * step + T] for k in range(H_MAX + 1))
        )


def between_body(
    sc, u_ref, v_ref, ub, vb, kk, tt, south, north, south1, north1, c1, m1,
    cy_in, a1_in, a1y_in, c2_in, c2y_in, a2_in,
    cy, a1, a1y, c2, c2y, a2, res,
):
    k, t = kk[...], tt[...]
    c0, cc2 = classes(sc)
    collide_rows(1, south1, north1, (south, north), cy, k, t)

    def first(z, _):
        advect_first(z, range(2, X), c1, a1, cy, u_ref, v_ref)
        return 0

    lax.fori_loop(4, 8, first, 0)
    advect_rows(range(1, X - 1), ub, vb, c1, cy, a1y)

    def second(z, _):
        settle_level(z, c0, cc2, a1, m1, c2, k, t)
        return 0

    lax.fori_loop(2, 6, second, 0, unroll=4)
    settle_rows(range(2, 6), ROW_TILES, c0, cc2, a1y, (south, north), c2y, k, t)

    def third(z, _):
        advect_second(z, range(2, X - 2), c2, a2, c2y, u_ref, v_ref)
        return 0

    lax.fori_loop(2, 6, third, 0)
    for z in range(4):
        fall_out(z, range(2, X - 2), c0, cc2, a2, res)


def rest_body(
    sc, u_ref, v_ref, kk, tt, south, north, c1, m1, cy, a1y,
    a1_in, c2_in, c2y_in, a2_in, res_in,
    a1, c2, c2y, a2, res,
):
    k, t = kk[...], tt[...]
    c0, cc2 = classes(sc)
    for z in range(4, 8):
        advect_first(z, EDGE, c1, a1, cy, u_ref, v_ref)
    settle_edges(range(2, 6), c0, cc2, a1, m1, c2, k, t)
    settle_rows(range(2, 6), ROW_EDGES, c0, cc2, a1y, (south, north), c2y, k, t)
    for z in range(2, 6):
        advect_second(z, ENDING, c2, a2, c2y, u_ref, v_ref)
    for z in range(4):
        fall_out(z, ENDING, c0, cc2, a2, res)


def spare_tiles(spare):
    return -(-EARLY // (B // spare)) if spare else 0


def unpacking(spare, sc):
    n0, start2 = sc[0], sc[1]
    within = lax.broadcasted_iota(jnp.int32, (T, B), 1) < start2 + n0

    def early(ref, tile):
        m = ref[tile * T : (tile + 1) * T]
        p6 = pltpu.roll(m, start2, 1)
        if spare:
            g, j = divmod(tile, spare_tiles(spare))
            more = ref[(EARLY + j) * T : (EARLY + j + 1) * T]
            turn = (n0 + start2 - g * spare + B) & (B - 1)
            p6 = jnp.where(within, p6, pltpu.roll(more, turn, 1))
        return m, p6

    def late(ref, i):
        m = ref[i * T : (i + 1) * T]
        return m, ref[(LATE + i) * T : (LATE + i + 1) * T] if spare else pltpu.roll(m, start2, 1)

    return early, late


def settle_top(columns, above, c0, cc2, a1, c2):
    for i in columns:
        p7, p6 = above(i)
        x6, x7 = (a1[(z * XA + i) * T : (z * XA + i + 1) * T] for z in (6, 7))
        c2[(6 * XA + i) * T : (6 * XA + i + 1) * T] = fall(c0, cc2, x6, x7, p6)
        c2[(7 * XA + i) * T : (7 * XA + i + 1) * T] = jnp.where(c0, x7, p7)


def settle_top_rows(tiles, row7, row6, c0, cc2, a1y, c2y):
    for i in tiles:
        x6, x7 = (a1y[pl.ds(i * T * Z + z, T, stride=Z), :] for z in (6, 7))
        at = 6 * 2 * X + i * T
        c2y[at : at + T] = fall(c0, cc2, x6, x7, row6[i * T : (i + 1) * T])
        c2y[at + 2 * X : at + 2 * X + T] = jnp.where(c0, x7, row7[i * T : (i + 1) * T])


def fall_top(z, i, above, c0, cc2, a2):
    x = [a2[(k * X + i) * T : (k * X + i + 1) * T] for k in range(z, min(z + 3, Z))]
    if z > 5:
        p7, p6 = above(i)
        x = x + [p6] if z == 6 else x + [p7, p7]
    return fall(c0, cc2, *x)


def upper_body(
    spare, sc, u_ref, v_ref, kk, tt, south, north, m1, a1, a1y, early, low, c2_in, c2y_in, a2_in,
    out, c2, c2y, a2, row7, row6, res, sem,
):
    k, t = kk[...], tt[...]
    c0, cc2 = classes(sc)
    copies = [pltpu.make_async_copy(low, out.at[pl.ds(0, 4 * X * T)], sem.at[4])]
    copies[0].start()
    unpack, _ = unpacking(spare, sc)
    settle_top(range(2, X), lambda i: unpack(early, i - 2), c0, cc2, a1, c2)
    for i in ROW_TILES:
        row7[i * T : (i + 1) * T], row6[i * T : (i + 1) * T] = unpack(early, X - 2 + i)
    settle_top_rows(ROW_TILES, row7, row6, c0, cc2, a1y, c2y)
    mask = jnp.concatenate([south[HALF : HALF + X], north[HALF : HALF + X]] * 2, axis=0)
    at = slice(12 * X, 16 * X)
    c2y[at] = collide(c2y[at], mask, k, t)
    for z in (6, 7):
        at = slice((z * XA + 2) * T, (z * XA + X) * T)
        c2[at] = collide(c2[at], m1[2 * T : X * T], k, t)
    columns = range(2, X - 2)
    for z in (6, 7):
        advect_second(z, columns, c2, a2, c2y, u_ref, v_ref)
    above = lambda i: unpack(early, X - 2 + 2 * X // T + i - 2)
    for z in range(4, 8):
        for i in columns:
            at = ((z - 4) * X + i) * T
            res[at : at + T] = fall_top(z, i, above, c0, cc2, a2)
        n = len(columns) * T
        copies.append(
            pltpu.make_async_copy(
                res.at[pl.ds(((z - 4) * X + 2) * T, n)],
                out.at[pl.ds((z * X + 2) * T, n)],
                sem.at[z - 4],
            )
        )
        copies[-1].start()
    for copy in copies:
        copy.wait()


def last_body(
    spare, sc, u_ref, v_ref, kk, tt, south, north, m1, a1, a1y, row7_in, row6_in, late, out_in,
    c2_in, c2y_in, a2_in, out, c2, c2y, a2, res, sem,
):
    k, t = kk[...], tt[...]
    c0, cc2 = classes(sc)
    _, unpack = unpacking(spare, sc)
    settle_top(EDGE, lambda i: unpack(late, EDGE.index(i)), c0, cc2, a1, c2)
    p7, p6 = unpack(late, 4)
    lane_row = lax.broadcasted_iota(jnp.int32, (T, B), 0)
    fixed = {}
    for i, tile in enumerate(ROW_EDGES):
        row = lane_row == (T - 1 if i % 2 else 0)
        fixed[tile] = [
            jnp.where(row, p[i : i + 1], ref[tile * T : (tile + 1) * T])
            for p, ref in ((p7, row7_in), (p6, row6_in))
        ]
    where, pieces, cloudy = [], [], []
    for z in (6, 7):
        for i in EDGE:
            where.append((c2, (z * XA + i) * T))
            pieces.append(c2[where[-1][1] : where[-1][1] + T])
            cloudy.append(m1[i * T : (i + 1) * T])
    for tile in ROW_EDGES:
        x6, x7 = (a1y[pl.ds(tile * T * Z + z, T, stride=Z), :] for z in (6, 7))
        side, first = divmod(tile * T, X)
        mask = (south, north)[side][HALF + first : HALF + first + T]
        for z, value in ((6, fall(c0, cc2, x6, x7, fixed[tile][1])), (7, jnp.where(c0, x7, fixed[tile][0]))):
            where.append((c2y, z * 2 * X + tile * T))
            pieces.append(value)
            cloudy.append(mask)
    c = collide(jnp.concatenate(pieces, axis=0), jnp.concatenate(cloudy, axis=0), k, t)
    for i, (ref, to) in enumerate(where):
        ref[to : to + T] = c[i * T : (i + 1) * T]
    for z in (6, 7):
        advect_second(z, ENDING, c2, a2, c2y, u_ref, v_ref)
    above = lambda i: unpack(late, 5 + ENDING.index(i))
    copies = []
    for z in range(4, 8):
        for half in range(2):
            at = ((z - 4) * 2 + half) * 2 * T
            for j in range(2):
                i = ENDING[half * 2 + j]
                res[at + j * T : at + (j + 1) * T] = fall_top(z, i, above, c0, cc2, a2)
            to = out.at[pl.ds((z * X + ENDING[half * 2]) * T, 2 * T)]
            copies.append(
                pltpu.make_async_copy(res.at[pl.ds(at, 2 * T)], to, sem.at[(z - 4) * 2 + half])
            )
            copies[-1].start()
    for copy in copies:
        copy.wait()


def ring(axis, step):
    n = lax.axis_size(axis)
    return [(i, (i + step) % n) for i in range(n)]


def swaps(axis, start):
    n = lax.axis_size(axis)
    pairs = [(i % n, (i + 1) % n) for i in range(start, n + start, 2)]
    return sorted({(a, b) for i, j in pairs for a, b in ((i, j), (j, i))})


def below(value):
    return lax.ppermute(value, "gz", [(i, i - 1) for i in range(1, lax.axis_size("gz"))])


def packed(spare, scalars, drops, capture, transfer, courant_u, courant_v, fall_class, cloud_mask):
    drops = drops.reshape(Z * X * Y, B)
    ub = jnp.broadcast_to(courant_u[:, None], (Z, B))
    vb = jnp.broadcast_to(courant_v[:, None], (Z, B))
    v = lambda n, d=F32: ((n, B), d, True)
    weights = [((2 * B, 2 * B), BF16, True)] * 2
    own, m1, ym0, ym1, yp0, yp1, kk, tt = call(
        edges_body,
        [v(Z * X * Y), v(XA * Y), v(ENDS + T), v(HALF), v(ENDS + T), v(HALF)] + weights,
        [drops, cloud_mask.T, capture, transfer],
        [HBM] * 4,
        [pltpu.VMEM((Y, X), jnp.int32), pltpu.VMEM((B, B), F32), pltpu.VMEM((B, B), F32), pltpu.SemaphoreType.DMA((Z + 3,))],
        cost=(1000, 4 << 20),
    )
    south0 = lax.ppermute(yp0, "gy", ring("gy", 1))
    north0 = lax.ppermute(ym0, "gy", ring("gy", -1))
    south1 = lax.ppermute(yp1, "gy", ring("gy", 1))
    north1 = lax.ppermute(ym1, "gy", ring("gy", -1))
    c1, kk, tt = call(
        own_body, [v(Z * XW * Y)], [own, m1, kk, tt], [VMEM] * 4, cost=(3 << 30, 8 << 20), keep=(2, 3)
    )
    shapes = [v(4 * XA * Z), v(Z * XA * T), v(2 * X * Z), v(Z * XA * T), v(Z * 2 * X), v(Z * X * T)]
    cy, a1, a1y, c2, c2y, a2, pay, kk, tt = call(
        functools.partial(early_body, spare),
        shapes + [v((EARLY + spare_tiles(spare)) * T)],
        [*scalars, ub, vb, c1, south0, north0, kk, tt, m1],
        [SMEM] * 3 + [VMEM] * 8,
        cost=(3 << 30, 8 << 20),
        keep=(8, 9),
    )
    pay, south1, north1 = lax.optimization_barrier((pay, south1, north1))
    early = below(pay)
    first, second = call(
        sides_body,
        [v(XMESSAGE)] * 2,
        [own, m1, south0, north0],
        [VMEM] * 4,
        cost=(1000, 1 << 18),
    )
    first = lax.ppermute(first, "gx", swaps("gx", 0))
    second = lax.ppermute(second, "gx", swaps("gx", 1))
    cy, a1, a1y, c2, c2y, a2, res, kk, tt = call(
        between_body,
        shapes + [v(4 * X * T)],
        [*scalars, ub, vb, kk, tt, south0, north0, south1, north1, c1, m1, cy, a1, a1y, c2, c2y, a2],
        [SMEM] * 3 + [VMEM] * 16,
        cost=(3 << 30, 8 << 20),
        aliases={13 + i: i for i in range(6)},
        keep=(5, 6),
    )
    c1, cy, m1, a1, a1y, c2, c2y, a2, pay, kk, tt = call(
        functools.partial(late_body, spare),
        [v(Z * XW * Y), shapes[0], v(XA * Y)] + shapes[1:] + [v((2 if spare else 1) * LATE * T)],
        [*scalars, ub, vb, first, second, kk, tt, south0, north0, c1, cy, m1, a1, a1y, c2, c2y, a2],
        [SMEM] * 3 + [VMEM] * 16,
        [pltpu.VMEM((2, XMESSAGE, B), F32)],
        cost=(1 << 28, 1 << 20),
        aliases={11 + i: i for i in range(8)},
        keep=(7, 8),
    )
    late = below(pay)
    a1, c2, c2y, a2, res, kk, tt = call(
        rest_body,
        [shapes[1], *shapes[3:], v(4 * X * T)],
        [*scalars, kk, tt, south0, north0, c1, m1, cy, a1y, a1, c2, c2y, a2, res],
        [SMEM] * 3 + [VMEM] * 13,
        cost=(1 << 29, 1 << 20),
        aliases={11 + i: i for i in range(5)},
        keep=(3, 4),
    )
    out, c2, c2y, a2, row7, row6, kk, tt = call(
        functools.partial(upper_body, spare),
        [((Z * X * Y, B), F32, False), *shapes[3:], v(2 * X), v(2 * X)],
        [*scalars, kk, tt, south0, north0, m1, a1, a1y, early, res, c2, c2y, a2],
        [SMEM] * 3 + [VMEM] * 12,
        [pltpu.VMEM((4 * X * T, B), F32), pltpu.SemaphoreType.DMA((5,))],
        cost=(3 << 30, 8 << 20),
        out_specs=[HBM] + [VMEM] * 5,
        aliases={12: 1, 13: 2, 14: 3},
        keep=(3, 4),
    )
    out, *_ = call(
        functools.partial(last_body, spare),
        [((Z * X * Y, B), F32, False), *shapes[3:]],
        [*scalars, kk, tt, south0, north0, m1, a1, a1y, row7, row6, late, out, c2, c2y, a2],
        [SMEM] * 3 + [VMEM] * 10 + [HBM] + [VMEM] * 3,
        [pltpu.VMEM((4 * len(ENDING) * T, B), F32), pltpu.SemaphoreType.DMA((8,))],
        cost=(1 << 28, 1 << 20),
        out_specs=[HBM] + [VMEM] * 3,
        aliases={13: 0, 14: 1, 15: 2, 16: 3},
    )
    return out.reshape(Z, X, Y, B)


def on_device(*args):
    way, *scalars = call(
        count_body,
        [((1,), jnp.int32, pltpu.SMEM), ((2,), jnp.int32, pltpu.SMEM)] + [((Z,), F32, pltpu.SMEM)] * 2,
        [args[5].reshape(1, B), args[3], args[4]],
        [HBM] * 3,
        [pltpu.VMEM((1, B), jnp.int32), pltpu.SemaphoreType.DMA((3,))],
        out_specs=[SMEM] * 4,
    )
    ways = [functools.partial(packed, spare) for spare in SPARES]
    return lax.switch(way.reshape(()), ways, scalars, *args)


def solution(mesh):
    in_specs = (P("gz", "gx", "gy", None), P(), P(), P("gz"), P("gz"), P(), P("gx", "gy"))
    out_specs = P("gz", "gx", "gy", None)
    return jax.shard_map(
        on_device, mesh=mesh, in_specs=in_specs, out_specs=out_specs, check_vma=False
    )
```

```python
import functools

import jax
import jax.numpy as jnp
from jax import lax
from jax.experimental import pallas as pl
from jax.experimental.pallas import tpu as pltpu
from jax.sharding import PartitionSpec as P

H_MAX = 2
Z, X, Y, B = 8, 64, 8, 128
T = 8
XW = X + 4
XA = X + 2
LOW = Z // 2
HALF = 2 * LOW * X
ENDS = HALF + T
XROWS = 2 * Z * Y
EARLY = (X - 2) + 2 * X // T + (X - 4)
SPARES = (0, 8, 24, B)
LATE = 4 + 1 + 4
EDGE = (0, 1, XA - 2, XA - 1)
ENDING = (0, 1, X - 2, X - 1)
ROW_TILES = range(2 * X // T)
ROW_EDGES = (0, X // T - 1, X // T, 2 * X // T - 1)
F32, BF16 = jnp.float32, jnp.bfloat16

VMEM = pl.BlockSpec(memory_space=pltpu.VMEM)
SMEM = pl.BlockSpec(memory_space=pltpu.SMEM)
HBM = pl.BlockSpec(memory_space=pltpu.HBM)


def rows(start, n=T):
    return pl.ds(start if isinstance(start, int) else pl.multiple_of(start, T), n)


def call(body, outs, args, specs, scratch=(), cost=(0, 0), out_specs=None, aliases=None, keep=()):
    shapes = [
        pltpu.VMEM(s, d) if m is True else m(s, d) if m else jax.ShapeDtypeStruct(s, d)
        for s, d, m in outs
    ]
    shapes += [pltpu.VMEM(args[i].shape, args[i].dtype) for i in keep]
    n_in, n_out = len(args), len(outs)
    aliases = {**(aliases or {}), **{i: n_out + k for k, i in enumerate(keep)}}

    def kernel(*refs):
        body(*refs[: n_in + n_out], *refs[n_in + n_out + len(keep) :])

    args = [
        pltpu.with_memory_space_constraint(a, s.memory_space)
        for a, s in zip(args, specs)
    ]
    return pl.pallas_call(
        kernel,
        out_shape=shapes,
        in_specs=list(specs),
        out_specs=(out_specs or [VMEM] * len(outs)) + [VMEM] * len(keep),
        scratch_shapes=list(scratch),
        input_output_aliases=aliases,
        cost_estimate=pl.CostEstimate(flops=cost[0], bytes_accessed=cost[1], transcendentals=0),
        compiler_params=pltpu.CompilerParams(vmem_limit_bytes=8 << 20),
    )(*args)


def split(x):
    high = x.astype(BF16)
    return high, (x - high.astype(F32)).astype(BF16)


def product(x, weights):
    out = jnp.dot(jnp.concatenate(split(x), axis=1), weights, preferred_element_type=F32)
    return out[:, :B] + out[:, B:]


def collide(s, cloudy, capture, transfer):
    loss = s * product(s, capture)
    return s + cloudy * (product(loss, transfer) - loss)


def eightfold(ref, row):
    return ref[pl.ds(row, T, stride=0), :]


def repeated(ref, start, n):
    return jnp.concatenate([eightfold(ref, start + i) for i in range(n)], axis=0)


def classes(sc_ref):
    lane = lax.broadcasted_iota(jnp.int32, (T, B), 1)
    return lane < sc_ref[0], lane >= sc_ref[1]


def fall(c0, c2, a, b, c):
    return jnp.where(c0, a, jnp.where(c2, c, b))


def count_body(falls, u_in, v_in, way, out, u, v, ref, sem):
    copies = [
        pltpu.make_async_copy(a, b, sem.at[i])
        for i, (a, b) in enumerate(((falls, ref), (u_in, u), (v_in, v)))
    ]
    for copy in copies:
        copy.start()
    for copy in copies:
        copy.wait()
    n0 = jnp.sum((ref[...] == 0).astype(jnp.int32))
    n2 = jnp.sum((ref[...] == H_MAX).astype(jnp.int32))
    out[0] = n0
    out[1] = B - n2
    way[0] = sum((n2 - n0 > spare).astype(jnp.int32) for spare in SPARES[:-1])


def edges_body(drops, cloud, k_in, t_in, own, m1, ym0, ym1, yp0, yp1, kk, tt, mask, k_ref, t_ref, sem):
    level = lambda z: pl.ds(z * X * Y, X * Y)
    copies = [
        pltpu.make_async_copy(a, b, sem.at[i])
        for i, (a, b) in enumerate(
            [(drops.at[level(z)], own.at[level(z)]) for z in range(Z)]
            + [(cloud, mask), (k_in, k_ref), (t_in, t_ref)]
        )
    ]
    for copy in copies[Z:] + copies[:Z]:
        copy.start()
    copies[Z].wait()
    columns = mask[...].astype(F32)
    wide = jnp.concatenate([columns, jnp.zeros((Y, B - X), F32)], axis=1)
    for x in range(X):
        m1[(x + 1) * Y : (x + 2) * Y] = jnp.broadcast_to(columns[:, x : x + 1], (Y, B))
    for i, (ref, out, turned) in enumerate(((k_ref, kk, True), (t_ref, tt, False))):
        copies[Z + 1 + i].wait()
        w = ref[...].T if turned else ref[...]
        high, low = split(w)
        half = jnp.concatenate([high, low], axis=1)
        out[...] = jnp.concatenate([half, half], axis=0)
    for out, ys in ((ym0, (0, 1)), (yp0, (Y - 1, Y - 2))):
        picked = [wide[y : y + 1] for y in ys] + [jnp.zeros((T - 2, B), F32)]
        out[HALF : HALF + T] = jnp.concatenate(picked, axis=0)
    for z in range(Z):
        copies[z].wait()
        for outs, ys in (((ym0, ym1), (0, 1)), ((yp0, yp1), (Y - 1, Y - 2))):
            for d, y in enumerate(ys):
                at = (d * LOW + z % LOW) * X
                outs[z // LOW][at : at + X] = own[pl.ds(z * X * Y + y, X, stride=Y), :]
    for out, y in ((ym0, 0), (yp0, Y - 1)):
        for i, x in enumerate((0, X - 1)):
            at, start = ENDS + i * LOW, (LOW * X + x) * Y + y
            out[at : at + LOW] = own[pl.ds(start, LOW, stride=X * Y), :]


def sides_body(own, m1, south, north, south_mask, north_mask, first, second):
    even = lax.axis_index("gx") % 2 == 0
    for out, to_right in ((first, even), (second, jnp.logical_not(even))):
        edge = jnp.where(to_right, X - 1, 0)
        inward = jnp.where(to_right, -1, 1)
        for d in range(2):
            x = edge + d * inward
            out[XROWS + d * Y : XROWS + (d + 1) * Y] = m1[rows((x + 1) * Y)]
            for z in range(Z):
                out[(d * Z + z) * Y : (d * Z + z + 1) * Y] = own[rows((z * X + x) * Y)]
        at = XROWS + 2 * Y
        out[at + 2 * Z :] = jnp.zeros((T, B), F32)
        for side, (ref, mask_ref) in enumerate(((south, south_mask), (north, north_mask))):
            row = at + side * Z
            end = ENDS + jnp.where(to_right, LOW, 0)
            out[row : row + LOW] = ref[pl.ds(edge, LOW, stride=X), :]
            out[row + LOW : row + Z] = ref[pl.ds(end, LOW), :]
            row = at + 2 * Z + side
            out[row : row + 1] = mask_ref[pl.ds(edge, 1), :]


XMESSAGE = XROWS + 2 * Y + 2 * Z + T


def own_body(own, m1, kk, tt, c1):
    k, t, mask = kk[...], tt[...], m1[Y : Y + X * Y]

    def level(z, _):
        c1[rows((z * XW + 2) * Y, X * Y)] = collide(own[rows(z * X * Y, X * Y)], mask, k, t)
        return 0

    lax.fori_loop(0, Z, level, 0, unroll=4)


def cy_at(side, d, x):
    return ((side * 2 + d) * XA + x + 1) * Z


def collide_rows(part, south, north, masks, cy, k, t):
    for side, (ref, mask_ref) in enumerate(zip((south, north), masks)):
        for d in range(2):
            mask = jnp.concatenate([mask_ref[d * X : (d + 1) * X]] * LOW, axis=0)
            c = collide(ref[d * LOW * X : (d + 1) * LOW * X], mask, k, t)
            for z in range(LOW):
                cy[pl.ds(cy_at(side, d, 0) + part * LOW + z, X, stride=Z), :] = c[z * X : (z + 1) * X]


def widen(ref, out):
    row, lane = (lax.broadcasted_iota(jnp.int32, (X, B), i) for i in range(2))
    ones = jnp.ones((B, B), BF16)
    for d in range(2):
        values = jnp.concatenate([eightfold(ref, HALF + d)] * (X // T), axis=0)
        picked = jnp.where(row == lane, values, 0.0).astype(BF16)
        out[d * X : (d + 1) * X] = jnp.dot(picked, ones, preferred_element_type=F32)


def upwind(z, u_ref, v_ref):
    u, v = u_ref[z], v_ref[z]
    at_edge = lax.broadcasted_iota(jnp.int32, (T, B), 0) == jnp.where(v > 0, 0, T - 1)
    return (
        jnp.abs(u),
        jnp.abs(v),
        jnp.where(u > 0, -Y, Y),
        jnp.where(v > 0, 1, T - 1),
        jnp.where(v > 0, 0, 1),
        at_edge,
    )


def advect(z, columns, c_ref, width, first, out_ref, out_width, edge, u_ref, v_ref):
    au, av, step, shift, side, at_edge = upwind(z, u_ref, v_ref)
    base, base_out = (z * width + first) * Y, z * out_width * Y
    edge_ref, edge_at, edge_stride = edge(z, side)
    for i in columns:
        c = c_ref[rows(base + i * Y)]
        x = c_ref[rows(base + step + i * Y)]
        e = eightfold(edge_ref, edge_at + i * edge_stride)
        y = jnp.where(at_edge, e, pltpu.roll(c, shift, 0))
        out_ref[rows(base_out + i * Y)] = c - au * (c - x) - av * (c - y)


def advect_first(z, columns, c1, a1, cy, u_ref, v_ref):
    edge = lambda z, side: (cy, side * (2 * XA * Z) + z, Z)
    advect(z, columns, c1, XW, 1, a1, XA, edge, u_ref, v_ref)


def advect_second(z, columns, c2, a2, c2y, u_ref, v_ref):
    edge = lambda z, side: (c2y, (z * 2 + side) * X, 1)
    advect(z, columns, c2, XA, 1, a2, X, edge, u_ref, v_ref)


def advect_rows(columns, ub, vb, c1, cy, a1y):
    au, av = jnp.abs(ub[...]), jnp.abs(vb[...])
    upos, vpos = ub[...] > 0, vb[...] > 0
    for side in range(2):
        for x in columns:
            at, far = cy_at(side, 0, x), cy_at(side, 1, x)
            c = cy[at : at + Z]
            xx = jnp.where(upos, cy[at - Z : at], cy[at + Z : at + 2 * Z])
            outer = cy[far : far + Z]
            inner = c1[pl.ds((x + 2) * Y + (Y - 1) * side, Z, stride=XW * Y), :]
            yy = jnp.where(vpos, *((outer, inner) if side == 0 else (inner, outer)))
            to = (side * X + x) * Z
            a1y[to : to + Z] = c - au * (c - xx) - av * (c - yy)


def settle(z, columns, c0, cc2, a1, c2):
    for i in columns:
        at = (z * XA + i) * T
        step = XA * T
        c2[rows(at)] = fall(c0, cc2, a1[rows(at)], a1[rows(at + step)], a1[rows(at + 2 * step)])


def settle_level(z, c0, cc2, a1, m1, c2, k, t):
    settle(z, range(XA), c0, cc2, a1, c2)
    at = rows(z * XA * T, XA * T)
    c2[at] = collide(c2[at], m1[...], k, t)


def settle_rows(levels, tiles, c0, cc2, a1y, masks, c2y, k, t):
    pieces, cloudy, where = [], [], []
    for z in levels:
        for i in tiles:
            a = [a1y[pl.ds(i * T * Z + z + j, T, stride=Z), :] for j in range(H_MAX + 1)]
            pieces.append(fall(c0, cc2, *a))
            side, first = divmod(i * T, X)
            cloudy.append(masks[side][first : first + T])
            where.append(z * 2 * X + i * T)
    c = collide(jnp.concatenate(pieces, axis=0), jnp.concatenate(cloudy, axis=0), k, t)
    for i, to in enumerate(where):
        c2y[to : to + T] = c[i * T : (i + 1) * T]


def settle_edges(levels, c0, cc2, a1, m1, c2, k, t):
    for z in levels:
        settle(z, EDGE, c0, cc2, a1, c2)
    tiles = [(z * XA + i) * T for z in levels for i in EDGE]
    c = collide(
        jnp.concatenate([c2[at : at + T] for at in tiles], axis=0),
        jnp.concatenate([m1[i * T : (i + 1) * T] for i in EDGE] * len(levels), axis=0),
        k,
        t,
    )
    for i, at in enumerate(tiles):
        c2[at : at + T] = c[i * T : (i + 1) * T]


def falling(a1, a1y, a2, tile):
    if tile < X - 2:
        at = (tile + 2) * T
        return lambda z: a1[z * XA * T + at : z * XA * T + at + T]
    tile -= X - 2
    if tile < 2 * X // T:
        return lambda z: a1y[pl.ds(tile * T * Z + z, T, stride=Z), :]
    at = (tile - 2 * X // T + 2) * T
    return lambda z: a2[z * X * T + at : z * X * T + at + T]


def early_body(
    spare, sc, u_ref, v_ref, ub, vb, c1, south, north, kk, tt, m1, cy, a1, a1y, c2, c2y, a2, pay, sm, nm
):
    k, t = kk[...], tt[...]
    c0, cc2 = classes(sc)
    widen(south, sm)
    widen(north, nm)
    collide_rows(0, south, north, (sm, nm), cy, k, t)

    def first(z, _):
        advect_first(z, range(2, X), c1, a1, cy, u_ref, v_ref)
        return 0

    lax.fori_loop(0, 4, first, 0)
    advect_rows(range(1, X - 1), ub, vb, c1, cy, a1y)

    def second(z, _):
        settle_level(z, c0, cc2, a1, m1, c2, k, t)
        return 0

    lax.fori_loop(0, 2, second, 0, unroll=2)
    settle_rows(range(2), ROW_TILES, c0, cc2, a1y, (sm, nm), c2y, k, t)

    def third(z, _):
        advect_second(z, range(2, X - 2), c2, a2, c2y, u_ref, v_ref)
        return 0

    lax.fori_loop(0, 2, third, 0)
    n0 = sc[0]
    n2 = B - sc[1]
    for tile in range(EARLY):
        level = falling(a1, a1y, a2, tile)
        l0 = level(0)
        packed = fall(c0, cc2, pltpu.roll(l0, n2, 1), l0, level(1))
        pay[tile * T : (tile + 1) * T] = packed
    tiles = spare_tiles(spare)
    lane = lax.broadcasted_iota(jnp.int32, (T, B), 1)
    for j in range(tiles):
        out = jnp.zeros((T, B), F32)
        for g in range(B // spare):
            if j + g * tiles < EARLY:
                l0 = falling(a1, a1y, a2, j + g * tiles)(0)
                turn = (n2 - n0 + g * spare + B) & (B - 1)
                here = (lane >= g * spare) & (lane < (g + 1) * spare)
                out = jnp.where(here, pltpu.roll(l0, turn, 1), out)
        pay[(EARLY + j) * T : (EARLY + j + 1) * T] = out


def late_body(
    spare, sc, u_ref, v_ref, ub, vb, first, second, kk, tt, south, north,
    c1_in, cy_in, m1_in, a1_in, a1y_in, c2_in, c2y_in, a2_in,
    c1, cy, m1, a1, a1y, c2, c2y, a2, pay, sides,
):
    k, t = kk[...], tt[...]
    c0, cc2 = classes(sc)
    even = lax.axis_index("gx") % 2 == 0
    for to, a, b in ((sides.at[0], second, first), (sides.at[1], first, second)):
        to[...] = jnp.where(even, a[...], b[...])
    left, right = sides.at[0], sides.at[1]
    m1[0:Y] = left[XROWS : XROWS + Y]
    m1[Y + X * Y :] = right[XROWS : XROWS + Y]
    at_mask = XROWS + 2 * Y
    pieces, masks = [], []
    for ref in (left, right):
        pieces += [ref[0:XROWS], ref[at_mask : at_mask + 2 * Z]]
        masks += [ref[XROWS + d * Y : XROWS + (d + 1) * Y] for d in range(2) for _ in range(Z)]
        masks += [eightfold(ref, at_mask + 2 * Z + side) for side in range(2)]
    c = collide(jnp.concatenate(pieces, axis=0), jnp.concatenate(masks, axis=0), k, t)
    size = XROWS + 2 * Z
    for i, (columns, x) in enumerate((((1, 0), -1), ((XW - 2, XW - 1), X))):
        for d in range(2):
            for z in range(Z):
                at, to = i * size + (d * Z + z) * Y, (z * XW + columns[d]) * Y
                c1[to : to + Y] = c[at : at + Y]
        for side in range(2):
            at, to = i * size + XROWS + side * Z, cy_at(side, 0, x)
            cy[to : to + Z] = c[at : at + Z]

    for z in range(4):
        advect_first(z, EDGE, c1, a1, cy, u_ref, v_ref)
    advect_rows((0, X - 1), ub, vb, c1, cy, a1y)
    settle_edges(range(2), c0, cc2, a1, m1, c2, k, t)
    settle_rows(range(2), ROW_EDGES, c0, cc2, a1y, (south, north), c2y, k, t)
    for z in range(2):
        advect_second(z, ENDING, c2, a2, c2y, u_ref, v_ref)
    tiles = [[a1[(z * XA + x) * T : (z * XA + x + 1) * T] for z in range(2)] for x in EDGE]
    ends = (0, X - 1, X, 2 * X - 1)
    tiles.append(
        [
            jnp.concatenate(
                [a1y[row * Z + z : row * Z + z + 1] for row in ends] + [jnp.zeros((T - 4, B), F32)],
                axis=0,
            )
            for z in range(2)
        ]
    )
    tiles += [[a2[(z * X + x) * T : (z * X + x + 1) * T] for z in range(2)] for x in ENDING]
    for i, (l0, l1) in enumerate(tiles):
        own = l0 if spare else pltpu.roll(l0, B - sc[1], 1)
        pay[i * T : (i + 1) * T] = fall(c0, cc2, own, l0, l1)
        if spare:
            pay[(LATE + i) * T : (LATE + i + 1) * T] = l0


def fall_out(z, columns, c0, cc2, a2, res):
    for i in columns:
        at, step = (z * X + i) * T, X * T
        res[at : at + T] = fall(
            c0, cc2, *(a2[at + k * step : at + k * step + T] for k in range(H_MAX + 1))
        )


def between_body(
    sc, u_ref, v_ref, ub, vb, kk, tt, south, north, south1, north1, c1, m1,
    cy_in, a1_in, a1y_in, c2_in, c2y_in, a2_in,
    cy, a1, a1y, c2, c2y, a2, res,
):
    k, t = kk[...], tt[...]
    c0, cc2 = classes(sc)
    collide_rows(1, south1, north1, (south, north), cy, k, t)

    def first(z, _):
        advect_first(z, range(2, X), c1, a1, cy, u_ref, v_ref)
        return 0

    lax.fori_loop(4, 8, first, 0)
    advect_rows(range(1, X - 1), ub, vb, c1, cy, a1y)

    def second(z, _):
        settle_level(z, c0, cc2, a1, m1, c2, k, t)
        return 0

    lax.fori_loop(2, 6, second, 0, unroll=4)
    settle_rows(range(2, 6), ROW_TILES, c0, cc2, a1y, (south, north), c2y, k, t)

    def third(z, _):
        advect_second(z, range(2, X - 2), c2, a2, c2y, u_ref, v_ref)
        return 0

    lax.fori_loop(2, 6, third, 0)
    for z in range(4):
        fall_out(z, range(2, X - 2), c0, cc2, a2, res)


def rest_body(
    sc, u_ref, v_ref, kk, tt, south, north, c1, m1, cy, a1y,
    a1_in, c2_in, c2y_in, a2_in, res_in,
    a1, c2, c2y, a2, res,
):
    k, t = kk[...], tt[...]
    c0, cc2 = classes(sc)
    for z in range(4, 8):
        advect_first(z, EDGE, c1, a1, cy, u_ref, v_ref)
    settle_edges(range(2, 6), c0, cc2, a1, m1, c2, k, t)
    settle_rows(range(2, 6), ROW_EDGES, c0, cc2, a1y, (south, north), c2y, k, t)
    for z in range(2, 6):
        advect_second(z, ENDING, c2, a2, c2y, u_ref, v_ref)
    for z in range(4):
        fall_out(z, ENDING, c0, cc2, a2, res)


def spare_tiles(spare):
    return -(-EARLY // (B // spare)) if spare else 0


def unpacking(spare, sc):
    n0, start2 = sc[0], sc[1]
    within = lax.broadcasted_iota(jnp.int32, (T, B), 1) < start2 + n0

    def early(ref, tile):
        m = ref[tile * T : (tile + 1) * T]
        p6 = pltpu.roll(m, start2, 1)
        if spare:
            g, j = divmod(tile, spare_tiles(spare))
            more = ref[(EARLY + j) * T : (EARLY + j + 1) * T]
            turn = (n0 + start2 - g * spare + B) & (B - 1)
            p6 = jnp.where(within, p6, pltpu.roll(more, turn, 1))
        return m, p6

    def late(ref, i):
        m = ref[i * T : (i + 1) * T]
        return m, ref[(LATE + i) * T : (LATE + i + 1) * T] if spare else pltpu.roll(m, start2, 1)

    return early, late


def settle_top(columns, above, c0, cc2, a1, c2):
    for i in columns:
        p7, p6 = above(i)
        x6, x7 = (a1[(z * XA + i) * T : (z * XA + i + 1) * T] for z in (6, 7))
        c2[(6 * XA + i) * T : (6 * XA + i + 1) * T] = fall(c0, cc2, x6, x7, p6)
        c2[(7 * XA + i) * T : (7 * XA + i + 1) * T] = jnp.where(c0, x7, p7)


def settle_top_rows(tiles, row7, row6, c0, cc2, a1y, c2y):
    for i in tiles:
        x6, x7 = (a1y[pl.ds(i * T * Z + z, T, stride=Z), :] for z in (6, 7))
        at = 6 * 2 * X + i * T
        c2y[at : at + T] = fall(c0, cc2, x6, x7, row6[i * T : (i + 1) * T])
        c2y[at + 2 * X : at + 2 * X + T] = jnp.where(c0, x7, row7[i * T : (i + 1) * T])


def fall_top(z, i, above, c0, cc2, a2):
    x = [a2[(k * X + i) * T : (k * X + i + 1) * T] for k in range(z, min(z + 3, Z))]
    if z > 5:
        p7, p6 = above(i)
        x = x + [p6] if z == 6 else x + [p7, p7]
    return fall(c0, cc2, *x)


def upper_body(
    spare, sc, u_ref, v_ref, kk, tt, south, north, m1, a1, a1y, early, low, c2_in, c2y_in, a2_in,
    out, c2, c2y, a2, row7, row6, res, sem,
):
    k, t = kk[...], tt[...]
    c0, cc2 = classes(sc)
    copies = [pltpu.make_async_copy(low, out.at[pl.ds(0, 4 * X * T)], sem.at[4])]
    copies[0].start()
    unpack, _ = unpacking(spare, sc)
    settle_top(range(2, X), lambda i: unpack(early, i - 2), c0, cc2, a1, c2)
    for i in ROW_TILES:
        row7[i * T : (i + 1) * T], row6[i * T : (i + 1) * T] = unpack(early, X - 2 + i)
    settle_top_rows(ROW_TILES, row7, row6, c0, cc2, a1y, c2y)
    mask = jnp.concatenate([south[0:X], north[0:X]] * 2, axis=0)
    at = slice(12 * X, 16 * X)
    c2y[at] = collide(c2y[at], mask, k, t)
    for z in (6, 7):
        at = slice((z * XA + 2) * T, (z * XA + X) * T)
        c2[at] = collide(c2[at], m1[2 * T : X * T], k, t)
    columns = range(2, X - 2)
    for z in (6, 7):
        advect_second(z, columns, c2, a2, c2y, u_ref, v_ref)
    above = lambda i: unpack(early, X - 2 + 2 * X // T + i - 2)
    for z in range(4, 8):
        for i in columns:
            at = ((z - 4) * X + i) * T
            res[at : at + T] = fall_top(z, i, above, c0, cc2, a2)
        n = len(columns) * T
        copies.append(
            pltpu.make_async_copy(
                res.at[pl.ds(((z - 4) * X + 2) * T, n)],
                out.at[pl.ds((z * X + 2) * T, n)],
                sem.at[z - 4],
            )
        )
        copies[-1].start()
    for copy in copies:
        copy.wait()


def last_body(
    spare, sc, u_ref, v_ref, kk, tt, south, north, m1, a1, a1y, row7_in, row6_in, late, out_in,
    c2_in, c2y_in, a2_in, out, c2, c2y, a2, res, sem,
):
    k, t = kk[...], tt[...]
    c0, cc2 = classes(sc)
    _, unpack = unpacking(spare, sc)
    settle_top(EDGE, lambda i: unpack(late, EDGE.index(i)), c0, cc2, a1, c2)
    p7, p6 = unpack(late, 4)
    lane_row = lax.broadcasted_iota(jnp.int32, (T, B), 0)
    fixed = {}
    for i, tile in enumerate(ROW_EDGES):
        row = lane_row == (T - 1 if i % 2 else 0)
        fixed[tile] = [
            jnp.where(row, p[i : i + 1], ref[tile * T : (tile + 1) * T])
            for p, ref in ((p7, row7_in), (p6, row6_in))
        ]
    where, pieces, cloudy = [], [], []
    for z in (6, 7):
        for i in EDGE:
            where.append((c2, (z * XA + i) * T))
            pieces.append(c2[where[-1][1] : where[-1][1] + T])
            cloudy.append(m1[i * T : (i + 1) * T])
    for tile in ROW_EDGES:
        x6, x7 = (a1y[pl.ds(tile * T * Z + z, T, stride=Z), :] for z in (6, 7))
        side, first = divmod(tile * T, X)
        mask = (south, north)[side][first : first + T]
        for z, value in ((6, fall(c0, cc2, x6, x7, fixed[tile][1])), (7, jnp.where(c0, x7, fixed[tile][0]))):
            where.append((c2y, z * 2 * X + tile * T))
            pieces.append(value)
            cloudy.append(mask)
    c = collide(jnp.concatenate(pieces, axis=0), jnp.concatenate(cloudy, axis=0), k, t)
    for i, (ref, to) in enumerate(where):
        ref[to : to + T] = c[i * T : (i + 1) * T]
    for z in (6, 7):
        advect_second(z, ENDING, c2, a2, c2y, u_ref, v_ref)
    above = lambda i: unpack(late, 5 + ENDING.index(i))
    copies = []
    for z in range(4, 8):
        for half in range(2):
            at = ((z - 4) * 2 + half) * 2 * T
            for j in range(2):
                i = ENDING[half * 2 + j]
                res[at + j * T : at + (j + 1) * T] = fall_top(z, i, above, c0, cc2, a2)
            to = out.at[pl.ds((z * X + ENDING[half * 2]) * T, 2 * T)]
            copies.append(
                pltpu.make_async_copy(res.at[pl.ds(at, 2 * T)], to, sem.at[(z - 4) * 2 + half])
            )
            copies[-1].start()
    for copy in copies:
        copy.wait()


def ring(axis, step):
    n = lax.axis_size(axis)
    return [(i, (i + step) % n) for i in range(n)]


def swaps(axis, start):
    n = lax.axis_size(axis)
    pairs = [(i % n, (i + 1) % n) for i in range(start, n + start, 2)]
    return sorted({(a, b) for i, j in pairs for a, b in ((i, j), (j, i))})


def below(value):
    return lax.ppermute(value, "gz", [(i, i - 1) for i in range(1, lax.axis_size("gz"))])


def packed(spare, scalars, drops, capture, transfer, courant_u, courant_v, fall_class, cloud_mask):
    drops = drops.reshape(Z * X * Y, B)
    ub = jnp.broadcast_to(courant_u[:, None], (Z, B))
    vb = jnp.broadcast_to(courant_v[:, None], (Z, B))
    v = lambda n, d=F32: ((n, B), d, True)
    weights = [((2 * B, 2 * B), BF16, True)] * 2
    own, m1, ym0, ym1, yp0, yp1, kk, tt = call(
        edges_body,
        [v(Z * X * Y), v(XA * Y), v(ENDS + T), v(HALF), v(ENDS + T), v(HALF)] + weights,
        [drops, cloud_mask.T, capture, transfer],
        [HBM] * 4,
        [pltpu.VMEM((Y, X), jnp.int32), pltpu.VMEM((B, B), F32), pltpu.VMEM((B, B), F32), pltpu.SemaphoreType.DMA((Z + 3,))],
        cost=(1000, 4 << 20),
    )
    south0 = lax.ppermute(yp0, "gy", ring("gy", 1))
    north0 = lax.ppermute(ym0, "gy", ring("gy", -1))
    south1 = lax.ppermute(yp1, "gy", ring("gy", 1))
    north1 = lax.ppermute(ym1, "gy", ring("gy", -1))
    c1, kk, tt = call(
        own_body, [v(Z * XW * Y)], [own, m1, kk, tt], [VMEM] * 4, cost=(1 << 30, 2 << 20), keep=(2, 3)
    )
    shapes = [v(4 * XA * Z), v(Z * XA * T), v(2 * X * Z), v(Z * XA * T), v(Z * 2 * X), v(Z * X * T)]
    cy, a1, a1y, c2, c2y, a2, pay, south_mask, north_mask, kk, tt = call(
        functools.partial(early_body, spare),
        shapes + [v((EARLY + spare_tiles(spare)) * T), v(2 * X), v(2 * X)],
        [*scalars, ub, vb, c1, south0, north0, kk, tt, m1],
        [SMEM] * 3 + [VMEM] * 8,
        cost=(3 << 30, 8 << 20),
        keep=(8, 9),
    )
    pay, south1, north1 = lax.optimization_barrier((pay, south1, north1))
    early = below(pay)
    first, second = call(
        sides_body,
        [v(XMESSAGE)] * 2,
        [own, m1, south0, north0, south_mask, north_mask],
        [VMEM] * 6,
        cost=(1000, 1 << 18),
    )
    first = lax.ppermute(first, "gx", swaps("gx", 0))
    second = lax.ppermute(second, "gx", swaps("gx", 1))
    cy, a1, a1y, c2, c2y, a2, res, kk, tt = call(
        between_body,
        shapes + [v(4 * X * T)],
        [*scalars, ub, vb, kk, tt, south_mask, north_mask, south1, north1, c1, m1, cy, a1, a1y, c2, c2y, a2],
        [SMEM] * 3 + [VMEM] * 16,
        cost=(3 << 30, 8 << 20),
        aliases={13 + i: i for i in range(6)},
        keep=(5, 6),
    )
    c1, cy, m1, a1, a1y, c2, c2y, a2, pay, kk, tt = call(
        functools.partial(late_body, spare),
        [v(Z * XW * Y), shapes[0], v(XA * Y)] + shapes[1:] + [v((2 if spare else 1) * LATE * T)],
        [*scalars, ub, vb, first, second, kk, tt, south_mask, north_mask, c1, cy, m1, a1, a1y, c2, c2y, a2],
        [SMEM] * 3 + [VMEM] * 16,
        [pltpu.VMEM((2, XMESSAGE, B), F32)],
        cost=(1 << 28, 1 << 20),
        aliases={11 + i: i for i in range(8)},
        keep=(7, 8),
    )
    late = below(pay)
    a1, c2, c2y, a2, res, kk, tt = call(
        rest_body,
        [shapes[1], *shapes[3:], v(4 * X * T)],
        [*scalars, kk, tt, south_mask, north_mask, c1, m1, cy, a1y, a1, c2, c2y, a2, res],
        [SMEM] * 3 + [VMEM] * 13,
        cost=(1 << 29, 1 << 20),
        aliases={11 + i: i for i in range(5)},
        keep=(3, 4),
    )
    out, c2, c2y, a2, row7, row6, kk, tt = call(
        functools.partial(upper_body, spare),
        [((Z * X * Y, B), F32, False), *shapes[3:], v(2 * X), v(2 * X)],
        [*scalars, kk, tt, south_mask, north_mask, m1, a1, a1y, early, res, c2, c2y, a2],
        [SMEM] * 3 + [VMEM] * 12,
        [pltpu.VMEM((4 * X * T, B), F32), pltpu.SemaphoreType.DMA((5,))],
        cost=(3 << 30, 8 << 20),
        out_specs=[HBM] + [VMEM] * 5,
        aliases={12: 1, 13: 2, 14: 3},
        keep=(3, 4),
    )
    out, *_ = call(
        functools.partial(last_body, spare),
        [((Z * X * Y, B), F32, False), *shapes[3:]],
        [*scalars, kk, tt, south_mask, north_mask, m1, a1, a1y, row7, row6, late, out, c2, c2y, a2],
        [SMEM] * 3 + [VMEM] * 10 + [HBM] + [VMEM] * 3,
        [pltpu.VMEM((4 * len(ENDING) * T, B), F32), pltpu.SemaphoreType.DMA((8,))],
        cost=(1 << 28, 1 << 20),
        out_specs=[HBM] + [VMEM] * 3,
        aliases={13: 0, 14: 1, 15: 2, 16: 3},
    )
    return out.reshape(Z, X, Y, B)


def on_device(*args):
    way, *scalars = call(
        count_body,
        [((1,), jnp.int32, pltpu.SMEM), ((2,), jnp.int32, pltpu.SMEM)] + [((Z,), F32, pltpu.SMEM)] * 2,
        [args[5].reshape(1, B), args[3], args[4]],
        [HBM] * 3,
        [pltpu.VMEM((1, B), jnp.int32), pltpu.SemaphoreType.DMA((3,))],
        out_specs=[SMEM] * 4,
    )
    ways = [functools.partial(packed, spare) for spare in SPARES]
    return lax.switch(way.reshape(()), ways, scalars, *args)


def solution(mesh):
    in_specs = (P("gz", "gx", "gy", None), P(), P(), P("gz"), P("gz"), P(), P("gx", "gy"))
    out_specs = P("gz", "gx", "gy", None)
    return jax.shard_map(
        on_device, mesh=mesh, in_specs=in_specs, out_specs=out_specs, check_vma=False
    )
```
